32 devices in a mesh: row: 4 (over z), ctx: 8 (over y, x, core).
Axes of the slice: x: 2, y: 2, z: 4, core: 2. Of those that a mesh axis runs over, the one named last changes fastest.
Arguments:
- inputs: bfloat16 [8, 2048, 2048], P('row', 'ctx'), may hold values from -6 to 6
- doc_len: int32 [8, 16], P('row'), may hold values from 0 to 2048, as said below
- w_query: bfloat16 [2048, 2048], P(('row', 'ctx')), may hold values from -0.125 to 0.125
- w_key: bfloat16 [2048, 2048], P(('row', 'ctx')), may hold values from -0.125 to 0.125
- w_value: bfloat16 [2048, 2048], P(('row', 'ctx')), may hold values from -0.125 to 0.125
- w_out: bfloat16 [2048, 2048], P(('row', 'ctx')), may hold values from -0.125 to 0.125
- w_up: bfloat16 [2048, 8192], P(('row', 'ctx')), may hold values from -0.125 to 0.125
- w_down: bfloat16 [8192, 2048], P(('row', 'ctx')), may hold values from -0.0625 to 0.0625
- gain_attn: bfloat16 [2048], P(('row', 'ctx')), may hold values from 0.099609375 to 1.8984375
- gain_attn_sub: bfloat16 [2048], P(('row', 'ctx')), may hold values from 0.099609375 to 1.8984375
- gain_ffn: bfloat16 [2048], P(('row', 'ctx')), may hold values from 0.099609375 to 1.8984375
- gain_ffn_sub: bfloat16 [8192], P(('row', 'ctx')), may hold values from 0.099609375 to 1.8984375
- out_cotangent: bfloat16 [8, 2048, 2048], P('row', 'ctx'), may hold values from -6 to 6
Outputs:
- output: bfloat16 [8, 2048, 2048], P('row', 'ctx')
- input_grad: float32 [8, 2048, 2048], P('row', 'ctx')
- query_grad: float32 [2048, 2048], P(('row', 'ctx'))
- key_grad: float32 [2048, 2048], P(('row', 'ctx'))
- value_grad: float32 [2048, 2048], P(('row', 'ctx'))
- out_grad: float32 [2048, 2048], P(('row', 'ctx'))
- up_grad: float32 [2048, 8192], P(('row', 'ctx'))
- down_grad: float32 [8192, 2048], P(('row', 'ctx'))
- gain_attn_grad: float32 [2048], P(('row', 'ctx'))
- gain_attn_sub_grad: float32 [2048], P(('row', 'ctx'))
- gain_ffn_grad: float32 [2048], P(('row', 'ctx'))
- gain_ffn_sub_grad: float32 [8192], P(('row', 'ctx'))
The draws below stay inside these ranges and needn't reach their ends.
Inputs may be any that keep to these rules, and one draw needn't show every extreme that they name: `doc_len`: each row lists the lengths of its documents in order, zeros after the last; a row's lengths add up to at most 2048, the rest of the row is padding; in each aligned block of 2 rows one row, drawn from the seed, holds a single document of 2048 tokens; every other nonzero length is at least max(1, 102).
All inputs are finite; a program needn't handle non-finite values.
Results may differ from the reference program's by a relative error of at most 0.017.
Values may be sent and summed in bfloat16 or wider, within the bound.
A program may use at most 512 MiB of HBM per device.

```python
import jax
import jax.numpy as jnp
from jax import lax

D = 2048
HEADS = 32
HEAD_DIM = 64
FF = 8192
ROW_LEN = 2048
ROWS_DEV = 2
SLOTS = 16
XPOS_BASE = 512
ROWS = 8


def draw_doc_len(key, part):
    first_key = jax.random.fold_in(key, 11)
    second_key = jax.random.fold_in(key, 23)
    lowest = max(1, ROW_LEN // 20)
    raw_lengths = jax.random.randint(first_key, (ROWS, SLOTS), lowest, ROW_LEN + 1)
    running = jnp.cumsum(raw_lengths, axis=1)
    kept_lengths = jnp.where(running <= ROW_LEN, raw_lengths, 0)
    chosen = jax.random.randint(second_key, (ROWS // ROWS_DEV,), 0, ROWS_DEV)
    whole_row = jnp.arange(ROWS) % ROWS_DEV == jnp.repeat(chosen, ROWS_DEV)
    single = jnp.where(jnp.arange(SLOTS) == 0, ROW_LEN, 0)
    return jnp.where(whole_row[:, None], single[None, :], kept_lengths).astype(jnp.int32)


def steps_of(key, dims, shards, smallest, largest):
    loudness, own = 1.0, jax.random.fold_in(key, 6)
    for dim, parts in shards:
        draws = jnp.exp(jax.random.uniform(jax.random.fold_in(own, dim), (parts,), jnp.float32, smallest / len(shards), largest / len(shards)))
        loudness = loudness * jnp.repeat(draws, dims[dim] // parts).reshape([-1 if axis == dim else 1 for axis in range(len(dims))])
    return loudness


def noise(key, extent, width, reach, split=(), kind=jnp.bfloat16):
    factor_of = steps_of(key, extent, split, -0.22, 0.18) if split else 1.0
    values = jax.random.normal(key, extent, jnp.float32) * width * factor_of
    return jnp.minimum(jnp.maximum(values, -reach), reach).astype(kind)


def setup_inputs(seed: int = 0) -> dict:
    key_of = jax.random.split(jax.random.key(seed), 14)
    inputs = noise(key_of[0], (ROWS, ROW_LEN, D), 1.0, 6.0, ((0, 4), (1, 8)))
    doc_len = draw_doc_len(jax.random.fold_in(key_of[13], 71), 0)
    w_query = noise(key_of[2], (D, D), D ** -0.5, 0.125, ((0, 32),))
    w_key = noise(key_of[3], (D, D), D ** -0.5, 0.125, ((0, 32),))
    w_value = noise(key_of[4], (D, D), D ** -0.5, 0.125, ((0, 32),))
    w_out = noise(key_of[5], (D, D), D ** -0.5, 0.125, ((0, 32),))
    w_up = noise(key_of[6], (D, FF), D ** -0.5, 0.125, ((0, 32),))
    w_down = noise(key_of[7], (FF, D), FF ** -0.5, 0.0625, ((0, 32),))
    gain_attn = jnp.clip(1.0 + 0.18 * jax.random.normal(key_of[8], (D,), jnp.float32), 0.099609375, 1.8984375).astype(jnp.bfloat16)
    gain_attn_sub = jnp.clip(1.0 + 0.18 * jax.random.normal(key_of[9], (D,), jnp.float32), 0.099609375, 1.8984375).astype(jnp.bfloat16)
    gain_ffn = jnp.clip(1.0 + 0.18 * jax.random.normal(key_of[10], (D,), jnp.float32), 0.099609375, 1.8984375).astype(jnp.bfloat16)
    gain_ffn_sub = jnp.clip(1.0 + 0.18 * jax.random.normal(key_of[11], (FF,), jnp.float32), 0.099609375, 1.8984375).astype(jnp.bfloat16)
    out_cotangent = noise(key_of[12], (ROWS, ROW_LEN, D), 1.0, 6.0, ((0, 4), (1, 8)))
    return {"inputs": inputs, "doc_len": doc_len, "w_query": w_query, "w_key": w_key, "w_value": w_value, "w_out": w_out, "w_up": w_up, "w_down": w_down, "gain_attn": gain_attn, "gain_attn_sub": gain_attn_sub, "gain_ffn": gain_ffn, "gain_ffn_sub": gain_ffn_sub, "out_cotangent": out_cotangent}


masked_score = -1e+30

@jax.custom_vjp
def low(v):
    return lax.optimization_barrier(v.astype(jnp.bfloat16)).astype(jnp.float32)

@jax.custom_vjp
def low_back(v):
    return v

def low_keep(v):
    return (low(v), None)

def low_pass(kept, grad):
    return (grad,)

def back_keep(v):
    return (v, None)

def back_low(kept, grad):
    return (low(grad),)
low.defvjp(low_keep, low_pass)
low_back.defvjp(back_keep, back_low)

def norm_gain(values, gain):
    center = values - lax.optimization_barrier(jnp.mean(values, axis=-1, keepdims=True))
    spread = lax.optimization_barrier(jnp.mean(center * center, axis=-1, keepdims=True))
    return center * lax.rsqrt(spread + 1e-05) * gain

def doc_info(lengths, places):
    doc_ends = jnp.cumsum(lengths, axis=-1).astype(jnp.int32)
    passed = doc_ends[..., None, :] <= places[..., :, None]
    doc_ids = lax.optimization_barrier(jnp.sum(passed.astype(jnp.int32), axis=-1)).astype(jnp.int32)
    starts = lax.optimization_barrier(jnp.sum(jnp.where(passed, lengths[..., None, :], 0), axis=-1)).astype(jnp.int32)
    is_valid = places < doc_ends[..., -1:]
    return (doc_ids, starts, is_valid)

def xpos_tables(relative):
    half_dim = HEAD_DIM // 2
    ladder = jnp.arange(half_dim, dtype=jnp.float32) / half_dim
    angle_rate = jnp.power(10000.0, -ladder)
    decay_base = (ladder + 0.4) / 1.4
    angles = relative[:, None] * angle_rate[None, :]
    factor = jnp.power(decay_base[None, :], (relative[:, None] - ROW_LEN / 2) / XPOS_BASE)
    return (jnp.cos(angles), jnp.sin(angles), factor)

def rotate(values, cosine, sine_part, factor):
    half_dim = HEAD_DIM // 2
    first_half = values[..., :half_dim]
    second = values[..., half_dim:]
    cosine = cosine[:, None, :]
    sine_part = sine_part[:, None, :]
    turned = jnp.concatenate([first_half * cosine - second * sine_part, second * cosine + first_half * sine_part], axis=-1)
    return turned * jnp.concatenate([factor, factor], axis=-1)[:, None, :]

def visible(query_pos, key_pos, query_doc, key_doc, key_valid):
    self_pair = query_pos[..., :, None] == key_pos[..., None, :]
    causal = (query_doc[..., :, None] == key_doc[..., None, :]) & (key_pos[..., None, :] <= query_pos[..., :, None]) & key_valid[..., None, :]
    return self_pair | causal

def matmul(first_op, second_op):
    return jnp.dot(first_op, second_op, precision=lax.Precision.HIGHEST)

def forward(tokens_flat, doc_len, w_query, w_key, w_value, w_out, w_up, w_down, gain_attn, gain_attn_sub, gain_ffn, gain_ffn_sub):
    normed = low(norm_gain(tokens_flat, gain_attn))
    query = low_back(matmul(normed, w_query))
    key_raw = low_back(matmul(normed, w_key))
    value_low = low(low_back(matmul(normed, w_value)))
    places = jnp.broadcast_to(jnp.arange(ROW_LEN, dtype=jnp.int32)[None, :], (ROWS, ROW_LEN))
    doc_ids, starts, is_valid = doc_info(doc_len, places)
    relative = (places - starts).astype(jnp.float32).reshape(-1)
    cosine, sine_part, factor = xpos_tables(relative)
    head_shape = (ROWS * ROW_LEN, HEADS, HEAD_DIM)
    query_rot = low(rotate(query.reshape(head_shape), cosine, sine_part, factor))
    key_rot = low(rotate(key_raw.reshape(head_shape), cosine, sine_part, 1.0 / factor))

    def per_head(tensor):
        return tensor.reshape(ROWS, ROW_LEN, HEADS, HEAD_DIM).transpose(0, 2, 1, 3).reshape(ROWS * HEADS, ROW_LEN, HEAD_DIM)
    head_docs = jnp.repeat(doc_ids, HEADS, axis=0)
    head_valid = jnp.repeat(is_valid, HEADS, axis=0)
    positions = jnp.arange(ROW_LEN, dtype=jnp.int32)

    def one_head(packed):
        query_head, key_head, value_head, docs_head, valid_head = packed
        scores = low_back(matmul(query_head, key_head.T) * HEAD_DIM ** (-0.5))
        allowed = visible(positions, positions, docs_head, docs_head, valid_head)
        scores = jnp.where(allowed, scores, masked_score)
        attention = jax.nn.softmax(scores, axis=-1)
        return matmul(low(attention), value_head)
    head_out = lax.map(jax.checkpoint(one_head), (per_head(query_rot), per_head(key_rot), per_head(value_low), head_docs, head_valid))
    attended = low_back(head_out.reshape(ROWS, HEADS, ROW_LEN, HEAD_DIM).transpose(0, 2, 1, 3).reshape(ROWS * ROW_LEN, D))
    context = low(norm_gain(attended, gain_attn_sub))
    residual = tokens_flat + low_back(matmul(context, w_out))
    ffn_input = low(norm_gain(residual, gain_ffn))
    hidden = low_back(matmul(ffn_input, w_up))
    squeezed = low(norm_gain(jax.nn.gelu(hidden, approximate=False), gain_ffn_sub))
    return residual + low_back(matmul(squeezed, w_down))

def reference(inputs, doc_len, w_query, w_key, w_value, w_out, w_up, w_down, gain_attn, gain_attn_sub, gain_ffn, gain_ffn_sub, out_cotangent):
    tokens_flat = inputs.astype(jnp.float32).reshape(ROWS * ROW_LEN, D)

    def wrapped(tok_in, wq_in, wk_in, wv_in, wo_in, wu_in, wd_in, ga_in, gs_in, gf_in, gg_in):
        return forward(tok_in, doc_len, wq_in, wk_in, wv_in, wo_in, wu_in, wd_in, ga_in, gs_in, gf_in, gg_in)
    result, pullback = jax.vjp(wrapped, tokens_flat, w_query.astype(jnp.float32), w_key.astype(jnp.float32), w_value.astype(jnp.float32), w_out.astype(jnp.float32), w_up.astype(jnp.float32), w_down.astype(jnp.float32), gain_attn.astype(jnp.float32), gain_attn_sub.astype(jnp.float32), gain_ffn.astype(jnp.float32), gain_ffn_sub.astype(jnp.float32))
    gradients = pullback(out_cotangent.astype(jnp.float32).reshape(ROWS * ROW_LEN, D))
    return (result.reshape(ROWS, ROW_LEN, D).astype(jnp.bfloat16), gradients[0].reshape(ROWS, ROW_LEN, D), gradients[1], gradients[2], gradients[3], gradients[4], gradients[5], gradients[6], gradients[7], gradients[8], gradients[9], gradients[10])
```

```python
import functools
import jax, jax.numpy as jnp
from jax import lax
from jax.experimental import pallas as pl
from jax.experimental.pallas import tpu as pltpu
bf16=jnp.bfloat16; f32=jnp.float32
HEAD_DIM=64
LOG2E=1.4426950408889634
NEG=-1e30

def fwd_kernel(nh, blk, span_ref, qT_ref, kT_ref, vT_ref, lo_ref, o_ref, oT_ref, lse_ref, k_s, qm_s, acc_s, m_s, l_s):
    r=pl.program_id(0); qb=pl.program_id(1)
    n=kT_ref.shape[1]//blk
    W=2*HEAD_DIM
    @pl.when(qb==0)
    def _():
        for c in range(n):
            k_s[pl.ds(c*blk,blk),:]=kT_ref[:,pl.ds(c*blk,blk)].T
    zero=jnp.zeros((HEAD_DIM,blk),bf16)
    for h in range(nh):
        own=h%2
        qm_s[h,pl.ds(own*HEAD_DIM,HEAD_DIM),:]=qT_ref[pl.ds(h*HEAD_DIM,HEAD_DIM),:]
        qm_s[h,pl.ds((1-own)*HEAD_DIM,HEAD_DIM),:]=zero
    acc_s[...]=jnp.zeros_like(acc_s)
    m_s[...]=jnp.full_like(m_s,NEG)
    l_s[...]=jnp.zeros_like(l_s)
    lo=lo_ref[0]
    def step(kb,masked):
        off=pl.multiple_of(kb*blk,blk)
        if masked:
            key=off+lax.broadcasted_iota(jnp.int32,(blk,blk),0)
            qry=qb*blk+lax.broadcasted_iota(jnp.int32,(blk,blk),1)
            ok=(key<=qry)&(key>=lo)
        for h in range(nh):
            kk=k_s[pl.ds(off,blk),pl.ds((h//2)*W,W)]
            s=jnp.dot(kk,qm_s[h],preferred_element_type=f32)*(LOG2E*HEAD_DIM**-0.5)
            if masked: s=jnp.where(ok,s,NEG)
            m0=m_s[h:h+1,:]
            m1=jnp.maximum(m0,jnp.max(s,axis=0,keepdims=True))
            p=jnp.exp2(s-m1)
            al=jnp.exp2(m0-m1)
            m_s[h:h+1,:]=m1
            l_s[h:h+1,:]=l_s[h:h+1,:]*al+jnp.sum(p,axis=0,keepdims=True)
            vv=vT_ref[pl.ds(h*HEAD_DIM,HEAD_DIM),pl.ds(off,blk)]
            sl=pl.ds(h*HEAD_DIM,HEAD_DIM)
            acc_s[sl,:]=acc_s[sl,:]*al+jnp.dot(vv,p.astype(bf16),preferred_element_type=f32)
    loops(span_ref,r,qb,blk,step)
    for h in range(nh):
        l=l_s[h:h+1,:]
        sl=pl.ds(h*HEAD_DIM,HEAD_DIM)
        oT_ref[sl,:]=acc_s[sl,:]/l
        lse_ref[h:h+1,:]=m_s[h:h+1,:]+jnp.log2(l)
    o_ref[...]=oT_ref[...].T.astype(bf16)

def loops(span_ref,r,qb,blk,step):
    k0=span_ref[r,qb,0]
    u0=span_ref[r,qb,1]
    def masked_body(t,c):
        kb=jnp.where(t<u0-k0,k0+t,qb)
        step(kb,True); return c
    def plain(kb,c):
        step(kb,False); return c
    lax.fori_loop(0,u0-k0+1,masked_body,0)
    lax.fori_loop(u0,qb,plain,0)

def bwd_kernel(nh, blk, span_ref, qT_ref, kT_ref, vT_ref, do_ref, oT_ref, lse_ref, lo_ref, dqT_ref, dkT_ref, dvT_ref,
               k_s, v_s, qm_s, dm_s, qn_s, dn_s, acc_s, dk_s, dv_s, p_s, ds_s, dl_s):
    r=pl.program_id(0); qb=pl.program_id(1)
    n=kT_ref.shape[1]//blk
    W=2*HEAD_DIM; scale=HEAD_DIM**-0.5
    @pl.when(qb==0)
    def _():
        for c in range(n):
            k_s[pl.ds(c*blk,blk),:]=kT_ref[:,pl.ds(c*blk,blk)].T
            v_s[pl.ds(c*blk,blk),:]=vT_ref[:,pl.ds(c*blk,blk)].T
        dk_s[...]=jnp.zeros_like(dk_s)
        dv_s[...]=jnp.zeros_like(dv_s)
    zero=jnp.zeros((HEAD_DIM,blk),bf16)
    doT=do_ref[...].T
    q=qT_ref[...].T
    lane=lax.broadcasted_iota(jnp.int32,(blk,W),1)
    prod=doT.astype(f32)*oT_ref[...]
    for h in range(nh):
        own=h%2
        sl=slice(h*HEAD_DIM,(h+1)*HEAD_DIM)
        qm_s[h,pl.ds(own*HEAD_DIM,HEAD_DIM),:]=qT_ref[pl.ds(h*HEAD_DIM,HEAD_DIM),:]
        qm_s[h,pl.ds((1-own)*HEAD_DIM,HEAD_DIM),:]=zero
        dm_s[h,pl.ds(own*HEAD_DIM,HEAD_DIM),:]=doT[sl,:]
        dm_s[h,pl.ds((1-own)*HEAD_DIM,HEAD_DIM),:]=zero
        mine=(lane//HEAD_DIM)==own
        pr=slice((h//2)*W,(h//2)*W+W)
        qn_s[h//2,pl.ds(own*blk,blk),:]=jnp.where(mine,q[:,pr],jnp.zeros((),bf16))
        dn_s[h//2,pl.ds(own*blk,blk),:]=jnp.where(mine,do_ref[:,pr],jnp.zeros((),bf16))
        dl_s[h:h+1,:]=jnp.sum(prod[sl,:],axis=0,keepdims=True)
    acc_s[...]=jnp.zeros_like(acc_s)
    lo=lo_ref[0]
    def step(kb,masked):
        off=pl.multiple_of(kb*blk,blk)
        if masked:
            key=off+lax.broadcasted_iota(jnp.int32,(blk,blk),0)
            qry=qb*blk+lax.broadcasted_iota(jnp.int32,(blk,blk),1)
            ok=(key<=qry)&(key>=lo)
        for g in range(nh//2):
            kk=k_s[pl.ds(off,blk),pl.ds(g*W,W)]
            vv=v_s[pl.ds(off,blk),pl.ds(g*W,W)]
            for own in range(2):
                h=2*g+own
                s=jnp.dot(kk,qm_s[h],preferred_element_type=f32)*(LOG2E*scale)
                p=jnp.exp2(s-lse_ref[h:h+1,:])
                if masked: p=jnp.where(ok,p,0.0)
                dp=jnp.dot(vv,dm_s[h],preferred_element_type=f32)
                ds=(p*(dp-dl_s[h:h+1,:])).astype(bf16)
                p_s[g,:,pl.ds(own*blk,blk)]=p.astype(bf16)
                ds_s[g,:,pl.ds(own*blk,blk)]=ds
                sl=pl.ds(h*HEAD_DIM,HEAD_DIM)
                acc_s[sl,:]+=jnp.dot(kT_ref[sl,pl.ds(off,blk)],ds,preferred_element_type=f32)
            dv_s[pl.ds(off,blk),pl.ds(g*W,W)]+=jnp.dot(p_s[g],dn_s[g],preferred_element_type=f32)
            dk_s[pl.ds(off,blk),pl.ds(g*W,W)]+=jnp.dot(ds_s[g],qn_s[g],preferred_element_type=f32)
    loops(span_ref,r,qb,blk,step)
    dqT_ref[...]=acc_s[...]*scale
    @pl.when(qb==n-1)
    def _():
        for c in range(n):
            dkT_ref[:,pl.ds(c*blk,blk)]=(dk_s[pl.ds(c*blk,blk),:]*scale).T
            dvT_ref[:,pl.ds(c*blk,blk)]=dv_s[pl.ds(c*blk,blk),:].T.astype(bf16)

def spans(lo,blk):
    rows,length=lo.shape
    n=length//blk
    lob=lo.reshape(rows,n,blk)
    first=lob[:,:,0]//blk
    last=(lob[:,:,-1]+blk-1)//blk
    own=jnp.arange(n,dtype=jnp.int32)[None,:]
    return jnp.stack([jnp.minimum(first,own),jnp.minimum(last,own)],axis=-1).astype(jnp.int32)

PARAMS=pltpu.CompilerParams(dimension_semantics=("arbitrary","arbitrary"),vmem_limit_bytes=60*2**20)

def attention_fwd(qT,kT,vT,lo,blk):
    rows,length=lo.shape
    dim,T=qT.shape
    nh=dim//HEAD_DIM; n=length//blk
    return pl.pallas_call(functools.partial(fwd_kernel,nh,blk),
        out_shape=(jax.ShapeDtypeStruct((T,dim),bf16),jax.ShapeDtypeStruct((dim,T),f32),jax.ShapeDtypeStruct((nh,T),f32)),
        grid_spec=pltpu.PrefetchScalarGridSpec(num_scalar_prefetch=1,grid=(rows,n),
            in_specs=[pl.BlockSpec((dim,blk),lambda r,q,s:(0,r*n+q)),
                      pl.BlockSpec((dim,length),lambda r,q,s:(0,r)),
                      pl.BlockSpec((dim,length),lambda r,q,s:(0,r)),
                      pl.BlockSpec((1,1,blk),lambda r,q,s:(r,0,q))],
            out_specs=[pl.BlockSpec((blk,dim),lambda r,q,s:(r*n+q,0)),
                       pl.BlockSpec((dim,blk),lambda r,q,s:(0,r*n+q)),
                       pl.BlockSpec((nh,blk),lambda r,q,s:(0,r*n+q))],
            scratch_shapes=[pltpu.VMEM((length,dim),bf16),pltpu.VMEM((nh,2*HEAD_DIM,blk),bf16),pltpu.VMEM((dim,blk),f32),
                            pltpu.VMEM((8,blk),f32),pltpu.VMEM((8,blk),f32)]),
        compiler_params=PARAMS,name="attention_forward",
        cost_estimate=pl.CostEstimate(flops=2*2*dim*T*length//2*2,bytes_accessed=20*2**20,transcendentals=nh*T*length//2))(spans(lo,blk),qT,kT,vT,lo[:,None,:])

def attention_bwd(qT,kT,vT,do,oT,lse,lo,blk):
    rows,length=lo.shape
    dim,T=qT.shape
    nh=dim//HEAD_DIM; n=length//blk; W=2*HEAD_DIM
    sds=jax.ShapeDtypeStruct
    return pl.pallas_call(functools.partial(bwd_kernel,nh,blk),
        out_shape=(sds((dim,T),f32),sds((dim,T),f32),sds((dim,T),bf16)),
        grid_spec=pltpu.PrefetchScalarGridSpec(num_scalar_prefetch=1,grid=(rows,n),
            in_specs=[pl.BlockSpec((dim,blk),lambda r,q,s:(0,r*n+q)),
                      pl.BlockSpec((dim,length),lambda r,q,s:(0,r)),
                      pl.BlockSpec((dim,length),lambda r,q,s:(0,r)),
                      pl.BlockSpec((blk,dim),lambda r,q,s:(r*n+q,0)),
                      pl.BlockSpec((dim,blk),lambda r,q,s:(0,r*n+q)),
                      pl.BlockSpec((nh,blk),lambda r,q,s:(0,r*n+q)),
                      pl.BlockSpec((1,1,blk),lambda r,q,s:(r,0,q))],
            out_specs=[pl.BlockSpec((dim,blk),lambda r,q,s:(0,r*n+q)),
                       pl.BlockSpec((dim,length),lambda r,q,s:(0,r)),
                       pl.BlockSpec((dim,length),lambda r,q,s:(0,r))],
            scratch_shapes=[pltpu.VMEM((length,dim),bf16),pltpu.VMEM((length,dim),bf16),
                            pltpu.VMEM((nh,W,blk),bf16),pltpu.VMEM((nh,W,blk),bf16),
                            pltpu.VMEM((nh//2,2*blk,W),bf16),pltpu.VMEM((nh//2,2*blk,W),bf16),
                            pltpu.VMEM((dim,blk),f32),pltpu.VMEM((length,dim),f32),pltpu.VMEM((length,dim),f32),
                            pltpu.VMEM((nh//2,blk,2*blk),bf16),pltpu.VMEM((nh//2,blk,2*blk),bf16),
                            pltpu.VMEM((8,blk),f32)]),
        compiler_params=PARAMS,name="attention_backward",
        cost_estimate=pl.CostEstimate(flops=5*2*dim*T*length//2*2,bytes_accessed=40*2**20,transcendentals=nh*T*length//2))(spans(lo,blk),qT,kT,vT,do,oT,lse,lo[:,None,:])


from jax.sharding import PartitionSpec as P

ROW_LEN = 2048
XPOS_BASE = 512
EPS = 1e-5
BOTH = ("row", "ctx")


def standardize(values):
    center = values - jnp.mean(values, axis=-1, keepdims=True)
    spread = jnp.mean(center * center, axis=-1, keepdims=True)
    rstd = lax.rsqrt(spread + EPS)
    return center * rstd, rstd


def standardize_back(hat, rstd, grad):
    return rstd * (grad - jnp.mean(grad, axis=-1, keepdims=True) - hat * jnp.mean(grad * hat, axis=-1, keepdims=True))


def row_places(lengths, row_len):
    places = jnp.arange(row_len, dtype=jnp.int32)
    ends = jnp.cumsum(lengths, axis=-1)
    passed = ends[:, None, :] <= places[None, :, None]
    starts = jnp.sum(jnp.where(passed, lengths[:, None, :], 0), axis=-1)
    valid = places[None, :] < ends[:, -1:]
    lowest = jnp.where(valid, starts, places[None, :]).astype(jnp.int32)
    return (places[None, :] - starts).astype(f32), lowest


def xpos_tables(relative):
    half = HEAD_DIM // 2
    ladder = jnp.arange(half, dtype=f32) / half
    rate = jnp.power(10000.0, -ladder)
    base = (ladder + 0.4) / 1.4
    angles = rate[:, None] * relative[None, :]
    factor = jnp.power(base[:, None], (relative[None, :] - ROW_LEN / 2) / XPOS_BASE)
    return jnp.cos(angles), jnp.sin(angles), factor


def turn(values, cosine, sine, factor):
    dim, tokens = values.shape
    half = HEAD_DIM // 2
    pairs = values.reshape(dim // HEAD_DIM, 2, half, tokens)
    one, two = pairs[:, 0], pairs[:, 1]
    cosine, sine = cosine * factor, sine * factor
    return jnp.stack([one * cosine - two * sine, two * cosine + one * sine], axis=1).reshape(dim, tokens)


def phi_parts(h):
    cdf = 0.5 * (1.0 + lax.erf(h * (2.0**-0.5)))
    pdf = jnp.exp(-0.5 * h * h) * 0.3989422804014327
    return cdf, pdf


def dot(a, b, spec, kind=f32):
    return jnp.einsum(spec, a, b, preferred_element_type=f32).astype(kind)


def gather_ctx(x):
    return lax.all_gather(x, "ctx", axis=1, tiled=True)


def scatter_ctx(x):
    return lax.psum_scatter(x, "ctx", scatter_dimension=1, tiled=True)


def body(inputs, doc_len, w_query, w_key, w_value, w_out, w_up, w_down, gain_attn, gain_attn_sub, gain_ffn,
         gain_ffn_sub, out_cotangent):
    rows, local_len, width = inputs.shape
    n, m = lax.axis_size("ctx"), lax.axis_size("row")
    row_len = local_len * n
    tokens, group = rows * local_len, rows * row_len
    piece = w_query.shape[0]
    heads_dim = width // n
    ff = w_up.shape[1]
    unit = ff // (n * m)
    ff_dev = unit * m
    blk = min(512, row_len)
    mine = lax.axis_index("ctx")
    mine_row = lax.axis_index("row")

    packed = jnp.concatenate([gain_attn, gain_attn_sub, gain_ffn, gain_ffn_sub])
    packed = jnp.pad(packed, (0, -packed.shape[0] % 2048)).reshape(16, -1)
    gains = lax.all_gather(packed, BOTH, axis=0, tiled=True).reshape(n * m, -1).astype(f32)
    g_attn = gains[:, :piece].reshape(width)
    g_sub = gains[:, piece:2 * piece].reshape(width)
    g_ffn = gains[:, 2 * piece:3 * piece].reshape(width)
    g_fsub = lax.dynamic_index_in_dim(gains[:, 3 * piece:3 * piece + unit].reshape(m, n, unit), mine, 1, False).reshape(ff_dev)

    qkv_local = jnp.concatenate([w.reshape(piece, n, heads_dim) for w in (w_query, w_key, w_value)], axis=2)
    qkv_part = lax.all_to_all(qkv_local, "ctx", split_axis=1, concat_axis=0, tiled=True).reshape(n * piece, 3 * heads_dim)
    w_qkv = lax.all_gather(qkv_part, "row", axis=0, tiled=True)
    x_all = gather_ctx(inputs)
    up_local = w_up.reshape(piece, m, n, unit).transpose(0, 2, 1, 3).reshape(piece, n, ff_dev)
    up_part = lax.all_to_all(up_local, "ctx", split_axis=1, concat_axis=0, tiled=True).reshape(n * piece, ff_dev)
    out_all = lax.all_gather(w_out, BOTH, axis=0, tiled=True)
    up_all = lax.all_gather(up_part, "row", axis=0, tiled=True)
    down_all = lax.all_gather(w_down, "row", axis=0, tiled=True)
    dy_all = gather_ctx(out_cotangent).reshape(group, width)

    x_flat = x_all.reshape(group, width).astype(f32)
    x_hat, x_rstd = standardize(x_flat)
    a = (x_hat * g_attn).astype(bf16)
    qkvT = dot(w_qkv, a, "df,td->ft")
    relative, lowest = row_places(doc_len, row_len)
    cosine, sine, factor = xpos_tables(relative.reshape(group))
    inverse = 1.0 / factor
    qT = turn(qkvT[:heads_dim], cosine, sine, factor).astype(bf16)
    kT = turn(qkvT[heads_dim:2 * heads_dim], cosine, sine, inverse).astype(bf16)
    vT = qkvT[2 * heads_dim:].astype(bf16)
    o_heads, oT, lse = attention_fwd(qT, kT, vT, lowest, blk)
    o = lax.all_to_all(o_heads.reshape(rows, row_len, heads_dim), "ctx", split_axis=1, concat_axis=2, tiled=True)
    o = o.reshape(tokens, width).astype(f32)
    o_hat, o_rstd = standardize(o)
    c = (o_hat * g_sub).astype(bf16)
    x_own = inputs.reshape(tokens, width).astype(f32)
    x1 = x_own + dot(c, out_all, "td,de->te")
    x1_hat, x1_rstd = standardize(x1)
    b = (x1_hat * g_ffn).astype(bf16)
    b_all = gather_ctx(b.reshape(rows, local_len, width)).reshape(group, width)

    de = dot(dy_all, down_all, "td,fd->tf")
    h = dot(b_all, up_all, "td,df->tf")
    cdf, pdf = phi_parts(h)
    gel = h * cdf
    d_hat = de * g_fsub
    mean_own = jnp.mean(gel, axis=-1)
    off = gel - mean_own[:, None]
    stats = jnp.stack([mean_own, jnp.sum(off * off, axis=-1), jnp.sum(d_hat, axis=-1), jnp.sum(d_hat * off, axis=-1)])
    stats = lax.all_gather(stats, "ctx", axis=0, tiled=False)
    mean = jnp.mean(stats[:, 0], axis=0)
    shift = stats[:, 0] - mean
    var = (jnp.sum(stats[:, 1], axis=0) + ff_dev * jnp.sum(shift * shift, axis=0)) / ff
    rstd = lax.rsqrt(var + EPS)
    d_mean = jnp.sum(stats[:, 2], axis=0) / ff
    d_corr = rstd * jnp.sum(stats[:, 3] + stats[:, 2] * shift, axis=0) / ff
    hat = (gel - mean[:, None]) * rstd[:, None]
    e = (hat * g_fsub).astype(bf16)
    gain_fsub_part = jnp.sum(de * hat, axis=0)
    d_gel = rstd[:, None] * (d_hat - d_mean[:, None] - hat * d_corr[:, None])
    dh = (d_gel * (cdf + h * pdf)).astype(bf16)
    db_part = dot(dh, up_all, "tf,df->td", bf16)
    db = scatter_ctx(db_part.reshape(rows, row_len, width)).reshape(tokens, width).astype(f32)
    out_part = dot(e, down_all, "tf,fd->td", bf16)
    output = scatter_ctx(out_part.reshape(rows, row_len, width)).reshape(tokens, width).astype(f32)
    output = (x1 + output).astype(bf16).reshape(rows, local_len, width)
    down_part = dot(e, dy_all, "tf,td->fd", bf16)
    down_grad = lax.psum_scatter(down_part, "row", scatter_dimension=0, tiled=True).astype(f32)
    up_grad_part = dot(b_all, dh, "td,tf->df", bf16)
    up_grad_part = lax.psum_scatter(up_grad_part, "row", scatter_dimension=0, tiled=True)
    up_grad = lax.all_to_all(up_grad_part.reshape(n, piece, ff_dev), "ctx", split_axis=0, concat_axis=2, tiled=True)
    up_grad = up_grad.reshape(piece, n, m, unit).transpose(0, 2, 1, 3).reshape(piece, ff).astype(f32)

    dy = out_cotangent.reshape(tokens, width).astype(f32)
    gain_ffn_part = jnp.sum(db * x1_hat, axis=0)
    dx1 = dy + standardize_back(x1_hat, x1_rstd, db * g_ffn)
    dx1b = dx1.astype(bf16)
    dc = dot(dx1b, out_all, "te,de->td")
    gain_sub_part = jnp.sum(dc * o_hat, axis=0)
    d_o = standardize_back(o_hat, o_rstd, dc * g_sub).astype(bf16).reshape(rows, local_len, width)
    do_heads = lax.all_to_all(d_o, "ctx", split_axis=2, concat_axis=1, tiled=True).reshape(group, heads_dim)
    out_grad_part = dot(c, dx1b, "td,te->de", bf16).reshape(m, n, piece, width)
    out_grad = lax.psum_scatter(out_grad_part, "ctx", scatter_dimension=1, tiled=False)
    out_grad = lax.psum_scatter(out_grad, "row", scatter_dimension=0, tiled=False).astype(f32)
    dqT, dkT, dvT = attention_bwd(qT, kT, vT, do_heads, oT, lse, lowest, blk)
    dqT = turn(dqT, cosine, -sine, factor).astype(bf16)
    dkT = turn(dkT, cosine, -sine, inverse).astype(bf16)
    dqkvT = jnp.concatenate([dqT, dkT, dvT], axis=0)
    da_part = dot(dqkvT, w_qkv, "ft,df->td")
    da = scatter_ctx(da_part.astype(bf16).reshape(rows, row_len, width)).reshape(tokens, width).astype(f32)
    gain_attn_part = jnp.sum(da_part * x_hat, axis=0)
    qkv_grad = dot(a, dqkvT, "td,ft->df", bf16)
    qkv_grad = lax.psum_scatter(qkv_grad, "row", scatter_dimension=0, tiled=True)
    qkv_grad = lax.all_to_all(qkv_grad.reshape(n, piece, 3 * heads_dim), "ctx", split_axis=0, concat_axis=2, tiled=True)
    qkv_grad = qkv_grad.reshape(piece, n, 3, heads_dim).astype(f32)
    query_grad, key_grad, value_grad = (qkv_grad[:, :, i].reshape(piece, width) for i in range(3))
    own_hat, own_rstd = standardize(x_own)
    input_grad = (dx1 + standardize_back(own_hat, own_rstd, da * g_attn)).reshape(rows, local_len, width)

    gain_parts = jnp.concatenate([gain_attn_part, gain_sub_part, gain_ffn_part, gain_fsub_part])
    gain_all = lax.all_gather(gain_parts, BOTH, axis=0, tiled=False)
    place = mine_row * n + mine
    wide = jnp.sum(gain_all[:, :3 * width], axis=0).reshape(3, n * m, piece)
    wide = lax.dynamic_index_in_dim(wide, place, 1, False)
    narrow = lax.dynamic_index_in_dim(gain_all[:, 3 * width:].reshape(m, n, m, unit), mine, 1, False)
    narrow = jnp.sum(lax.dynamic_index_in_dim(narrow, mine_row, 1, False), axis=0)
    return (output, input_grad, query_grad, key_grad, value_grad, out_grad, up_grad, down_grad,
            wide[0], wide[1], wide[2], narrow)


def solution(mesh):
    split = P(BOTH, None)
    acts = P("row", "ctx", None)
    gain = P(BOTH)
    return jax.shard_map(
        body,
        mesh=mesh,
        in_specs=(acts, P("row", None)) + (split,) * 6 + (gain,) * 4 + (acts,),
        out_specs=(acts, acts) + (split,) * 6 + (gain,) * 4,
        check_vma=False,
    )
```

```python
import functools

import jax
import jax.numpy as jnp
from jax import lax
from jax.experimental import pallas as pl
from jax.experimental.pallas import tpu as pltpu
from jax.sharding import PartitionSpec as P

bf16 = jnp.bfloat16
f32 = jnp.float32
HEAD_DIM = 64
HALF = HEAD_DIM // 2
PAIR = 2 * HEAD_DIM
LOG2E = 1.4426950408889634
NEG = -1e30
ROW_LEN = 2048
XPOS_BASE = 512
EPS = 1e-5
BOTH = ("row", "ctx")


def walk(span_ref, qb, step):
    first = span_ref[2 + 2 * (qb)]
    clear = span_ref[3 + 2 * (qb)]

    def edge(t, carry):
        step(jnp.where(t < clear - first, first + t, qb), True)
        return carry

    def plain(kb, carry):
        step(kb, False)
        return carry

    lax.fori_loop(0, clear - first + 1, edge, 0)
    lax.fori_loop(clear, qb, plain, 0)


def allowed(lowest, kb, qb, blk):
    key = kb * blk + lax.broadcasted_iota(jnp.int32, (blk, blk), 0)
    query = qb * blk + lax.broadcasted_iota(jnp.int32, (blk, blk), 1)
    return (key <= query) & (key >= lowest)


def forward_kernel(nh, blk, unit, span_ref, q0_ref, q1_ref, k0_ref, k1_ref, v0_ref, v1_ref, table_ref, lo_ref,
                   o_ref, oT_ref, lse_ref, qT_ref, kT_ref, vT_ref, k_s, qm_s, acc_s, m_s, l_s):
    qb = pl.program_id(0)
    dim = nh * HEAD_DIM
    length = kT_ref.shape[1]
    core, place = span_ref[0], span_ref[1]
    spots = blk // (2 * unit)
    inner = lax.rem(place, spots)

    def turned(values, at, kind):
        cosine = table_ref[2 * kind, :, pl.ds(at, unit)]
        sine = table_ref[2 * kind + 1, :, pl.ds(at, unit)]
        out = []
        for h in range(nh):
            one = values[h * HEAD_DIM:h * HEAD_DIM + HALF]
            two = values[h * HEAD_DIM + HALF:(h + 1) * HEAD_DIM]
            out += [one * cosine - two * sine, two * cosine + one * sine]
        return jnp.concatenate(out, axis=0).astype(bf16)

    @pl.when(qb == 0)
    def _():
        def load(j, carry):
            src = pl.multiple_of((j ^ place) * unit, unit)
            for half, ref, v_ref in ((0, k0_ref, v0_ref), (1, k1_ref, v1_ref)):
                at = pl.multiple_of((2 * j + (core ^ half)) * unit, unit)
                key = turned(ref[:, pl.ds(src, unit)], at, 1)
                kT_ref[:, pl.ds(at, unit)] = key
                k_s[pl.ds(at, unit), :] = key.T
                vT_ref[:, pl.ds(at, unit)] = v_ref[:, pl.ds(src, unit)].astype(bf16)
            return carry

        lax.fori_loop(0, length // (2 * unit), load, 0)

    for u in range(spots):
        src = pl.multiple_of((u ^ inner) * unit, unit)
        for half, ref in ((0, q0_ref), (1, q1_ref)):
            at = pl.multiple_of((2 * u + (core ^ half)) * unit, unit)
            qT_ref[:, pl.ds(at, unit)] = turned(ref[:, pl.ds(src, unit)], pl.multiple_of(qb * blk + at, unit), 0)
    for h in range(nh):
        own = h % 2
        qm_s[h, pl.ds(own * HEAD_DIM, HEAD_DIM), :] = qT_ref[pl.ds(h * HEAD_DIM, HEAD_DIM), :]
        qm_s[h, pl.ds((1 - own) * HEAD_DIM, HEAD_DIM), :] = jnp.zeros((HEAD_DIM, blk), bf16)
    acc_s[...] = jnp.zeros_like(acc_s)
    m_s[...] = jnp.full_like(m_s, NEG)
    l_s[...] = jnp.zeros_like(l_s)
    lowest = lo_ref[...]

    def step(kb, masked):
        at = pl.multiple_of(kb * blk, blk)
        if masked:
            ok = allowed(lowest, kb, qb, blk)
        for h in range(nh):
            rows = pl.ds(h * HEAD_DIM, HEAD_DIM)
            s = jnp.dot(k_s[pl.ds(at, blk), pl.ds((h // 2) * PAIR, PAIR)], qm_s[h], preferred_element_type=f32)
            s = s * (LOG2E * HEAD_DIM**-0.5)
            if masked:
                s = jnp.where(ok, s, NEG)
            before = m_s[h:h + 1, :]
            now = jnp.maximum(before, jnp.max(s, axis=0, keepdims=True))
            p = jnp.exp2(s - now)
            fade = jnp.exp2(before - now)
            m_s[h:h + 1, :] = now
            l_s[h:h + 1, :] = l_s[h:h + 1, :] * fade + jnp.sum(p, axis=0, keepdims=True)
            acc_s[rows, :] = acc_s[rows, :] * fade + jnp.dot(
                vT_ref[rows, pl.ds(at, blk)], p.astype(bf16), preferred_element_type=f32)

    walk(span_ref, qb, step)
    for h in range(nh):
        rows = pl.ds(h * HEAD_DIM, HEAD_DIM)
        oT_ref[rows, :] = acc_s[rows, :] / l_s[h:h + 1, :]
        lse_ref[h:h + 1, :] = m_s[h:h + 1, :] + jnp.log2(l_s[h:h + 1, :])
    o_ref[...] = oT_ref[...].T.astype(bf16)


def backward_kernel(nh, blk, unit, span_ref, qT_ref, kT_ref, vT_ref, do_ref, oT_ref, lse_ref, table_ref, lo_ref,
                    old0_ref, old1_ref, d0_ref, d1_ref, k_s, v_s, qm_s, dm_s, qn_s, dn_s, acc_s, dk_s, dv_s, p_s, ds_s, dl_s):
    qb = pl.program_id(0)
    dim = nh * HEAD_DIM
    length = kT_ref.shape[1]
    count = length // blk
    scale = HEAD_DIM**-0.5
    core, place = span_ref[0], span_ref[1]

    @pl.when(qb == 0)
    def _():
        for c in range(count):
            k_s[pl.ds(c * blk, blk), :] = kT_ref[:, pl.ds(c * blk, blk)].T
            v_s[pl.ds(c * blk, blk), :] = vT_ref[:, pl.ds(c * blk, blk)].T
        dk_s[...] = jnp.zeros_like(dk_s)
        dv_s[...] = jnp.zeros_like(dv_s)

    doT = do_ref[...].T
    q = qT_ref[...].T
    lane = lax.broadcasted_iota(jnp.int32, (blk, PAIR), 1)
    prod = doT.astype(f32) * oT_ref[...]
    for h in range(nh):
        own = h % 2
        rows = slice(h * HEAD_DIM, (h + 1) * HEAD_DIM)
        zero = jnp.zeros((HEAD_DIM, blk), bf16)
        qm_s[h, pl.ds(own * HEAD_DIM, HEAD_DIM), :] = qT_ref[pl.ds(h * HEAD_DIM, HEAD_DIM), :]
        qm_s[h, pl.ds((1 - own) * HEAD_DIM, HEAD_DIM), :] = zero
        dm_s[h, pl.ds(own * HEAD_DIM, HEAD_DIM), :] = doT[rows, :]
        dm_s[h, pl.ds((1 - own) * HEAD_DIM, HEAD_DIM), :] = zero
        mine = (lane // HEAD_DIM) == own
        pair = slice((h // 2) * PAIR, (h // 2) * PAIR + PAIR)
        qn_s[h // 2, pl.ds(own * blk, blk), :] = jnp.where(mine, q[:, pair], jnp.zeros((), bf16))
        dn_s[h // 2, pl.ds(own * blk, blk), :] = jnp.where(mine, do_ref[:, pair], jnp.zeros((), bf16))
        dl_s[h:h + 1, :] = jnp.sum(prod[rows, :], axis=0, keepdims=True)
    acc_s[...] = jnp.zeros_like(acc_s)
    lowest = lo_ref[...]

    def step(kb, masked):
        at = pl.multiple_of(kb * blk, blk)
        if masked:
            ok = allowed(lowest, kb, qb, blk)
        for g in range(nh // 2):
            lanes = pl.ds(g * PAIR, PAIR)
            for own in range(2):
                h = 2 * g + own
                rows = pl.ds(h * HEAD_DIM, HEAD_DIM)
                s = jnp.dot(k_s[pl.ds(at, blk), lanes], qm_s[h], preferred_element_type=f32) * (LOG2E * scale)
                p = jnp.exp2(s - lse_ref[h:h + 1, :])
                if masked:
                    p = jnp.where(ok, p, 0.0)
                dp = jnp.dot(v_s[pl.ds(at, blk), lanes], dm_s[h], preferred_element_type=f32)
                ds = (p * (dp - dl_s[h:h + 1, :])).astype(bf16)
                p_s[g, :, pl.ds(own * blk, blk)] = p.astype(bf16)
                ds_s[g, :, pl.ds(own * blk, blk)] = ds
                acc_s[rows, :] += jnp.dot(kT_ref[rows, pl.ds(at, blk)], ds, preferred_element_type=f32)
            dv_s[pl.ds(at, blk), lanes] += jnp.dot(p_s[g], dn_s[g], preferred_element_type=f32)
            dk_s[pl.ds(at, blk), lanes] += jnp.dot(ds_s[g], qn_s[g], preferred_element_type=f32)

    walk(span_ref, qb, step)

    def turned_back(values, at, size, kind):
        cosine = table_ref[2 * kind, :, pl.ds(at, size)] * scale
        sine = table_ref[2 * kind + 1, :, pl.ds(at, size)] * scale
        out = []
        for h in range(nh):
            one = values[h * HEAD_DIM:h * HEAD_DIM + HALF]
            two = values[h * HEAD_DIM + HALF:(h + 1) * HEAD_DIM]
            out += [one * cosine + two * sine, two * cosine - one * sine]
        return jnp.concatenate(out, axis=0).T.astype(bf16)

    spots = blk // (2 * unit)
    for u in range(spots):
        dst = pl.multiple_of(((qb * spots + u) ^ place) * unit, unit)
        for half, ref in ((0, d0_ref), (1, d1_ref)):
            at = pl.multiple_of((2 * u + (core ^ half)) * unit, unit)
            ref[pl.ds(dst, unit), pl.ds(0, dim)] = turned_back(
                acc_s[:, pl.ds(at, unit)], pl.multiple_of(qb * blk + at, unit), unit, 0)

    @pl.when(qb == count - 1)
    def _():
        def store(j, carry):
            dst = pl.multiple_of((j ^ place) * unit, unit)
            for half, ref in ((0, d0_ref), (1, d1_ref)):
                at = pl.multiple_of((2 * j + (core ^ half)) * unit, unit)
                ref[pl.ds(dst, unit), pl.ds(dim, dim)] = turned_back(dk_s[pl.ds(at, unit), :].T, at, unit, 1)
                ref[pl.ds(dst, unit), pl.ds(2 * dim, dim)] = dv_s[pl.ds(at, unit), :].astype(bf16)
            return carry

        lax.fori_loop(0, length // (2 * unit), store, 0)


PARAMS = pltpu.CompilerParams(dimension_semantics=("arbitrary",), vmem_limit_bytes=60 * 2**20)


def span_of(lowest, blk, core, place):
    count = lowest.shape[0] // blk
    blocks = lowest.reshape(count, blk)
    own = jnp.arange(count, dtype=jnp.int32)
    first = jnp.minimum(blocks[:, 0] // blk, own)
    clear = jnp.minimum((blocks[:, -1] + blk - 1) // blk, own)
    both = jnp.stack([first, clear], axis=-1).reshape(-1)
    return jnp.concatenate([jnp.stack([core, place]), both]).astype(jnp.int32)


def attention_forward(row, half0, half1, table, lowest, span, blk, unit):
    length = lowest.shape[0]
    dim = half0.shape[0] // 3
    nh, count = dim // HEAD_DIM, length // blk
    spots = blk // (2 * unit)
    sds = jax.ShapeDtypeStruct
    pick = pl.BlockSpec((dim, blk // 2), lambda q, s: (0, row * count + (q ^ lax.div(s[1], spots))))
    keys = pl.BlockSpec((dim, length // 2), lambda q, s: (1, row))
    values = pl.BlockSpec((dim, length // 2), lambda q, s: (2, row))
    wide = pl.BlockSpec((dim, length), lambda q, s: (0, 0))
    cut = pl.BlockSpec((dim, blk), lambda q, s: (0, q))
    return pl.pallas_call(
        functools.partial(forward_kernel, nh, blk, unit),
        out_shape=(sds((length, dim), bf16), sds((dim, length), f32), sds((nh, length), f32),
                   sds((dim, length), bf16), sds((dim, length), bf16), sds((dim, length), bf16)),
        grid_spec=pltpu.PrefetchScalarGridSpec(
            num_scalar_prefetch=1, grid=(count,),
            in_specs=[pick, pick, keys, keys, values, values,
                      pl.BlockSpec((4, HALF, length), lambda q, s: (0, 0, 0)),
                      pl.BlockSpec((1, blk), lambda q, s: (0, q))],
            out_specs=[pl.BlockSpec((blk, dim), lambda q, s: (q, 0)), cut,
                       pl.BlockSpec((nh, blk), lambda q, s: (0, q)), cut, wide, wide],
            scratch_shapes=[pltpu.VMEM((length, dim), bf16), pltpu.VMEM((nh, PAIR, blk), bf16), pltpu.VMEM((dim, blk), f32),
                            pltpu.VMEM((8, blk), f32), pltpu.VMEM((8, blk), f32)]),
        compiler_params=PARAMS, name="attention_forward",
        cost_estimate=pl.CostEstimate(flops=4 * 4 * dim * length * length // 2, bytes_accessed=10 * 2**20,
                                      transcendentals=nh * length * length // 2),
    )(span, half0, half1, half0, half1, half0, half1, table, lowest[None, :])


def attention_backward(row, rows, saved, do, table, lowest, span, blk, unit, before):
    oT, lse, qT, kT, vT = saved
    length = lowest.shape[0]
    dim = qT.shape[0]
    nh, count = dim // HEAD_DIM, length // blk
    sds = jax.ShapeDtypeStruct
    cut = pl.BlockSpec((dim, blk), lambda q, s: (0, q))
    wide = pl.BlockSpec((dim, length), lambda q, s: (0, 0))
    grad = pl.BlockSpec((length // 2, 3 * dim), lambda q, s: (row, 0))
    whole = sds((rows * length // 2, 3 * dim), bf16)
    kernel = functools.partial(backward_kernel, nh, blk, unit)
    if before is None:
        def call(span_ref, *refs):
            kernel(span_ref, *refs[:8], None, None, *refs[8:])
    else:
        call = kernel
    return pl.pallas_call(
        call,
        out_shape=(whole, whole),
        grid_spec=pltpu.PrefetchScalarGridSpec(
            num_scalar_prefetch=1, grid=(count,),
            in_specs=[cut, wide, wide, pl.BlockSpec((blk, dim), lambda q, s: (q, 0)), cut,
                      pl.BlockSpec((nh, blk), lambda q, s: (0, q)),
                      pl.BlockSpec((4, HALF, length), lambda q, s: (0, 0, 0)),
                      pl.BlockSpec((1, blk), lambda q, s: (0, q))]
            + ([] if before is None else [pl.BlockSpec(memory_space=pl.ANY)] * 2),
            out_specs=[grad, grad],
            scratch_shapes=[pltpu.VMEM((length, dim), bf16), pltpu.VMEM((length, dim), bf16),
                            pltpu.VMEM((nh, PAIR, blk), bf16), pltpu.VMEM((nh, PAIR, blk), bf16),
                            pltpu.VMEM((nh // 2, 2 * blk, PAIR), bf16), pltpu.VMEM((nh // 2, 2 * blk, PAIR), bf16),
                            pltpu.VMEM((dim, blk), f32), pltpu.VMEM((length, dim), f32), pltpu.VMEM((length, dim), f32),
                            pltpu.VMEM((nh // 2, blk, 2 * blk), bf16), pltpu.VMEM((nh // 2, blk, 2 * blk), bf16),
                            pltpu.VMEM((8, blk), f32)]),
        compiler_params=PARAMS, name="attention_backward",
        input_output_aliases={} if before is None else {9: 0, 10: 1},
        cost_estimate=pl.CostEstimate(flops=10 * 4 * dim * length * length // 2, bytes_accessed=20 * 2**20,
                                      transcendentals=nh * length * length // 2),
    )(span, qT, kT, vT, do, oT, lse, table, lowest[None, :], *(before or ()))


def hat_of(values):
    center = values - jnp.mean(values, axis=-1, keepdims=True)
    rstd = lax.rsqrt(jnp.mean(center * center, axis=-1, keepdims=True) + EPS)
    return center * rstd, rstd


def hat_back(hat, rstd, grad):
    return rstd * (grad - jnp.mean(grad, axis=-1, keepdims=True) - hat * jnp.mean(grad * hat, axis=-1, keepdims=True))


def wide_row(o_ref):
    return jnp.concatenate([o_ref[i] for i in range(o_ref.shape[0])], axis=1).astype(f32)


def middle_forward_kernel(o_ref, x_ref, w_ref, c_ref, x1_ref, b_ref):
    c = hat_of(wide_row(o_ref))[0].astype(bf16)
    c_ref[...] = c
    x1 = x_ref[...].astype(f32) + jnp.dot(c, w_ref[...], preferred_element_type=f32)
    x1_ref[...] = x1
    b_ref[...] = hat_of(x1)[0].astype(bf16)


def middle_forward(o, x, w):
    n, size, dim = o.shape
    width = n * dim
    step = min(128, size)
    sds = jax.ShapeDtypeStruct
    flat = pl.BlockSpec((step, width), lambda t: (t, 0))
    return pl.pallas_call(
        middle_forward_kernel,
        out_shape=(sds((size, width), bf16), sds((size, width), f32), sds((size, width), bf16)),
        grid=(size // step,),
        in_specs=[pl.BlockSpec((n, step, dim), lambda t: (0, t, 0)), flat,
                  pl.BlockSpec((width, width), lambda t: (0, 0))],
        out_specs=(flat, flat, flat),
        compiler_params=PARAMS, name="middle_forward",
        cost_estimate=pl.CostEstimate(flops=2 * size * width * width, bytes_accessed=14 * 2**20, transcendentals=0),
    )(o, x, w)


def middle_backward_kernel(o_ref, x1_ref, db_ref, dy_ref, w_ref, dx_ref, low_ref, do_ref):
    hat, rstd = hat_of(x1_ref[...])
    dx1 = dy_ref[...].astype(f32) + hat_back(hat, rstd, db_ref[...])
    dx_ref[...] = dx1
    low_ref[...] = dx1.astype(bf16)
    dc = jnp.dot(dx1.astype(bf16), w_ref[...], preferred_element_type=f32)
    hat, rstd = hat_of(wide_row(o_ref))
    d_o = hat_back(hat, rstd, dc).astype(bf16)
    dim = do_ref.shape[2]
    for i in range(do_ref.shape[0]):
        do_ref[i] = d_o[:, i * dim:(i + 1) * dim]


def middle_backward(row, o, x1, db, dy, w):
    n, size, dim = o.shape
    width = n * dim
    step = min(128, size)
    sds = jax.ShapeDtypeStruct
    flat = pl.BlockSpec((step, width), lambda t: (t, 0))
    part = pl.BlockSpec((n, step, dim), lambda t: (0, t, 0))
    return pl.pallas_call(
        middle_backward_kernel,
        out_shape=(sds((size, width), f32), sds((size, width), bf16), sds((n, size, dim), bf16)),
        grid=(size // step,),
        in_specs=[part, flat, pl.BlockSpec((step, width), lambda t: (row * (size // step) + t, 0)), flat,
                  pl.BlockSpec((width, width), lambda t: (0, 0))],
        out_specs=(flat, flat, part),
        compiler_params=PARAMS, name="middle_backward",
        cost_estimate=pl.CostEstimate(flops=2 * size * width * width, bytes_accessed=16 * 2**20, transcendentals=0),
    )(o, x1, db, dy, w)


def ways(row, n):
    bits = [1 << k for k in range(1, n.bit_length() - 1)]
    return bits if row % 2 == 0 else bits[::-1]


def product_sum_kernel(n, rows, cols, x0_ref, x1_ref, w_ref, o_ref, part_s, core_s, sum_s, got_s, send_sem, recv_sem):
    mine = lax.axis_index("ctx")
    spots = n // 2
    size = x0_ref.shape[0] // (rows * spots)
    width = w_ref.shape[1]
    barrier = pltpu.get_barrier_semaphore()
    bits = [1] + ways(0, n)
    for bit in bits:
        pl.semaphore_signal(barrier, inc=1, device_id={"ctx": mine ^ bit}, device_id_type=pl.DeviceIdType.MESH)
    pl.semaphore_wait(barrier, len(bits))
    copies = []

    def send(src, dst, bit):
        at = len(copies)
        copy = pltpu.make_async_remote_copy(
            src_ref=src, dst_ref=dst, send_sem=send_sem.at[at], recv_sem=recv_sem.at[at],
            device_id={"ctx": mine ^ bit}, device_id_type=pl.DeviceIdType.MESH)
        copy.start()
        copies.append(copy)
        return copy

    def key(row, k):
        return [-(k & (bit >> 1)) for bit in ways(row, n)]

    orders = []
    for r in range(rows):
        way = [bit >> 1 for bit in ways(r, n)]
        orders.append(sorted(range(spots), key=lambda k: [0 if k & bit else 1 for bit in way]))
    todo = [(r, orders[r][t]) for t in range(spots) for r in range(rows)]
    inbox, slot, slots = {}, {}, 0

    def product(x_ref, r, k, finish):
        begin = (r * spots + k) * size

        @pl.loop(0, width // cols)
        def _(c):
            at = pl.ds(pl.multiple_of(c * cols, cols), cols)
            finish(at, jnp.dot(x_ref[pl.ds(begin, size), :], w_ref[:, at], preferred_element_type=f32))

    def pair(r, k):
        spot = r * spots + k

        def keep(at, value):
            part_s[spot, :, at] = value.astype(bf16)

        product(x1_ref, r, k, keep)
        inbox[r, k] = send(part_s.at[spot], core_s.at[spot], 1)

    def own(r, k):
        spot = r * spots + k
        inbox[r, k].wait_recv()

        def add(at, value):
            sum_s[spot, :, at] = (value + core_s[spot, :, at].astype(f32)).astype(bf16)

        product(x0_ref, r, k, add)

    def pass_on(r, k, stage):
        nonlocal slots
        bit = ways(r, n)[stage]
        if k & (bit >> 1):
            inbox[r, k ^ (bit >> 1), stage] = (send(sum_s.at[r * spots + k], got_s.at[slots], bit), slots)
            slots += 1

    group = max(rows * spots // 2, 1)
    for begin in range(0, len(todo), group):
        for r, k in todo[begin:begin + group]:
            pair(r, k)
        for r, k in todo[begin:begin + group]:
            own(r, k)
            pass_on(r, k, 0)
    stages = len(bits) - 1
    for stage in range(stages):
        for r, k in todo:
            way = [bit >> 1 for bit in ways(r, n)]
            if any(k & bit for bit in way[:stage + 1]):
                continue
            copy, at = inbox[r, k, stage]
            copy.wait_recv()
            spot = r * spots + k
            if stage == stages - 1:
                o_ref[pl.ds(r * size, size), :] = sum_s[spot].astype(f32) + got_s[at].astype(f32)
            else:
                sum_s[spot] = (sum_s[spot].astype(f32) + got_s[at].astype(f32)).astype(bf16)
                pass_on(r, k, stage + 1)
    for copy in copies:
        copy.wait_send()


def product_sum(x0, x1, w, rows, n, collective_id):
    size = x0.shape[0] // (rows * (n // 2))
    width = w.shape[1]
    count = rows * (n // 2)
    moves = count + rows * (n // 2 - 1)
    vmem = pl.BlockSpec(memory_space=pltpu.VMEM)
    flops = 4 * x0.shape[0] * x0.shape[1] * width
    return pl.pallas_call(
        functools.partial(product_sum_kernel, n, rows, min(512, width)),
        out_shape=jax.ShapeDtypeStruct((rows * size, width), f32),
        in_specs=[vmem] * 3, out_specs=vmem,
        scratch_shapes=[pltpu.VMEM((count, size, width), bf16), pltpu.VMEM((count, size, width), bf16),
                        pltpu.VMEM((count, size, width), bf16), pltpu.VMEM((moves - count, size, width), bf16),
                        pltpu.SemaphoreType.DMA((moves,)), pltpu.SemaphoreType.DMA((moves,))],
        compiler_params=pltpu.CompilerParams(collective_id=collective_id, has_side_effects=True, vmem_limit_bytes=60 * 2**20),
        name="product_sum",
        cost_estimate=pl.CostEstimate(flops=4 * flops, bytes_accessed=20 * 2**20, transcendentals=0),
    )(x0, x1, w)


def standardize(values):
    center = values - jnp.mean(values, axis=-1, keepdims=True)
    spread = jnp.mean(center * center, axis=-1, keepdims=True)
    rstd = lax.rsqrt(spread + EPS)
    return center * rstd, rstd


def standardize_back(hat, rstd, grad):
    return rstd * (grad - jnp.mean(grad, axis=-1, keepdims=True) - hat * jnp.mean(grad * hat, axis=-1, keepdims=True))


def row_places(lengths, row_len):
    places = jnp.arange(row_len, dtype=jnp.int32)
    ends = jnp.cumsum(lengths, axis=-1)
    passed = ends[:, None, :] <= places[None, :, None]
    starts = jnp.sum(jnp.where(passed, lengths[:, None, :], 0), axis=-1)
    valid = places[None, :] < ends[:, -1:]
    lowest = jnp.where(valid, starts, places[None, :]).astype(jnp.int32)
    return (places[None, :] - starts).astype(f32), lowest


def xpos_tables(relative):
    ladder = jnp.arange(HALF, dtype=f32) / HALF
    rate = jnp.power(10000.0, -ladder)
    base = (ladder + 0.4) / 1.4
    angles = rate[None, :, None] * relative[:, None, :]
    power = (relative[:, None, :] - ROW_LEN / 2) / XPOS_BASE
    factor = jnp.power(base[None, :, None], power)
    cosine, sine = jnp.cos(angles), jnp.sin(angles)
    return jnp.stack([cosine * factor, sine * factor, cosine / factor, sine / factor], axis=1)


def dot(a, b, spec, kind=f32):
    return jnp.einsum(spec, a, b, preferred_element_type=f32).astype(kind)


def swap(x, bit):
    n = lax.axis_size("ctx")
    return lax.ppermute(x, "ctx", [(i, i ^ bit) for i in range(n)])


def exchange(blocks):
    n = lax.axis_size("ctx")
    mine = lax.axis_index("ctx")
    out = jnp.zeros_like(blocks)
    for bit in range(n):
        block = lax.dynamic_index_in_dim(blocks, mine ^ bit, 0, False)
        block = swap(block, bit) if bit else block
        out = lax.dynamic_update_index_in_dim(out, block, mine ^ bit, 0)
    return out


def after(x, *others):
    return lax.optimization_barrier((x, *others))[0]


def gather_start(x):
    return [{0: x[r]} for r in range(x.shape[0])]


def gather_step(held, step):
    n = lax.axis_size("ctx")
    out = []
    for r, parts in enumerate(held):
        bit = ways(r, n)[step]
        out.append({**parts, **{k | bit: swap(v, bit) for k, v in parts.items()}})
    return out


def gather_steps():
    return lax.axis_size("ctx").bit_length() - 2


def gather_end(held):
    return jnp.concatenate([parts[k] for parts in held for k in sorted(parts)], axis=0)


def gather_half(x):
    held = gather_start(x)
    for step in range(gather_steps()):
        held = gather_step(held, step)
    return gather_end(held)


def plus(a, b, kind=bf16):
    return (a.astype(f32) + b.astype(f32)).astype(kind)


def reduce_start(half0, half1, rows):
    n = lax.axis_size("ctx")
    width = half0.shape[-1]
    both = plus(half0, swap(half1, 1)).reshape(rows, n // 2, -1, width)
    return [{2 * k: both[r, k] for k in range(n // 2)} for r in range(rows)]


def reduce_step(held, step):
    n = lax.axis_size("ctx")
    out = []
    for r, parts in enumerate(held):
        bit = ways(r, n)[step]
        kind = bf16 if len(parts) > 2 else f32
        out.append({k: plus(v, swap(parts[k | bit], bit), kind) for k, v in parts.items() if not k & bit})
    return out


def reduce_end(held):
    return jnp.concatenate([parts[0] for parts in held], axis=0)


def reduce_halves(half0, half1, rows):
    held = reduce_start(half0, half1, rows)
    for step in range(gather_steps()):
        held = reduce_step(held, step)
    return reduce_end(held)


def body(inputs, doc_len, w_query, w_key, w_value, w_out, w_up, w_down, gain_attn, gain_attn_sub, gain_ffn,
         gain_ffn_sub, out_cotangent):
    rows, local_len, width = inputs.shape
    n, m = lax.axis_size("ctx"), lax.axis_size("row")
    row_len = local_len * n
    tokens, half = rows * local_len, rows * row_len // 2
    piece = w_query.shape[0]
    heads_dim = width // n
    ff = w_up.shape[1]
    unit = ff // (n * m)
    ff_dev = unit * m
    blk = min(512, row_len)
    mine = lax.axis_index("ctx")
    core, place = mine & 1, mine >> 1

    def scaled(w, gain):
        return (w.astype(f32) * gain.astype(f32)[:, None]).astype(bf16)

    x_own = inputs.reshape(tokens, width).astype(f32)
    x_hat, x_rstd = standardize(x_own)
    x_low = x_hat.astype(bf16)
    xh0 = gather_half(x_low.reshape(rows, local_len, width))
    xh1 = swap(xh0, 1)

    qkv_local = jnp.concatenate(
        [scaled(w, gain_attn).reshape(piece, n, heads_dim) for w in (w_query, w_key, w_value)], axis=2)
    qkv_part = exchange(qkv_local.transpose(1, 0, 2)).reshape(n * piece, 3 * heads_dim)
    w_qkv = lax.all_gather(qkv_part, "row", axis=0, tiled=True)
    out_all = lax.all_gather(scaled(w_out, gain_attn_sub), BOTH, axis=0, tiled=True)

    relative, lowest = row_places(doc_len, row_len)
    table = xpos_tables(relative)
    span = [span_of(lowest[r], blk, core, place) for r in range(rows)]
    qkv0 = dot(w_qkv, xh0, "df,td->ft")
    qkv1 = dot(w_qkv, xh1, "df,td->ft")
    qkv0, qkv1, w_up_in, cot = lax.optimization_barrier((qkv0, qkv1, w_up, out_cotangent))
    up_local = scaled(w_up_in, gain_ffn).reshape(piece, m, n, unit).transpose(2, 0, 1, 3).reshape(n, piece, ff_dev)
    up_part = lax.all_to_all(up_local, "ctx", split_axis=0, concat_axis=0, tiled=True).reshape(n * piece, ff_dev)
    dy_held = gather_step(gather_start(cot), 0)
    dy_steps = gather_steps()
    saved, o = [], []
    for r in range(rows):
        o_row, *kept = attention_forward(r, qkv0, qkv1, table[r], lowest[r], span[r], blk, local_len)
        if r == 0:
            o_row, kept, qkv0, qkv1, dy_held, out_all = lax.optimization_barrier((o_row, kept, qkv0, qkv1, dy_held, out_all))
            down_all = lax.all_gather(after(scaled(w_down, gain_ffn_sub), out_all), "row", axis=0, tiled=True)
            for step in range(1, dy_steps):
                dy_held = gather_step(dy_held, step)
        if r == rows - 1:
            o_row, o = lax.optimization_barrier((o_row, o))
        saved.append(kept)
        o.append(lax.all_to_all(o_row.reshape(n, local_len, heads_dim), "ctx", split_axis=0, concat_axis=0, tiled=True))
    o, down_all, up_part = lax.optimization_barrier((o, down_all, up_part))
    up_all = lax.all_gather(up_part, "row", axis=0, tiled=True)
    c, x1, b_low = zip(*[middle_forward(o[r], inputs[r], out_all) for r in range(rows)])
    b_low, dy_held = lax.optimization_barrier((b_low, dy_held))
    dy0 = gather_end(dy_held)
    dy1 = swap(dy0, 1)
    b_held = gather_step([{0: v} for v in b_low], 0)
    d_hat0 = dot(dy0, down_all, "td,fd->tf")
    b_held, d_hat0 = lax.optimization_barrier((b_held, d_hat0))
    for step in range(1, gather_steps()):
        b_held = gather_step(b_held, step)
    d_hat1 = dot(dy1, down_all, "td,fd->tf")
    b_held, d_hat1 = lax.optimization_barrier((b_held, d_hat1))
    b0 = gather_end(b_held)
    b1 = swap(b0, 1)

    def activate(b):
        h = dot(b, up_all, "td,df->tf")
        return h, 0.5 * (1.0 + lax.erf(h * (2.0**-0.5)))

    def own_stats(h, cdf, d_hat):
        gel = h * cdf
        mean = jnp.mean(gel, axis=-1)
        off = gel - mean[:, None]
        return jnp.stack([mean, jnp.sum(off * off, axis=-1), jnp.sum(d_hat, axis=-1), jnp.sum(d_hat * off, axis=-1)])

    h0, cdf0 = activate(b0)
    h1, cdf1 = activate(b1)
    stats = jnp.stack([own_stats(h0, cdf0, d_hat0), own_stats(h1, cdf1, d_hat1)], axis=1)
    order = jnp.arange(n // 2, dtype=jnp.int32) ^ place
    halves = jnp.arange(2, dtype=jnp.int32) ^ core

    def reorder(v):
        v = v.reshape(v.shape[0], 2, rows, n // 2, local_len)
        return jnp.take(jnp.take(v, halves, axis=1), order, axis=3).reshape(v.shape[0], 2 * half)

    stats = lax.all_gather(reorder(stats.reshape(4, 2 * half)), "ctx", axis=0, tiled=False)
    mean = jnp.mean(stats[:, 0], axis=0)
    shift = stats[:, 0] - mean
    var = (jnp.sum(stats[:, 1], axis=0) + ff_dev * jnp.sum(shift * shift, axis=0)) / ff
    rstd = lax.rsqrt(var + EPS)
    d_mean = jnp.sum(stats[:, 2], axis=0) / ff
    d_corr = rstd * jnp.sum(stats[:, 3] + stats[:, 2] * shift, axis=0) / ff
    merged = reorder(jnp.stack([mean, rstd, d_mean, d_corr])).reshape(4, 2, half, 1)

    def finish(h, cdf, d_hat, which):
        mean, rstd, d_mean, d_corr = (merged[k, which] for k in range(4))
        hat = (h * cdf - mean) * rstd
        d_gel = rstd * (d_hat - d_mean - hat * d_corr)
        pdf = jnp.exp(-0.5 * h * h) * 0.3989422804014327
        return hat.astype(bf16), (d_gel * (cdf + h * pdf)).astype(bf16)

    e0, dh0 = finish(h0, cdf0, d_hat0, 0)
    e1, dh1 = finish(h1, cdf1, d_hat1, 1)
    down_part = (dot(e0, dy0, "tf,td->fd") + dot(e1, dy1, "tf,td->fd")).astype(bf16)
    up_part = (dot(b0, dh0, "td,tf->df") + dot(b1, dh1, "td,tf->df")).astype(bf16)
    e0, e1, dh0, dh1, down_part, up_part = lax.optimization_barrier((e0, e1, dh0, dh1, down_part, up_part))
    down_sum = lax.psum_scatter(down_part, "row", scatter_dimension=0, tiled=True)
    db = product_sum(dh0, dh1, up_all.T, rows, n, 1)
    e0, e1, db, up_part, down_sum = lax.optimization_barrier((e0, e1, db, up_part, down_sum))
    down_raw = down_sum.astype(f32)
    up_sum = lax.psum_scatter(up_part, "row", scatter_dimension=0, tiled=True)
    ffn = product_sum(e0, e1, down_all, rows, n, 3)
    db, ffn, up_sum = lax.optimization_barrier((db, ffn, up_sum))
    output = (jnp.stack(x1) + ffn.reshape(rows, local_len, width)).astype(bf16)

    out_allT = out_all.T
    dx1, dx1b, d_o = zip(*[middle_backward(r, o[r], x1[r], db, out_cotangent[r], out_allT) for r in range(rows)])
    do_heads = [lax.all_to_all(v, "ctx", split_axis=0, concat_axis=0, tiled=True).reshape(row_len, heads_dim) for v in d_o]
    c_order = jnp.concatenate(c).reshape(tokens, m, n, piece).transpose(0, 2, 1, 3).reshape(tokens, width)
    out_part = dot(c_order, jnp.concatenate(dx1b), "td,te->de", bf16)
    do_heads[0], out_part = lax.optimization_barrier((do_heads[0], out_part))
    out_part = lax.psum_scatter(out_part, "ctx", scatter_dimension=0, tiled=True)
    up_moved = lax.all_to_all(after(up_sum.reshape(n, piece, ff_dev), do_heads[-1]), "ctx", split_axis=0, concat_axis=2, tiled=True)
    grads = None
    for r in range(rows):
        grads = attention_backward(r, rows, saved[r], do_heads[r], table[r], lowest[r], span[r], blk, local_len, grads)
    grads, out_part, up_moved = lax.optimization_barrier((grads, out_part, up_moved))
    d0, d1 = grads
    out_sum = lax.psum_scatter(out_part, "row", scatter_dimension=0, tiled=True)
    qkv_part = (dot(xh0, d0, "td,tf->df") + dot(xh1, d1, "td,tf->df")).astype(bf16)
    d0, d1, qkv_part, out_sum = lax.optimization_barrier((d0, d1, qkv_part, out_sum))
    out_raw = out_sum.astype(f32)
    qkv_part = lax.psum_scatter(qkv_part, "row", scatter_dimension=0, tiled=True)
    da = product_sum(d0, d1, w_qkv.T, rows, n, 2)
    da, qkv_part = lax.optimization_barrier((da, qkv_part))
    up_raw = up_moved.reshape(piece, n, m, unit).transpose(0, 2, 1, 3).reshape(piece, ff).astype(f32)
    qkv_raw = lax.all_to_all(qkv_part.reshape(n, piece, 3 * heads_dim), "ctx", split_axis=0, concat_axis=2, tiled=True)
    qkv_raw = qkv_raw.reshape(piece, n, 3, heads_dim).astype(f32)
    query_raw, key_raw, value_raw = (qkv_raw[:, :, i].reshape(piece, width) for i in range(3))
    input_grad = jnp.stack(dx1) + standardize_back(x_hat, x_rstd, da).reshape(rows, local_len, width)

    def against(w, raw):
        return jnp.sum(w.astype(f32) * raw, axis=-1)

    def grown(raw, gain):
        return raw * gain.astype(f32)[:, None]

    gain_one = against(w_query, query_raw) + against(w_key, key_raw) + against(w_value, value_raw)
    return (output, input_grad, grown(query_raw, gain_attn), grown(key_raw, gain_attn), grown(value_raw, gain_attn),
            grown(out_raw, gain_attn_sub), grown(up_raw, gain_ffn), grown(down_raw, gain_ffn_sub),
            gain_one, against(w_out, out_raw), against(w_up, up_raw), against(w_down, down_raw))


def solution(mesh):
    split = P(BOTH, None)
    acts = P("row", "ctx", None)
    gain = P(BOTH)
    return jax.shard_map(
        body,
        mesh=mesh,
        in_specs=(acts, P("row", None)) + (split,) * 6 + (gain,) * 4 + (acts,),
        out_specs=(acts, acts) + (split,) * 6 + (gain,) * 4,
        check_vma=False,
    )
```

```python
import functools

import jax
import jax.numpy as jnp
from jax import lax
from jax.experimental import pallas as pl
from jax.experimental.pallas import tpu as pltpu
from jax.sharding import PartitionSpec as P

bf16 = jnp.bfloat16
f32 = jnp.float32
HEAD_DIM = 64
HALF = HEAD_DIM // 2
PAIR = 2 * HEAD_DIM
LOG2E = 1.4426950408889634
NEG = -1e30
ROW_LEN = 2048
XPOS_BASE = 512
EPS = 1e-5
BOTH = ("row", "ctx")


def walk(span_ref, qb, step):
    first = span_ref[2 + 2 * (qb)]
    clear = span_ref[3 + 2 * (qb)]

    def edge(t, carry):
        step(jnp.where(t < clear - first, first + t, qb), True)
        return carry

    def plain(kb, carry):
        step(kb, False)
        return carry

    lax.fori_loop(0, clear - first + 1, edge, 0)
    lax.fori_loop(clear, qb, plain, 0)


def allowed(lowest, kb, qb, blk):
    key = kb * blk + lax.broadcasted_iota(jnp.int32, (blk, blk), 0)
    query = qb * blk + lax.broadcasted_iota(jnp.int32, (blk, blk), 1)
    return (key <= query) & (key >= lowest)


def forward_kernel(nh, blk, unit, span_ref, q0_ref, q1_ref, k0_ref, k1_ref, v0_ref, v1_ref, table_ref, lo_ref,
                   o_ref, oT_ref, lse_ref, qT_ref, kT_ref, vT_ref, k_s, qm_s, acc_s, m_s, l_s):
    qb = pl.program_id(0)
    dim = nh * HEAD_DIM
    length = kT_ref.shape[1]
    core, place = span_ref[0], span_ref[1]
    spots = blk // (2 * unit)
    inner = lax.rem(place, spots)

    def turned(values, at, kind):
        cosine = table_ref[2 * kind, :, pl.ds(at, unit)]
        sine = table_ref[2 * kind + 1, :, pl.ds(at, unit)]
        out = []
        for h in range(nh):
            one = values[h * HEAD_DIM:h * HEAD_DIM + HALF]
            two = values[h * HEAD_DIM + HALF:(h + 1) * HEAD_DIM]
            out += [one * cosine - two * sine, two * cosine + one * sine]
        return jnp.concatenate(out, axis=0).astype(bf16)

    @pl.when(qb == 0)
    def _():
        def load(j, carry):
            src = pl.multiple_of((j ^ place) * unit, unit)
            for half, ref, v_ref in ((0, k0_ref, v0_ref), (1, k1_ref, v1_ref)):
                at = pl.multiple_of((2 * j + (core ^ half)) * unit, unit)
                key = turned(ref[:, pl.ds(src, unit)], at, 1)
                kT_ref[:, pl.ds(at, unit)] = key
                k_s[pl.ds(at, unit), :] = key.T
                vT_ref[:, pl.ds(at, unit)] = v_ref[:, pl.ds(src, unit)].astype(bf16)
            return carry

        lax.fori_loop(0, length // (2 * unit), load, 0)

    for u in range(spots):
        src = pl.multiple_of((u ^ inner) * unit, unit)
        for half, ref in ((0, q0_ref), (1, q1_ref)):
            at = pl.multiple_of((2 * u + (core ^ half)) * unit, unit)
            qT_ref[:, pl.ds(at, unit)] = turned(ref[:, pl.ds(src, unit)], pl.multiple_of(qb * blk + at, unit), 0)
    for h in range(nh):
        own = h % 2
        qm_s[h, pl.ds(own * HEAD_DIM, HEAD_DIM), :] = qT_ref[pl.ds(h * HEAD_DIM, HEAD_DIM), :]
        qm_s[h, pl.ds((1 - own) * HEAD_DIM, HEAD_DIM), :] = jnp.zeros((HEAD_DIM, blk), bf16)
    acc_s[...] = jnp.zeros_like(acc_s)
    m_s[...] = jnp.full_like(m_s, NEG)
    l_s[...] = jnp.zeros_like(l_s)
    lowest = lo_ref[...]

    def step(kb, masked):
        at = pl.multiple_of(kb * blk, blk)
        if masked:
            ok = allowed(lowest, kb, qb, blk)
        for h in range(nh):
            rows = pl.ds(h * HEAD_DIM, HEAD_DIM)
            s = jnp.dot(k_s[pl.ds(at, blk), pl.ds((h // 2) * PAIR, PAIR)], qm_s[h], preferred_element_type=f32)
            s = s * (LOG2E * HEAD_DIM**-0.5)
            if masked:
                s = jnp.where(ok, s, NEG)
            before = m_s[h:h + 1, :]
            now = jnp.maximum(before, jnp.max(s, axis=0, keepdims=True))
            p = jnp.exp2(s - now)
            fade = jnp.exp2(before - now)
            m_s[h:h + 1, :] = now
            l_s[h:h + 1, :] = l_s[h:h + 1, :] * fade + jnp.sum(p, axis=0, keepdims=True)
            acc_s[rows, :] = acc_s[rows, :] * fade + jnp.dot(
                vT_ref[rows, pl.ds(at, blk)], p.astype(bf16), preferred_element_type=f32)

    walk(span_ref, qb, step)
    for h in range(nh):
        rows = pl.ds(h * HEAD_DIM, HEAD_DIM)
        oT_ref[rows, :] = acc_s[rows, :] / l_s[h:h + 1, :]
        lse_ref[h:h + 1, :] = m_s[h:h + 1, :] + jnp.log2(l_s[h:h + 1, :])
    o_ref[...] = oT_ref[...].T.astype(bf16)


def backward_kernel(nh, blk, unit, span_ref, qT_ref, kT_ref, vT_ref, do_ref, oT_ref, lse_ref, table_ref, lo_ref,
                    old0_ref, old1_ref, d0_ref, d1_ref, k_s, v_s, qm_s, dm_s, qn_s, dn_s, acc_s, dk_s, dv_s, p_s, ds_s, dl_s):
    qb = pl.program_id(0)
    dim = nh * HEAD_DIM
    length = kT_ref.shape[1]
    count = length // blk
    scale = HEAD_DIM**-0.5
    core, place = span_ref[0], span_ref[1]

    @pl.when(qb == 0)
    def _():
        for c in range(count):
            k_s[pl.ds(c * blk, blk), :] = kT_ref[:, pl.ds(c * blk, blk)].T
            v_s[pl.ds(c * blk, blk), :] = vT_ref[:, pl.ds(c * blk, blk)].T
        dk_s[...] = jnp.zeros_like(dk_s)
        dv_s[...] = jnp.zeros_like(dv_s)

    doT = do_ref[...].T
    q = qT_ref[...].T
    lane = lax.broadcasted_iota(jnp.int32, (blk, PAIR), 1)
    prod = doT.astype(f32) * oT_ref[...]
    for h in range(nh):
        own = h % 2
        rows = slice(h * HEAD_DIM, (h + 1) * HEAD_DIM)
        zero = jnp.zeros((HEAD_DIM, blk), bf16)
        qm_s[h, pl.ds(own * HEAD_DIM, HEAD_DIM), :] = qT_ref[pl.ds(h * HEAD_DIM, HEAD_DIM), :]
        qm_s[h, pl.ds((1 - own) * HEAD_DIM, HEAD_DIM), :] = zero
        dm_s[h, pl.ds(own * HEAD_DIM, HEAD_DIM), :] = doT[rows, :]
        dm_s[h, pl.ds((1 - own) * HEAD_DIM, HEAD_DIM), :] = zero
        mine = (lane // HEAD_DIM) == own
        pair = slice((h // 2) * PAIR, (h // 2) * PAIR + PAIR)
        qn_s[h // 2, pl.ds(own * blk, blk), :] = jnp.where(mine, q[:, pair], jnp.zeros((), bf16))
        dn_s[h // 2, pl.ds(own * blk, blk), :] = jnp.where(mine, do_ref[:, pair], jnp.zeros((), bf16))
        dl_s[h:h + 1, :] = jnp.sum(prod[rows, :], axis=0, keepdims=True)
    acc_s[...] = jnp.zeros_like(acc_s)
    lowest = lo_ref[...]

    def step(kb, masked):
        at = pl.multiple_of(kb * blk, blk)
        if masked:
            ok = allowed(lowest, kb, qb, blk)
        for g in range(nh // 2):
            lanes = pl.ds(g * PAIR, PAIR)
            for own in range(2):
                h = 2 * g + own
                rows = pl.ds(h * HEAD_DIM, HEAD_DIM)
                s = jnp.dot(k_s[pl.ds(at, blk), lanes], qm_s[h], preferred_element_type=f32) * (LOG2E * scale)
                p = jnp.exp2(s - lse_ref[h:h + 1, :])
                if masked:
                    p = jnp.where(ok, p, 0.0)
                dp = jnp.dot(v_s[pl.ds(at, blk), lanes], dm_s[h], preferred_element_type=f32)
                ds = (p * (dp - dl_s[h:h + 1, :])).astype(bf16)
                p_s[g, :, pl.ds(own * blk, blk)] = p.astype(bf16)
                ds_s[g, :, pl.ds(own * blk, blk)] = ds
                acc_s[rows, :] += jnp.dot(kT_ref[rows, pl.ds(at, blk)], ds, preferred_element_type=f32)
            dv_s[pl.ds(at, blk), lanes] += jnp.dot(p_s[g], dn_s[g], preferred_element_type=f32)
            dk_s[pl.ds(at, blk), lanes] += jnp.dot(ds_s[g], qn_s[g], preferred_element_type=f32)

    walk(span_ref, qb, step)

    def turned_back(values, at, size, kind):
        cosine = table_ref[2 * kind, :, pl.ds(at, size)] * scale
        sine = table_ref[2 * kind + 1, :, pl.ds(at, size)] * scale
        out = []
        for h in range(nh):
            one = values[h * HEAD_DIM:h * HEAD_DIM + HALF]
            two = values[h * HEAD_DIM + HALF:(h + 1) * HEAD_DIM]
            out += [one * cosine + two * sine, two * cosine - one * sine]
        return jnp.concatenate(out, axis=0).T.astype(bf16)

    spots = blk // (2 * unit)
    for u in range(spots):
        dst = pl.multiple_of(((qb * spots + u) ^ place) * unit, unit)
        for half, ref in ((0, d0_ref), (1, d1_ref)):
            at = pl.multiple_of((2 * u + (core ^ half)) * unit, unit)
            ref[pl.ds(dst, unit), pl.ds(0, dim)] = turned_back(
                acc_s[:, pl.ds(at, unit)], pl.multiple_of(qb * blk + at, unit), unit, 0)

    @pl.when(qb == count - 1)
    def _():
        def store(j, carry):
            dst = pl.multiple_of((j ^ place) * unit, unit)
            for half, ref in ((0, d0_ref), (1, d1_ref)):
                at = pl.multiple_of((2 * j + (core ^ half)) * unit, unit)
                ref[pl.ds(dst, unit), pl.ds(dim, dim)] = turned_back(dk_s[pl.ds(at, unit), :].T, at, unit, 1)
                ref[pl.ds(dst, unit), pl.ds(2 * dim, dim)] = dv_s[pl.ds(at, unit), :].astype(bf16)
            return carry

        lax.fori_loop(0, length // (2 * unit), store, 0)


PARAMS = pltpu.CompilerParams(dimension_semantics=("arbitrary",), vmem_limit_bytes=60 * 2**20)


def span_of(lowest, blk, core, place):
    count = lowest.shape[0] // blk
    blocks = lowest.reshape(count, blk)
    own = jnp.arange(count, dtype=jnp.int32)
    first = jnp.minimum(blocks[:, 0] // blk, own)
    clear = jnp.minimum((blocks[:, -1] + blk - 1) // blk, own)
    both = jnp.stack([first, clear], axis=-1).reshape(-1)
    return jnp.concatenate([jnp.stack([core, place]), both]).astype(jnp.int32)


def attention_forward(row, half0, half1, table, lowest, span, blk, unit):
    length = lowest.shape[0]
    dim = half0.shape[0] // 3
    nh, count = dim // HEAD_DIM, length // blk
    spots = blk // (2 * unit)
    sds = jax.ShapeDtypeStruct
    pick = pl.BlockSpec((dim, blk // 2), lambda q, s: (0, row * count + (q ^ lax.div(s[1], spots))))
    keys = pl.BlockSpec((dim, length // 2), lambda q, s: (1, row))
    values = pl.BlockSpec((dim, length // 2), lambda q, s: (2, row))
    wide = pl.BlockSpec((dim, length), lambda q, s: (0, 0))
    cut = pl.BlockSpec((dim, blk), lambda q, s: (0, q))
    return pl.pallas_call(
        functools.partial(forward_kernel, nh, blk, unit),
        out_shape=(sds((length, dim), bf16), sds((dim, length), f32), sds((nh, length), f32),
                   sds((dim, length), bf16), sds((dim, length), bf16), sds((dim, length), bf16)),
        grid_spec=pltpu.PrefetchScalarGridSpec(
            num_scalar_prefetch=1, grid=(count,),
            in_specs=[pick, pick, keys, keys, values, values,
                      pl.BlockSpec((4, HALF, length), lambda q, s: (0, 0, 0)),
                      pl.BlockSpec((1, blk), lambda q, s: (0, q))],
            out_specs=[pl.BlockSpec((blk, dim), lambda q, s: (q, 0)), cut,
                       pl.BlockSpec((nh, blk), lambda q, s: (0, q)), cut, wide, wide],
            scratch_shapes=[pltpu.VMEM((length, dim), bf16), pltpu.VMEM((nh, PAIR, blk), bf16), pltpu.VMEM((dim, blk), f32),
                            pltpu.VMEM((8, blk), f32), pltpu.VMEM((8, blk), f32)]),
        compiler_params=PARAMS, name="attention_forward",
        cost_estimate=pl.CostEstimate(flops=4 * 4 * dim * length * length // 2, bytes_accessed=10 * 2**20,
                                      transcendentals=nh * length * length // 2),
    )(span, half0, half1, half0, half1, half0, half1, table, lowest[None, :])


def attention_backward(row, rows, saved, do, table, lowest, span, blk, unit, before):
    oT, lse, qT, kT, vT = saved
    length = lowest.shape[0]
    dim = qT.shape[0]
    nh, count = dim // HEAD_DIM, length // blk
    sds = jax.ShapeDtypeStruct
    cut = pl.BlockSpec((dim, blk), lambda q, s: (0, q))
    wide = pl.BlockSpec((dim, length), lambda q, s: (0, 0))
    grad = pl.BlockSpec((length // 2, 3 * dim), lambda q, s: (row, 0))
    whole = sds((rows * length // 2, 3 * dim), bf16)
    kernel = functools.partial(backward_kernel, nh, blk, unit)
    if before is None:
        def call(span_ref, *refs):
            kernel(span_ref, *refs[:8], None, None, *refs[8:])
    else:
        call = kernel
    return pl.pallas_call(
        call,
        out_shape=(whole, whole),
        grid_spec=pltpu.PrefetchScalarGridSpec(
            num_scalar_prefetch=1, grid=(count,),
            in_specs=[cut, wide, wide, pl.BlockSpec((blk, dim), lambda q, s: (q, 0)), cut,
                      pl.BlockSpec((nh, blk), lambda q, s: (0, q)),
                      pl.BlockSpec((4, HALF, length), lambda q, s: (0, 0, 0)),
                      pl.BlockSpec((1, blk), lambda q, s: (0, q))]
            + ([] if before is None else [pl.BlockSpec(memory_space=pl.ANY)] * 2),
            out_specs=[grad, grad],
            scratch_shapes=[pltpu.VMEM((length, dim), bf16), pltpu.VMEM((length, dim), bf16),
                            pltpu.VMEM((nh, PAIR, blk), bf16), pltpu.VMEM((nh, PAIR, blk), bf16),
                            pltpu.VMEM((nh // 2, 2 * blk, PAIR), bf16), pltpu.VMEM((nh // 2, 2 * blk, PAIR), bf16),
                            pltpu.VMEM((dim, blk), f32), pltpu.VMEM((length, dim), f32), pltpu.VMEM((length, dim), f32),
                            pltpu.VMEM((nh // 2, blk, 2 * blk), bf16), pltpu.VMEM((nh // 2, blk, 2 * blk), bf16),
                            pltpu.VMEM((8, blk), f32)]),
        compiler_params=PARAMS, name="attention_backward",
        input_output_aliases={} if before is None else {9: 0, 10: 1},
        cost_estimate=pl.CostEstimate(flops=10 * 4 * dim * length * length // 2, bytes_accessed=20 * 2**20,
                                      transcendentals=nh * length * length // 2),
    )(span, qT, kT, vT, do, oT, lse, table, lowest[None, :], *(before or ()))


def hat_of(values):
    center = values - jnp.mean(values, axis=-1, keepdims=True)
    rstd = lax.rsqrt(jnp.mean(center * center, axis=-1, keepdims=True) + EPS)
    return center * rstd, rstd


def hat_back(hat, rstd, grad):
    return rstd * (grad - jnp.mean(grad, axis=-1, keepdims=True) - hat * jnp.mean(grad * hat, axis=-1, keepdims=True))


def wide_row(o_ref):
    return jnp.concatenate([o_ref[i] for i in range(o_ref.shape[0])], axis=1).astype(f32)


def middle_forward_kernel(o_ref, x_ref, w_ref, c_ref, x1_ref, b_ref):
    c = hat_of(wide_row(o_ref))[0].astype(bf16)
    c_ref[...] = c
    x1 = x_ref[...].astype(f32) + jnp.dot(c, w_ref[...], preferred_element_type=f32)
    x1_ref[...] = x1
    b_ref[...] = hat_of(x1)[0].astype(bf16)


def middle_forward(o, x, w):
    n, size, dim = o.shape
    width = n * dim
    step = min(128, size)
    sds = jax.ShapeDtypeStruct
    flat = pl.BlockSpec((step, width), lambda t: (t, 0))
    return pl.pallas_call(
        middle_forward_kernel,
        out_shape=(sds((size, width), bf16), sds((size, width), f32), sds((size, width), bf16)),
        grid=(size // step,),
        in_specs=[pl.BlockSpec((n, step, dim), lambda t: (0, t, 0)), flat,
                  pl.BlockSpec((width, width), lambda t: (0, 0))],
        out_specs=(flat, flat, flat),
        compiler_params=PARAMS, name="middle_forward",
        cost_estimate=pl.CostEstimate(flops=2 * size * width * width, bytes_accessed=14 * 2**20, transcendentals=0),
    )(o, x, w)


def middle_backward_kernel(o_ref, x1_ref, db_ref, dy_ref, w_ref, dx_ref, low_ref, do_ref):
    hat, rstd = hat_of(x1_ref[...])
    dx1 = dy_ref[...].astype(f32) + hat_back(hat, rstd, db_ref[...])
    dx_ref[...] = dx1
    low_ref[...] = dx1.astype(bf16)
    dc = times_rows(dx1.astype(bf16), w_ref[...])
    hat, rstd = hat_of(wide_row(o_ref))
    d_o = hat_back(hat, rstd, dc).astype(bf16)
    dim = do_ref.shape[2]
    for i in range(do_ref.shape[0]):
        do_ref[i] = d_o[:, i * dim:(i + 1) * dim]


def middle_backward(row, o, x1, db, dy, w):
    n, size, dim = o.shape
    width = n * dim
    step = min(128, size)
    sds = jax.ShapeDtypeStruct
    flat = pl.BlockSpec((step, width), lambda t: (t, 0))
    part = pl.BlockSpec((n, step, dim), lambda t: (0, t, 0))
    return pl.pallas_call(
        middle_backward_kernel,
        out_shape=(sds((size, width), f32), sds((size, width), bf16), sds((n, size, dim), bf16)),
        grid=(size // step,),
        in_specs=[part, flat, pl.BlockSpec((step, width), lambda t: (row * (size // step) + t, 0)), flat,
                  pl.BlockSpec((width, width), lambda t: (0, 0))],
        out_specs=(flat, flat, part),
        compiler_params=PARAMS, name="middle_backward",
        cost_estimate=pl.CostEstimate(flops=2 * size * width * width, bytes_accessed=16 * 2**20, transcendentals=0),
    )(o, x1, db, dy, w)


def ways(row, n):
    bits = [1 << k for k in range(1, n.bit_length() - 1)]
    return bits if row % 2 == 0 else bits[::-1]


def times_rows(a, w):
    return lax.dot_general(a, w, (((1,), (1,)), ((), ())), preferred_element_type=f32)


def product_sum_kernel(n, rows, cols, turned, x0_ref, x1_ref, w_ref, o_ref, part_s, core_s, sum_s, got_s, send_sem, recv_sem):
    mine = lax.axis_index("ctx")
    spots = n // 2
    size = x0_ref.shape[0] // (rows * spots)
    width = o_ref.shape[1]
    barrier = pltpu.get_barrier_semaphore()
    bits = [1] + ways(0, n)
    for bit in bits:
        pl.semaphore_signal(barrier, inc=1, device_id={"ctx": mine ^ bit}, device_id_type=pl.DeviceIdType.MESH)
    pl.semaphore_wait(barrier, len(bits))
    copies = []

    def send(src, dst, bit):
        at = len(copies)
        copy = pltpu.make_async_remote_copy(
            src_ref=src, dst_ref=dst, send_sem=send_sem.at[at], recv_sem=recv_sem.at[at],
            device_id={"ctx": mine ^ bit}, device_id_type=pl.DeviceIdType.MESH)
        copy.start()
        copies.append(copy)
        return copy

    def key(row, k):
        return [-(k & (bit >> 1)) for bit in ways(row, n)]

    orders = []
    for r in range(rows):
        way = [bit >> 1 for bit in ways(r, n)]
        orders.append(sorted(range(spots), key=lambda k: [0 if k & bit else 1 for bit in way]))
    todo = [(r, orders[r][t]) for t in range(spots) for r in range(rows)]
    inbox, slot, slots = {}, {}, 0

    def product(x_ref, r, k, finish):
        begin = (r * spots + k) * size

        @pl.loop(0, width // cols)
        def _(c):
            at = pl.ds(pl.multiple_of(c * cols, cols), cols)
            x = x_ref[pl.ds(begin, size), :]
            finish(at, times_rows(x, w_ref[at, :]) if turned else jnp.dot(x, w_ref[:, at], preferred_element_type=f32))

    def pair(r, k):
        spot = r * spots + k

        def keep(at, value):
            part_s[spot, :, at] = value.astype(bf16)

        product(x1_ref, r, k, keep)
        inbox[r, k] = send(part_s.at[spot], core_s.at[spot], 1)

    def own(r, k):
        spot = r * spots + k
        inbox[r, k].wait_recv()

        def add(at, value):
            sum_s[spot, :, at] = (value + core_s[spot, :, at].astype(f32)).astype(bf16)

        product(x0_ref, r, k, add)

    def pass_on(r, k, stage):
        nonlocal slots
        bit = ways(r, n)[stage]
        if k & (bit >> 1):
            inbox[r, k ^ (bit >> 1), stage] = (send(sum_s.at[r * spots + k], got_s.at[slots], bit), slots)
            slots += 1

    group = max(rows * spots // 2, 1)
    for begin in range(0, len(todo), group):
        for r, k in todo[begin:begin + group]:
            pair(r, k)
        for r, k in todo[begin:begin + group]:
            own(r, k)
            pass_on(r, k, 0)
    stages = len(bits) - 1
    for stage in range(stages):
        for r, k in todo:
            way = [bit >> 1 for bit in ways(r, n)]
            if any(k & bit for bit in way[:stage + 1]):
                continue
            copy, at = inbox[r, k, stage]
            copy.wait_recv()
            spot = r * spots + k
            if stage == stages - 1:
                o_ref[pl.ds(r * size, size), :] = sum_s[spot].astype(f32) + got_s[at].astype(f32)
            else:
                sum_s[spot] = (sum_s[spot].astype(f32) + got_s[at].astype(f32)).astype(bf16)
                pass_on(r, k, stage + 1)
    for copy in copies:
        copy.wait_send()


def product_sum(x0, x1, w, rows, n, collective_id, turned=False):
    size = x0.shape[0] // (rows * (n // 2))
    width = w.shape[0 if turned else 1]
    count = rows * (n // 2)
    moves = count + rows * (n // 2 - 1)
    vmem = pl.BlockSpec(memory_space=pltpu.VMEM)
    flops = 4 * x0.shape[0] * x0.shape[1] * width
    return pl.pallas_call(
        functools.partial(product_sum_kernel, n, rows, min(512, width), turned),
        out_shape=jax.ShapeDtypeStruct((rows * size, width), f32),
        in_specs=[vmem] * 3, out_specs=vmem,
        scratch_shapes=[pltpu.VMEM((count, size, width), bf16), pltpu.VMEM((count, size, width), bf16),
                        pltpu.VMEM((count, size, width), bf16), pltpu.VMEM((moves - count, size, width), bf16),
                        pltpu.SemaphoreType.DMA((moves,)), pltpu.SemaphoreType.DMA((moves,))],
        compiler_params=pltpu.CompilerParams(collective_id=collective_id, has_side_effects=True, vmem_limit_bytes=60 * 2**20),
        name="product_sum",
        cost_estimate=pl.CostEstimate(flops=4 * flops, bytes_accessed=20 * 2**20, transcendentals=0),
    )(x0, x1, w)


def gather_product_kernel(n, rows, cols, b_ref, dy0_ref, dy1_ref, up_ref, down_ref, b0_ref, b1_ref, h0_ref, h1_ref, d0_ref, d1_ref,
                          stat_ref, got_s, d_s, h_s, dy_s, send_sem, recv_sem, dy_sem, b_sem, h_sem, d_sem):
    mine = lax.axis_index("ctx")
    spots = n // 2
    size = b_ref.shape[0] // rows
    ff = up_ref.shape[1]
    count = rows * spots
    barrier = pltpu.get_barrier_semaphore()
    bits = [1] + ways(0, n)
    for bit in bits:
        pl.semaphore_signal(barrier, inc=1, device_id={"ctx": mine ^ bit}, device_id_type=pl.DeviceIdType.MESH)
    pl.semaphore_wait(barrier, len(bits))
    sends, locals_, arrival = [], [], {}

    def send(src, half, row, k, bit):
        at, to = len(sends), half * count + row * spots + k
        copy = pltpu.make_async_remote_copy(
            src_ref=src, dst_ref=got_s.at[to], send_sem=send_sem.at[at], recv_sem=recv_sem.at[at],
            device_id={"ctx": mine ^ bit}, device_id_type=pl.DeviceIdType.MESH)
        copy.start()
        sends.append(copy)
        arrival[half, row, k] = copy

    def held(half, row, k):
        if half == 0 and k == 0:
            return b_ref.at[pl.ds(row * size, size), :]
        return got_s.at[half * count + row * spots + k]

    def onward(row, k):
        way = ways(row, n)
        top = max([s for s, bit in enumerate(way) if k & (bit >> 1)], default=-1)
        for bit in way[top + 1:]:
            send(held(0, row, k), 0, row, k | (bit >> 1), bit)
        send(held(0, row, k), 1, row, k, 1)

    for r in range(rows):
        onward(r, 0)

    def fetch(t, slot):
        begin = pl.multiple_of(lax.rem(t, count) * size, size)

        @pl.when(t < count)
        def _():
            pltpu.make_async_copy(dy0_ref.at[pl.ds(begin, size), :], dy_s.at[slot], dy_sem.at[slot]).start()

        @pl.when(t >= count)
        def _():
            pltpu.make_async_copy(dy1_ref.at[pl.ds(begin, size), :], dy_s.at[slot], dy_sem.at[slot]).start()

    fetch(0, 0)

    @pl.loop(0, 2 * count)
    def _(t):
        slot = lax.rem(t, 2)

        @pl.when(t + 1 < 2 * count)
        def _():
            fetch(t + 1, 1 - slot)

        pltpu.make_async_copy(dy0_ref.at[pl.ds(0, size), :], dy_s.at[slot], dy_sem.at[slot]).wait()

        @pl.loop(0, ff // cols)
        def _(c):
            at = pl.ds(pl.multiple_of(c * cols, cols), cols)
            d_s[t, :, at] = times_rows(dy_s[slot], down_ref[at, :])

    for t in range(2 * count):
        dst = (d0_ref, d1_ref)[t // count].at[pl.ds((t % count) * size, size), :]
        copy = pltpu.make_async_copy(d_s.at[t], dst, d_sem.at[t])
        copy.start()
        locals_.append(copy)

    outs = []
    lane = lax.broadcasted_iota(jnp.int32, (32, 128), 1)

    def block(half, row, k):
        t = half * count + row * spots + k
        src = held(half, row, k)
        copy = pltpu.make_async_copy(src, (b0_ref, b1_ref)[half].at[pl.ds((t % count) * size, size), :], b_sem.at[t])
        copy.start()
        locals_.append(copy)
        slot = len(outs) % 2
        if len(outs) >= 2:
            outs[-2].wait()

        @pl.loop(0, ff // cols)
        def _(c):
            at = pl.ds(pl.multiple_of(c * cols, cols), cols)
            h_s[slot, :, at] = jnp.dot(src[...], up_ref[:, at], preferred_element_type=f32)

        copy = pltpu.make_async_copy(h_s.at[slot], (h0_ref, h1_ref)[half].at[pl.ds((t % count) * size, size), :], h_sem.at[t])
        copy.start()
        outs.append(copy)

        @pl.loop(0, size // 32)
        def _(c):
            at = pl.ds(pl.multiple_of(c * 32, 32), 32)
            h = h_s[slot, at, :]
            gel = h * (0.5 * (1.0 + lax.erf(h * (2.0**-0.5))))
            d = d_s[t, at, :]
            mean = jnp.mean(gel, axis=-1, keepdims=True)
            off = gel - mean
            spread = jnp.sum(off * off, axis=-1, keepdims=True)
            total = jnp.sum(d, axis=-1, keepdims=True)
            cross = jnp.sum(d * off, axis=-1, keepdims=True)
            line = jnp.where(lane == 0, mean, jnp.where(lane == 1, spread, jnp.where(lane == 2, total, cross)))
            stat_ref[pl.ds(pl.multiple_of(t * size + c * 32, 32), 32), :] = line

    order = []
    for k in range(spots):
        for r in range(rows):
            way = ways(r, n)
            order.append((r, sum((bit >> 1) for s, bit in enumerate(way) if k >> s & 1)))
    for begin in range(0, len(order), rows):
        some = order[begin:begin + rows]
        for r, k in some:
            if k:
                arrival[0, r, k].wait_recv()
                onward(r, k)
        for r, k in some:
            block(0, r, k)
        for r, k in some:
            arrival[1, r, k].wait_recv()
            block(1, r, k)
    for copy in outs[-2:] + locals_:
        copy.wait()
    for copy in sends:
        copy.wait_send()


def gather_product(b, dy0, dy1, up, down, rows, n, collective_id):
    size = b.shape[0] // rows
    width, ff = up.shape
    count = rows * (n // 2)
    half = count * size
    moves = rows * (n - 1)
    vmem, here = pl.BlockSpec(memory_space=pltpu.VMEM), pl.BlockSpec(memory_space=pl.ANY)
    sds = jax.ShapeDtypeStruct
    return pl.pallas_call(
        functools.partial(gather_product_kernel, n, rows, min(256, ff)),
        out_shape=(sds((half, width), bf16),) * 2 + (sds((half, ff), f32),) * 4 + (sds((2 * half, 128), f32),),
        in_specs=[vmem, here, here, vmem, vmem], out_specs=(here,) * 6 + (vmem,),
        scratch_shapes=[pltpu.VMEM((2 * count, size, width), bf16), pltpu.VMEM((2 * count, size, ff), f32),
                        pltpu.VMEM((2, size, ff), f32), pltpu.VMEM((2, size, width), bf16),
                        pltpu.SemaphoreType.DMA((moves,)), pltpu.SemaphoreType.DMA((moves,)), pltpu.SemaphoreType.DMA((2,))]
        + [pltpu.SemaphoreType.DMA((2 * count,))] * 3,
        compiler_params=pltpu.CompilerParams(collective_id=collective_id, has_side_effects=True, vmem_limit_bytes=62 * 2**20),
        name="gather_product",
        cost_estimate=pl.CostEstimate(flops=16 * half * width * ff, bytes_accessed=70 * 2**20, transcendentals=0),
    )(b, dy0, dy1, up, down)


def standardize(values):
    center = values - jnp.mean(values, axis=-1, keepdims=True)
    spread = jnp.mean(center * center, axis=-1, keepdims=True)
    rstd = lax.rsqrt(spread + EPS)
    return center * rstd, rstd


def standardize_back(hat, rstd, grad):
    return rstd * (grad - jnp.mean(grad, axis=-1, keepdims=True) - hat * jnp.mean(grad * hat, axis=-1, keepdims=True))


def row_places(lengths, row_len):
    places = jnp.arange(row_len, dtype=jnp.int32)
    ends = jnp.cumsum(lengths, axis=-1)
    passed = ends[:, None, :] <= places[None, :, None]
    starts = jnp.sum(jnp.where(passed, lengths[:, None, :], 0), axis=-1)
    valid = places[None, :] < ends[:, -1:]
    lowest = jnp.where(valid, starts, places[None, :]).astype(jnp.int32)
    return (places[None, :] - starts).astype(f32), lowest


def xpos_tables(relative):
    ladder = jnp.arange(HALF, dtype=f32) / HALF
    rate = jnp.power(10000.0, -ladder)
    base = (ladder + 0.4) / 1.4
    angles = rate[None, :, None] * relative[:, None, :]
    power = (relative[:, None, :] - ROW_LEN / 2) / XPOS_BASE
    factor = jnp.power(base[None, :, None], power)
    cosine, sine = jnp.cos(angles), jnp.sin(angles)
    return jnp.stack([cosine * factor, sine * factor, cosine / factor, sine / factor], axis=1)


def dot(a, b, spec, kind=f32):
    return jnp.einsum(spec, a, b, preferred_element_type=f32).astype(kind)


def swap(x, bit):
    n = lax.axis_size("ctx")
    return lax.ppermute(x, "ctx", [(i, i ^ bit) for i in range(n)])


def exchange(blocks):
    n = lax.axis_size("ctx")
    mine = lax.axis_index("ctx")
    out = jnp.zeros_like(blocks)
    for bit in range(n):
        block = lax.dynamic_index_in_dim(blocks, mine ^ bit, 0, False)
        block = swap(block, bit) if bit else block
        out = lax.dynamic_update_index_in_dim(out, block, mine ^ bit, 0)
    return out


def after(x, *others):
    return lax.optimization_barrier((x, *others))[0]


def gather_start(x):
    return [{0: x[r]} for r in range(x.shape[0])]


def gather_step(held, step):
    n = lax.axis_size("ctx")
    out = []
    for r, parts in enumerate(held):
        bit = ways(r, n)[step]
        out.append({**parts, **{k | bit: swap(v, bit) for k, v in parts.items()}})
    return out


def gather_steps():
    return lax.axis_size("ctx").bit_length() - 2


def gather_end(held):
    return jnp.concatenate([parts[k] for parts in held for k in sorted(parts)], axis=0)


def gather_half(x):
    held = gather_start(x)
    for step in range(gather_steps()):
        held = gather_step(held, step)
    return gather_end(held)


def plus(a, b, kind=bf16):
    return (a.astype(f32) + b.astype(f32)).astype(kind)


def reduce_start(half0, half1, rows):
    n = lax.axis_size("ctx")
    width = half0.shape[-1]
    both = plus(half0, swap(half1, 1)).reshape(rows, n // 2, -1, width)
    return [{2 * k: both[r, k] for k in range(n // 2)} for r in range(rows)]


def reduce_step(held, step):
    n = lax.axis_size("ctx")
    out = []
    for r, parts in enumerate(held):
        bit = ways(r, n)[step]
        kind = bf16 if len(parts) > 2 else f32
        out.append({k: plus(v, swap(parts[k | bit], bit), kind) for k, v in parts.items() if not k & bit})
    return out


def reduce_end(held):
    return jnp.concatenate([parts[0] for parts in held], axis=0)


def reduce_halves(half0, half1, rows):
    held = reduce_start(half0, half1, rows)
    for step in range(gather_steps()):
        held = reduce_step(held, step)
    return reduce_end(held)


def body(inputs, doc_len, w_query, w_key, w_value, w_out, w_up, w_down, gain_attn, gain_attn_sub, gain_ffn,
         gain_ffn_sub, out_cotangent):
    rows, local_len, width = inputs.shape
    n, m = lax.axis_size("ctx"), lax.axis_size("row")
    row_len = local_len * n
    tokens, half = rows * local_len, rows * row_len // 2
    piece = w_query.shape[0]
    heads_dim = width // n
    ff = w_up.shape[1]
    unit = ff // (n * m)
    ff_dev = unit * m
    blk = min(512, row_len)
    mine = lax.axis_index("ctx")
    core, place = mine & 1, mine >> 1

    def scaled(w, gain):
        return (w.astype(f32) * gain.astype(f32)[:, None]).astype(bf16)

    x_own = inputs.reshape(tokens, width).astype(f32)
    x_hat, x_rstd = standardize(x_own)
    x_low = x_hat.astype(bf16)
    xh0 = gather_half(x_low.reshape(rows, local_len, width))
    xh1 = swap(xh0, 1)

    qkv_local = jnp.concatenate(
        [scaled(w, gain_attn).reshape(piece, n, heads_dim) for w in (w_query, w_key, w_value)], axis=2)
    qkv_part = exchange(qkv_local.transpose(1, 0, 2)).reshape(n * piece, 3 * heads_dim)
    w_qkv = lax.all_gather(qkv_part, "row", axis=0, tiled=True)
    out_all = lax.all_gather(scaled(w_out, gain_attn_sub), BOTH, axis=0, tiled=True)

    relative, lowest = row_places(doc_len, row_len)
    table = xpos_tables(relative)
    span = [span_of(lowest[r], blk, core, place) for r in range(rows)]
    qkv0 = dot(w_qkv, xh0, "df,td->ft")
    qkv1 = dot(w_qkv, xh1, "df,td->ft")
    qkv0, qkv1, w_up_in, cot = lax.optimization_barrier((qkv0, qkv1, w_up, out_cotangent))
    up_local = scaled(w_up_in, gain_ffn).reshape(piece, m, n, unit).transpose(2, 0, 1, 3).reshape(n, piece, ff_dev)
    up_part = lax.all_to_all(up_local, "ctx", split_axis=0, concat_axis=0, tiled=True).reshape(n * piece, ff_dev)
    dy_held = gather_step(gather_start(cot), 0)
    dy_steps = gather_steps()
    saved, o = [], []
    for r in range(rows):
        o_row, *kept = attention_forward(r, qkv0, qkv1, table[r], lowest[r], span[r], blk, local_len)
        if r == 0:
            o_row, kept, qkv0, qkv1, dy_held, out_all = lax.optimization_barrier((o_row, kept, qkv0, qkv1, dy_held, out_all))
            down_all = lax.all_gather(after(scaled(w_down, gain_ffn_sub), out_all), "row", axis=0, tiled=True)
            for step in range(1, dy_steps):
                dy_held = gather_step(dy_held, step)
        if r == rows - 1:
            o_row, o = lax.optimization_barrier((o_row, o))
        saved.append(kept)
        o.append(lax.all_to_all(o_row.reshape(n, local_len, heads_dim), "ctx", split_axis=0, concat_axis=0, tiled=True))
    o, down_all, up_part = lax.optimization_barrier((o, down_all, up_part))
    up_all = lax.all_gather(up_part, "row", axis=0, tiled=True)
    c, x1, b_low = zip(*[middle_forward(o[r], inputs[r], out_all) for r in range(rows)])
    b_low, dy_held = lax.optimization_barrier((b_low, dy_held))
    dy0 = gather_end(dy_held)
    dy1 = swap(dy0, 1)

    b0, b1, h0, h1, d_hat0, d_hat1, stats = gather_product(jnp.concatenate(b_low), dy0, dy1, up_all, down_all, rows, n, 4)
    stats = stats[:, :4].T
    order = jnp.arange(n // 2, dtype=jnp.int32) ^ place
    halves = jnp.arange(2, dtype=jnp.int32) ^ core

    def reorder(v):
        v = v.reshape(v.shape[0], 2, rows, n // 2, local_len)
        return jnp.take(jnp.take(v, halves, axis=1), order, axis=3).reshape(v.shape[0], 2 * half)

    stats = lax.all_gather(reorder(stats), "ctx", axis=0, tiled=False)
    mean = jnp.mean(stats[:, 0], axis=0)
    shift = stats[:, 0] - mean
    var = (jnp.sum(stats[:, 1], axis=0) + ff_dev * jnp.sum(shift * shift, axis=0)) / ff
    rstd = lax.rsqrt(var + EPS)
    d_mean = jnp.sum(stats[:, 2], axis=0) / ff
    d_corr = rstd * jnp.sum(stats[:, 3] + stats[:, 2] * shift, axis=0) / ff
    merged = reorder(jnp.stack([mean, rstd, d_mean, d_corr])).reshape(4, 2, half, 1)

    def finish(h, d_hat, which):
        cdf = 0.5 * (1.0 + lax.erf(h * (2.0**-0.5)))
        mean, rstd, d_mean, d_corr = (merged[k, which] for k in range(4))
        hat = (h * cdf - mean) * rstd
        d_gel = rstd * (d_hat - d_mean - hat * d_corr)
        pdf = jnp.exp(-0.5 * h * h) * 0.3989422804014327
        return hat.astype(bf16), (d_gel * (cdf + h * pdf)).astype(bf16)

    e0, dh0 = finish(h0, d_hat0, 0)
    e1, dh1 = finish(h1, d_hat1, 1)
    down_part = (dot(e0, dy0, "tf,td->fd") + dot(e1, dy1, "tf,td->fd")).astype(bf16)
    up_part = (dot(b0, dh0, "td,tf->df") + dot(b1, dh1, "td,tf->df")).astype(bf16)
    e0, e1, dh0, dh1, down_part, up_part = lax.optimization_barrier((e0, e1, dh0, dh1, down_part, up_part))
    down_sum = lax.psum_scatter(down_part, "row", scatter_dimension=0, tiled=True)
    db = product_sum(dh0, dh1, up_all, rows, n, 1, True)
    e0, e1, db, up_part, down_sum = lax.optimization_barrier((e0, e1, db, up_part, down_sum))
    down_raw = down_sum.astype(f32)
    up_sum = lax.psum_scatter(up_part, "row", scatter_dimension=0, tiled=True)
    ffn = product_sum(e0, e1, down_all, rows, n, 3)
    db, ffn, up_sum = lax.optimization_barrier((db, ffn, up_sum))
    output = (jnp.stack(x1) + ffn.reshape(rows, local_len, width)).astype(bf16)

    dx1, dx1b, d_o = zip(*[middle_backward(r, o[r], x1[r], db, out_cotangent[r], out_all) for r in range(rows)])
    do_heads = [lax.all_to_all(v, "ctx", split_axis=0, concat_axis=0, tiled=True).reshape(row_len, heads_dim) for v in d_o]
    c_order = jnp.concatenate(c).reshape(tokens, m, n, piece).transpose(0, 2, 1, 3).reshape(tokens, width)
    out_part = dot(c_order, jnp.concatenate(dx1b), "td,te->de", bf16)
    do_heads[0], out_part = lax.optimization_barrier((do_heads[0], out_part))
    out_part = lax.psum_scatter(out_part, "ctx", scatter_dimension=0, tiled=True)
    up_moved = lax.all_to_all(after(up_sum.reshape(n, piece, ff_dev), do_heads[-1]), "ctx", split_axis=0, concat_axis=2, tiled=True)
    grads = None
    for r in range(rows):
        grads = attention_backward(r, rows, saved[r], do_heads[r], table[r], lowest[r], span[r], blk, local_len, grads)
    grads, out_part, up_moved = lax.optimization_barrier((grads, out_part, up_moved))
    d0, d1 = grads
    out_sum = lax.psum_scatter(out_part, "row", scatter_dimension=0, tiled=True)
    qkv_part = (dot(xh0, d0, "td,tf->df") + dot(xh1, d1, "td,tf->df")).astype(bf16)
    d0, d1, qkv_part, out_sum = lax.optimization_barrier((d0, d1, qkv_part, out_sum))
    out_raw = out_sum.astype(f32)
    qkv_part = lax.psum_scatter(qkv_part, "row", scatter_dimension=0, tiled=True)
    da = product_sum(d0, d1, w_qkv, rows, n, 2, True)
    da, qkv_part = lax.optimization_barrier((da, qkv_part))
    up_raw = up_moved.reshape(piece, n, m, unit).transpose(0, 2, 1, 3).reshape(piece, ff).astype(f32)
    qkv_raw = lax.all_to_all(qkv_part.reshape(n, piece, 3 * heads_dim), "ctx", split_axis=0, concat_axis=2, tiled=True)
    qkv_raw = qkv_raw.reshape(piece, n, 3, heads_dim).astype(f32)
    query_raw, key_raw, value_raw = (qkv_raw[:, :, i].reshape(piece, width) for i in range(3))
    input_grad = jnp.stack(dx1) + standardize_back(x_hat, x_rstd, da).reshape(rows, local_len, width)

    def against(w, raw):
        return jnp.sum(w.astype(f32) * raw, axis=-1)

    def grown(raw, gain):
        return raw * gain.astype(f32)[:, None]

    gain_one = against(w_query, query_raw) + against(w_key, key_raw) + against(w_value, value_raw)
    return (output, input_grad, grown(query_raw, gain_attn), grown(key_raw, gain_attn), grown(value_raw, gain_attn),
            grown(out_raw, gain_attn_sub), grown(up_raw, gain_ffn), grown(down_raw, gain_ffn_sub),
            gain_one, against(w_out, out_raw), against(w_up, up_raw), against(w_down, down_raw))


def solution(mesh):
    split = P(BOTH, None)
    acts = P("row", "ctx", None)
    gain = P(BOTH)
    return jax.shard_map(
        body,
        mesh=mesh,
        in_specs=(acts, P("row", None)) + (split,) * 6 + (gain,) * 4 + (acts,),
        out_specs=(acts, acts) + (split,) * 6 + (gain,) * 4,
        check_vma=False,
    )
```

```python
import functools

import jax
import jax.numpy as jnp
from jax import lax
from jax.experimental import pallas as pl
from jax.experimental.pallas import tpu as pltpu
from jax.sharding import PartitionSpec as P

bf16 = jnp.bfloat16
f32 = jnp.float32
HEAD_DIM = 64
HALF = HEAD_DIM // 2
PAIR = 2 * HEAD_DIM
LOG2E = 1.4426950408889634
NEG = -1e30
ROW_LEN = 2048
XPOS_BASE = 512
EPS = 1e-5
BOTH = ("row", "ctx")


def walk(span_ref, qb, step):
    first = span_ref[2 + 2 * (qb)]
    clear = span_ref[3 + 2 * (qb)]

    def edge(t, carry):
        step(jnp.where(t < clear - first, first + t, qb), True)
        return carry

    def plain(kb, carry):
        step(kb, False)
        return carry

    lax.fori_loop(0, clear - first + 1, edge, 0)
    lax.fori_loop(clear, qb, plain, 0)


def allowed(lowest, kb, qb, blk):
    key = kb * blk + lax.broadcasted_iota(jnp.int32, (blk, blk), 0)
    query = qb * blk + lax.broadcasted_iota(jnp.int32, (blk, blk), 1)
    return (key <= query) & (key >= lowest)


def forward_kernel(nh, blk, unit, span_ref, q0_ref, q1_ref, k0_ref, k1_ref, v0_ref, v1_ref, table_ref, lo_ref,
                   o_ref, oT_ref, lse_ref, qT_ref, kT_ref, vT_ref, k_s, qm_s, acc_s, m_s, l_s):
    qb = pl.program_id(0)
    dim = nh * HEAD_DIM
    length = kT_ref.shape[1]
    core, place = span_ref[0], span_ref[1]
    spots = blk // (2 * unit)
    inner = lax.rem(place, spots)

    def turned(values, at, kind):
        cosine = table_ref[2 * kind, :, pl.ds(at, unit)]
        sine = table_ref[2 * kind + 1, :, pl.ds(at, unit)]
        out = []
        for h in range(nh):
            one = values[h * HEAD_DIM:h * HEAD_DIM + HALF]
            two = values[h * HEAD_DIM + HALF:(h + 1) * HEAD_DIM]
            out += [one * cosine - two * sine, two * cosine + one * sine]
        return jnp.concatenate(out, axis=0).astype(bf16)

    @pl.when(qb == 0)
    def _():
        def load(j, carry):
            src = pl.multiple_of((j ^ place) * unit, unit)
            for half, ref, v_ref in ((0, k0_ref, v0_ref), (1, k1_ref, v1_ref)):
                at = pl.multiple_of((2 * j + (core ^ half)) * unit, unit)
                key = turned(ref[:, pl.ds(src, unit)], at, 1)
                kT_ref[:, pl.ds(at, unit)] = key
                k_s[pl.ds(at, unit), :] = key.T
                vT_ref[:, pl.ds(at, unit)] = v_ref[:, pl.ds(src, unit)].astype(bf16)
            return carry

        lax.fori_loop(0, length // (2 * unit), load, 0)

    for u in range(spots):
        src = pl.multiple_of((u ^ inner) * unit, unit)
        for half, ref in ((0, q0_ref), (1, q1_ref)):
            at = pl.multiple_of((2 * u + (core ^ half)) * unit, unit)
            qT_ref[:, pl.ds(at, unit)] = turned(ref[:, pl.ds(src, unit)], pl.multiple_of(qb * blk + at, unit), 0)
    for h in range(nh):
        own = h % 2
        qm_s[h, pl.ds(own * HEAD_DIM, HEAD_DIM), :] = qT_ref[pl.ds(h * HEAD_DIM, HEAD_DIM), :]
        qm_s[h, pl.ds((1 - own) * HEAD_DIM, HEAD_DIM), :] = jnp.zeros((HEAD_DIM, blk), bf16)
    acc_s[...] = jnp.zeros_like(acc_s)
    m_s[...] = jnp.full_like(m_s, NEG)
    l_s[...] = jnp.zeros_like(l_s)
    lowest = lo_ref[...]

    def step(kb, masked):
        at = pl.multiple_of(kb * blk, blk)
        if masked:
            ok = allowed(lowest, kb, qb, blk)
        for h in range(nh):
            rows = pl.ds(h * HEAD_DIM, HEAD_DIM)
            s = jnp.dot(k_s[pl.ds(at, blk), pl.ds((h // 2) * PAIR, PAIR)], qm_s[h], preferred_element_type=f32)
            s = s * (LOG2E * HEAD_DIM**-0.5)
            if masked:
                s = jnp.where(ok, s, NEG)
            before = m_s[h:h + 1, :]
            now = jnp.maximum(before, jnp.max(s, axis=0, keepdims=True))
            p = jnp.exp2(s - now)
            fade = jnp.exp2(before - now)
            m_s[h:h + 1, :] = now
            l_s[h:h + 1, :] = l_s[h:h + 1, :] * fade + jnp.sum(p, axis=0, keepdims=True)
            acc_s[rows, :] = acc_s[rows, :] * fade + jnp.dot(
                vT_ref[rows, pl.ds(at, blk)], p.astype(bf16), preferred_element_type=f32)

    walk(span_ref, qb, step)
    for h in range(nh):
        rows = pl.ds(h * HEAD_DIM, HEAD_DIM)
        oT_ref[rows, :] = acc_s[rows, :] / l_s[h:h + 1, :]
        lse_ref[h:h + 1, :] = m_s[h:h + 1, :] + jnp.log2(l_s[h:h + 1, :])
    o_ref[...] = oT_ref[...].T.astype(bf16)


def backward_kernel(nh, blk, unit, span_ref, qT_ref, kT_ref, vT_ref, do_ref, oT_ref, lse_ref, table_ref, lo_ref,
                    old0_ref, old1_ref, d0_ref, d1_ref, k_s, v_s, qm_s, dm_s, qn_s, dn_s, acc_s, dk_s, dv_s, p_s, ds_s, dl_s):
    qb = pl.program_id(0)
    dim = nh * HEAD_DIM
    length = kT_ref.shape[1]
    count = length // blk
    scale = HEAD_DIM**-0.5
    core, place = span_ref[0], span_ref[1]

    @pl.when(qb == 0)
    def _():
        for c in range(count):
            k_s[pl.ds(c * blk, blk), :] = kT_ref[:, pl.ds(c * blk, blk)].T
            v_s[pl.ds(c * blk, blk), :] = vT_ref[:, pl.ds(c * blk, blk)].T
        dk_s[...] = jnp.zeros_like(dk_s)
        dv_s[...] = jnp.zeros_like(dv_s)

    doT = do_ref[...].T
    q = qT_ref[...].T
    lane = lax.broadcasted_iota(jnp.int32, (blk, PAIR), 1)
    prod = doT.astype(f32) * oT_ref[...]
    for h in range(nh):
        own = h % 2
        rows = slice(h * HEAD_DIM, (h + 1) * HEAD_DIM)
        zero = jnp.zeros((HEAD_DIM, blk), bf16)
        qm_s[h, pl.ds(own * HEAD_DIM, HEAD_DIM), :] = qT_ref[pl.ds(h * HEAD_DIM, HEAD_DIM), :]
        qm_s[h, pl.ds((1 - own) * HEAD_DIM, HEAD_DIM), :] = zero
        dm_s[h, pl.ds(own * HEAD_DIM, HEAD_DIM), :] = doT[rows, :]
        dm_s[h, pl.ds((1 - own) * HEAD_DIM, HEAD_DIM), :] = zero
        mine = (lane // HEAD_DIM) == own
        pair = slice((h // 2) * PAIR, (h // 2) * PAIR + PAIR)
        qn_s[h // 2, pl.ds(own * blk, blk), :] = jnp.where(mine, q[:, pair], jnp.zeros((), bf16))
        dn_s[h // 2, pl.ds(own * blk, blk), :] = jnp.where(mine, do_ref[:, pair], jnp.zeros((), bf16))
        dl_s[h:h + 1, :] = jnp.sum(prod[rows, :], axis=0, keepdims=True)
    acc_s[...] = jnp.zeros_like(acc_s)
    lowest = lo_ref[...]

    def step(kb, masked):
        at = pl.multiple_of(kb * blk, blk)
        if masked:
            ok = allowed(lowest, kb, qb, blk)
        for g in range(nh // 2):
            lanes = pl.ds(g * PAIR, PAIR)
            for own in range(2):
                h = 2 * g + own
                rows = pl.ds(h * HEAD_DIM, HEAD_DIM)
                s = jnp.dot(k_s[pl.ds(at, blk), lanes], qm_s[h], preferred_element_type=f32) * (LOG2E * scale)
                p = jnp.exp2(s - lse_ref[h:h + 1, :])
                if masked:
                    p = jnp.where(ok, p, 0.0)
                dp = jnp.dot(v_s[pl.ds(at, blk), lanes], dm_s[h], preferred_element_type=f32)
                ds = (p * (dp - dl_s[h:h + 1, :])).astype(bf16)
                p_s[g, :, pl.ds(own * blk, blk)] = p.astype(bf16)
                ds_s[g, :, pl.ds(own * blk, blk)] = ds
                acc_s[rows, :] += jnp.dot(kT_ref[rows, pl.ds(at, blk)], ds, preferred_element_type=f32)
            dv_s[pl.ds(at, blk), lanes] += jnp.dot(p_s[g], dn_s[g], preferred_element_type=f32)
            dk_s[pl.ds(at, blk), lanes] += jnp.dot(ds_s[g], qn_s[g], preferred_element_type=f32)

    walk(span_ref, qb, step)

    def turned_back(values, at, size, kind):
        cosine = table_ref[2 * kind, :, pl.ds(at, size)] * scale
        sine = table_ref[2 * kind + 1, :, pl.ds(at, size)] * scale
        out = []
        for h in range(nh):
            one = values[h * HEAD_DIM:h * HEAD_DIM + HALF]
            two = values[h * HEAD_DIM + HALF:(h + 1) * HEAD_DIM]
            out += [one * cosine + two * sine, two * cosine - one * sine]
        return jnp.concatenate(out, axis=0).T.astype(bf16)

    spots = blk // (2 * unit)
    for u in range(spots):
        dst = pl.multiple_of(((qb * spots + u) ^ place) * unit, unit)
        for half, ref in ((0, d0_ref), (1, d1_ref)):
            at = pl.multiple_of((2 * u + (core ^ half)) * unit, unit)
            ref[pl.ds(dst, unit), pl.ds(0, dim)] = turned_back(
                acc_s[:, pl.ds(at, unit)], pl.multiple_of(qb * blk + at, unit), unit, 0)

    @pl.when(qb == count - 1)
    def _():
        def store(j, carry):
            dst = pl.multiple_of((j ^ place) * unit, unit)
            for half, ref in ((0, d0_ref), (1, d1_ref)):
                at = pl.multiple_of((2 * j + (core ^ half)) * unit, unit)
                ref[pl.ds(dst, unit), pl.ds(dim, dim)] = turned_back(dk_s[pl.ds(at, unit), :].T, at, unit, 1)
                ref[pl.ds(dst, unit), pl.ds(2 * dim, dim)] = dv_s[pl.ds(at, unit), :].astype(bf16)
            return carry

        lax.fori_loop(0, length // (2 * unit), store, 0)


PARAMS = pltpu.CompilerParams(dimension_semantics=("arbitrary",), vmem_limit_bytes=60 * 2**20)


def span_of(lowest, blk, core, place):
    count = lowest.shape[0] // blk
    blocks = lowest.reshape(count, blk)
    own = jnp.arange(count, dtype=jnp.int32)
    first = jnp.minimum(blocks[:, 0] // blk, own)
    clear = jnp.minimum((blocks[:, -1] + blk - 1) // blk, own)
    both = jnp.stack([first, clear], axis=-1).reshape(-1)
    return jnp.concatenate([jnp.stack([core, place]), both]).astype(jnp.int32)


def attention_forward(row, half0, half1, table, lowest, span, blk, unit):
    length = lowest.shape[0]
    dim = half0.shape[0] // 3
    nh, count = dim // HEAD_DIM, length // blk
    spots = blk // (2 * unit)
    sds = jax.ShapeDtypeStruct
    pick = pl.BlockSpec((dim, blk // 2), lambda q, s: (0, row * count + (q ^ lax.div(s[1], spots))))
    keys = pl.BlockSpec((dim, length // 2), lambda q, s: (1, row))
    values = pl.BlockSpec((dim, length // 2), lambda q, s: (2, row))
    wide = pl.BlockSpec((dim, length), lambda q, s: (0, 0))
    cut = pl.BlockSpec((dim, blk), lambda q, s: (0, q))
    return pl.pallas_call(
        functools.partial(forward_kernel, nh, blk, unit),
        out_shape=(sds((length, dim), bf16), sds((dim, length), f32), sds((nh, length), f32),
                   sds((dim, length), bf16), sds((dim, length), bf16), sds((dim, length), bf16)),
        grid_spec=pltpu.PrefetchScalarGridSpec(
            num_scalar_prefetch=1, grid=(count,),
            in_specs=[pick, pick, keys, keys, values, values,
                      pl.BlockSpec((4, HALF, length), lambda q, s: (0, 0, 0)),
                      pl.BlockSpec((1, blk), lambda q, s: (0, q))],
            out_specs=[pl.BlockSpec((blk, dim), lambda q, s: (q, 0)), cut,
                       pl.BlockSpec((nh, blk), lambda q, s: (0, q)), cut, wide, wide],
            scratch_shapes=[pltpu.VMEM((length, dim), bf16), pltpu.VMEM((nh, PAIR, blk), bf16), pltpu.VMEM((dim, blk), f32),
                            pltpu.VMEM((8, blk), f32), pltpu.VMEM((8, blk), f32)]),
        compiler_params=PARAMS, name="attention_forward",
        cost_estimate=pl.CostEstimate(flops=4 * 4 * dim * length * length // 2, bytes_accessed=10 * 2**20,
                                      transcendentals=nh * length * length // 2),
    )(span, half0, half1, half0, half1, half0, half1, table, lowest[None, :])


def attention_backward(row, rows, saved, do, table, lowest, span, blk, unit, before):
    oT, lse, qT, kT, vT = saved
    length = lowest.shape[0]
    dim = qT.shape[0]
    nh, count = dim // HEAD_DIM, length // blk
    sds = jax.ShapeDtypeStruct
    cut = pl.BlockSpec((dim, blk), lambda q, s: (0, q))
    wide = pl.BlockSpec((dim, length), lambda q, s: (0, 0))
    grad = pl.BlockSpec((length // 2, 3 * dim), lambda q, s: (row, 0))
    whole = sds((rows * length // 2, 3 * dim), bf16)
    kernel = functools.partial(backward_kernel, nh, blk, unit)
    if before is None:
        def call(span_ref, *refs):
            kernel(span_ref, *refs[:8], None, None, *refs[8:])
    else:
        call = kernel
    return pl.pallas_call(
        call,
        out_shape=(whole, whole),
        grid_spec=pltpu.PrefetchScalarGridSpec(
            num_scalar_prefetch=1, grid=(count,),
            in_specs=[cut, wide, wide, pl.BlockSpec((blk, dim), lambda q, s: (q, 0)), cut,
                      pl.BlockSpec((nh, blk), lambda q, s: (0, q)),
                      pl.BlockSpec((4, HALF, length), lambda q, s: (0, 0, 0)),
                      pl.BlockSpec((1, blk), lambda q, s: (0, q))]
            + ([] if before is None else [pl.BlockSpec(memory_space=pl.ANY)] * 2),
            out_specs=[grad, grad],
            scratch_shapes=[pltpu.VMEM((length, dim), bf16), pltpu.VMEM((length, dim), bf16),
                            pltpu.VMEM((nh, PAIR, blk), bf16), pltpu.VMEM((nh, PAIR, blk), bf16),
                            pltpu.VMEM((nh // 2, 2 * blk, PAIR), bf16), pltpu.VMEM((nh // 2, 2 * blk, PAIR), bf16),
                            pltpu.VMEM((dim, blk), f32), pltpu.VMEM((length, dim), f32), pltpu.VMEM((length, dim), f32),
                            pltpu.VMEM((nh // 2, blk, 2 * blk), bf16), pltpu.VMEM((nh // 2, blk, 2 * blk), bf16),
                            pltpu.VMEM((8, blk), f32)]),
        compiler_params=PARAMS, name="attention_backward",
        input_output_aliases={} if before is None else {9: 0, 10: 1},
        cost_estimate=pl.CostEstimate(flops=10 * 4 * dim * length * length // 2, bytes_accessed=20 * 2**20,
                                      transcendentals=nh * length * length // 2),
    )(span, qT, kT, vT, do, oT, lse, table, lowest[None, :], *(before or ()))


def hat_of(values):
    center = values - jnp.mean(values, axis=-1, keepdims=True)
    rstd = lax.rsqrt(jnp.mean(center * center, axis=-1, keepdims=True) + EPS)
    return center * rstd, rstd


def hat_back(hat, rstd, grad):
    return rstd * (grad - jnp.mean(grad, axis=-1, keepdims=True) - hat * jnp.mean(grad * hat, axis=-1, keepdims=True))


def wide_row(o_ref):
    return jnp.concatenate([o_ref[i] for i in range(o_ref.shape[0])], axis=1).astype(f32)


def middle_forward_kernel(o_ref, x_ref, w_ref, c_ref, x1_ref, b_ref):
    c = hat_of(wide_row(o_ref))[0].astype(bf16)
    c_ref[...] = c
    x1 = x_ref[...].astype(f32) + jnp.dot(c, w_ref[...], preferred_element_type=f32)
    x1_ref[...] = x1
    b_ref[...] = hat_of(x1)[0].astype(bf16)


def middle_forward(o, x, w):
    n, size, dim = o.shape
    width = n * dim
    step = min(128, size)
    sds = jax.ShapeDtypeStruct
    flat = pl.BlockSpec((step, width), lambda t: (t, 0))
    return pl.pallas_call(
        middle_forward_kernel,
        out_shape=(sds((size, width), bf16), sds((size, width), f32), sds((size, width), bf16)),
        grid=(size // step,),
        in_specs=[pl.BlockSpec((n, step, dim), lambda t: (0, t, 0)), flat,
                  pl.BlockSpec((width, width), lambda t: (0, 0))],
        out_specs=(flat, flat, flat),
        compiler_params=PARAMS, name="middle_forward",
        cost_estimate=pl.CostEstimate(flops=2 * size * width * width, bytes_accessed=14 * 2**20, transcendentals=0),
    )(o, x, w)


def middle_backward_kernel(o_ref, x1_ref, db_ref, dy_ref, w_ref, dx_ref, low_ref, do_ref):
    hat, rstd = hat_of(x1_ref[...])
    dx1 = dy_ref[...].astype(f32) + hat_back(hat, rstd, db_ref[...])
    dx_ref[...] = dx1
    low_ref[...] = dx1.astype(bf16)
    dc = times_rows(dx1.astype(bf16), w_ref[...])
    hat, rstd = hat_of(wide_row(o_ref))
    d_o = hat_back(hat, rstd, dc).astype(bf16)
    dim = do_ref.shape[2]
    for i in range(do_ref.shape[0]):
        do_ref[i] = d_o[:, i * dim:(i + 1) * dim]


def middle_backward(row, o, x1, db, dy, w):
    n, size, dim = o.shape
    width = n * dim
    step = min(128, size)
    sds = jax.ShapeDtypeStruct
    flat = pl.BlockSpec((step, width), lambda t: (t, 0))
    part = pl.BlockSpec((n, step, dim), lambda t: (0, t, 0))
    return pl.pallas_call(
        middle_backward_kernel,
        out_shape=(sds((size, width), f32), sds((size, width), bf16), sds((n, size, dim), bf16)),
        grid=(size // step,),
        in_specs=[part, flat, pl.BlockSpec((step, width), lambda t: (row * (size // step) + t, 0)), flat,
                  pl.BlockSpec((width, width), lambda t: (0, 0))],
        out_specs=(flat, flat, part),
        compiler_params=PARAMS, name="middle_backward",
        cost_estimate=pl.CostEstimate(flops=2 * size * width * width, bytes_accessed=16 * 2**20, transcendentals=0),
    )(o, x1, db, dy, w)


def ways(row, n):
    bits = [1 << k for k in range(1, n.bit_length() - 1)]
    return bits if row % 2 == 0 else bits[::-1]


def times_rows(a, w):
    return lax.dot_general(a, w, (((1,), (1,)), ((), ())), preferred_element_type=f32)


def weight_copies(all_ref, kind, dst_ref, sems, first=0):
    m, lines, ff = all_ref.shape
    unit = ff // m
    pieces = dst_ref.shape[1 if kind == "down" else 0] // ff
    depth = lines - unit * pieces
    copies = []
    for r in range(m):
        if kind == "up":
            moves = [(all_ref.at[r, pl.ds(0, depth), :], dst_ref.at[pl.ds(r * depth, depth), :])]
        else:
            moves = [(all_ref.at[r, pl.ds(depth + q * unit, unit), :],
                      dst_ref.at[pl.ds(r * unit, unit), pl.ds(q * ff, ff)]) for q in range(pieces)]
        for src, dst in moves:
            copies.append(pltpu.make_async_copy(src, dst, sems.at[first + len(copies)]))
    for copy in copies:
        copy.start()
    return copies


def product_sum_kernel(n, rows, cols, turned, kind, x0_ref, x1_ref, w_ref, o_ref, part_s, core_s, sum_s, got_s, send_sem, recv_sem,
                       *own_w):
    mine = lax.axis_index("ctx")
    loads = []
    if kind:
        loads = weight_copies(w_ref, kind, *own_w)
        w_ref = own_w[0]
    spots = n // 2
    size = x0_ref.shape[0] // (rows * spots)
    width = o_ref.shape[1]
    barrier = pltpu.get_barrier_semaphore()
    bits = [1] + ways(0, n)
    for bit in bits:
        pl.semaphore_signal(barrier, inc=1, device_id={"ctx": mine ^ bit}, device_id_type=pl.DeviceIdType.MESH)
    pl.semaphore_wait(barrier, len(bits))
    for copy in loads:
        copy.wait()
    copies = []

    def send(src, dst, bit):
        at = len(copies)
        copy = pltpu.make_async_remote_copy(
            src_ref=src, dst_ref=dst, send_sem=send_sem.at[at], recv_sem=recv_sem.at[at],
            device_id={"ctx": mine ^ bit}, device_id_type=pl.DeviceIdType.MESH)
        copy.start()
        copies.append(copy)
        return copy

    def key(row, k):
        return [-(k & (bit >> 1)) for bit in ways(row, n)]

    orders = []
    for r in range(rows):
        way = [bit >> 1 for bit in ways(r, n)]
        orders.append(sorted(range(spots), key=lambda k: [0 if k & bit else 1 for bit in way]))
    todo = [(r, orders[r][t]) for t in range(spots) for r in range(rows)]
    inbox, slot, slots = {}, {}, 0

    def product(x_ref, r, k, finish):
        begin = (r * spots + k) * size

        @pl.loop(0, width // cols)
        def _(c):
            at = pl.ds(pl.multiple_of(c * cols, cols), cols)
            x = x_ref[pl.ds(begin, size), :]
            finish(at, times_rows(x, w_ref[at, :]) if turned else jnp.dot(x, w_ref[:, at], preferred_element_type=f32))

    def pair(r, k):
        spot = r * spots + k

        def keep(at, value):
            part_s[spot, :, at] = value.astype(bf16)

        product(x1_ref, r, k, keep)
        inbox[r, k] = send(part_s.at[spot], core_s.at[spot], 1)

    def own(r, k):
        spot = r * spots + k
        inbox[r, k].wait_recv()

        def add(at, value):
            sum_s[spot, :, at] = (value + core_s[spot, :, at].astype(f32)).astype(bf16)

        product(x0_ref, r, k, add)

    def pass_on(r, k, stage):
        nonlocal slots
        bit = ways(r, n)[stage]
        if k & (bit >> 1):
            inbox[r, k ^ (bit >> 1), stage] = (send(sum_s.at[r * spots + k], got_s.at[slots], bit), slots)
            slots += 1

    group = max(rows * spots // 2, 1)
    for begin in range(0, len(todo), group):
        for r, k in todo[begin:begin + group]:
            pair(r, k)
        for r, k in todo[begin:begin + group]:
            own(r, k)
            pass_on(r, k, 0)
    stages = len(bits) - 1
    for stage in range(stages):
        for r, k in todo:
            way = [bit >> 1 for bit in ways(r, n)]
            if any(k & bit for bit in way[:stage + 1]):
                continue
            copy, at = inbox[r, k, stage]
            copy.wait_recv()
            spot = r * spots + k
            if stage == stages - 1:
                o_ref[pl.ds(r * size, size), :] = sum_s[spot].astype(f32) + got_s[at].astype(f32)
            else:
                sum_s[spot] = (sum_s[spot].astype(f32) + got_s[at].astype(f32)).astype(bf16)
                pass_on(r, k, stage + 1)
    for copy in copies:
        copy.wait_send()


def product_sum(x0, x1, w, rows, n, collective_id, turned=False, kind=None, wide=None):
    size = x0.shape[0] // (rows * (n // 2))
    depth = x0.shape[1]
    width = wide if kind else w.shape[0 if turned else 1]
    count = rows * (n // 2)
    moves = count + rows * (n // 2 - 1)
    vmem = pl.BlockSpec(memory_space=pltpu.VMEM)
    flops = 4 * x0.shape[0] * x0.shape[1] * width
    return pl.pallas_call(
        functools.partial(product_sum_kernel, n, rows, min(512, width), turned, kind),
        out_shape=jax.ShapeDtypeStruct((rows * size, width), f32),
        in_specs=[vmem, vmem, pl.BlockSpec(memory_space=pl.ANY) if kind else vmem], out_specs=vmem,
        scratch_shapes=[pltpu.VMEM((count, size, width), bf16), pltpu.VMEM((count, size, width), bf16),
                        pltpu.VMEM((count, size, width), bf16), pltpu.VMEM((moves - count, size, width), bf16),
                        pltpu.SemaphoreType.DMA((moves,)), pltpu.SemaphoreType.DMA((moves,))]
        + ([pltpu.VMEM((width, depth) if turned else (depth, width), bf16), pltpu.SemaphoreType.DMA((64,))] if kind else []),
        compiler_params=pltpu.CompilerParams(collective_id=collective_id, has_side_effects=True, vmem_limit_bytes=60 * 2**20),
        name="product_sum",
        cost_estimate=pl.CostEstimate(flops=4 * flops, bytes_accessed=20 * 2**20, transcendentals=0),
    )(x0, x1, w)


def gather_product_kernel(n, rows, cols, b_ref, dy0_ref, dy1_ref, w_ref, b0_ref, b1_ref, h0_ref, h1_ref, d0_ref, d1_ref,
                          stat_ref, up_ref, down_ref, got_s, d_s, h_s, dy_s, w_sem, send_sem, recv_sem, dy_sem, b_sem, h_sem, d_sem):
    mine = lax.axis_index("ctx")
    spots = n // 2
    size = b_ref.shape[0] // rows
    ff = up_ref.shape[1]
    loads = weight_copies(w_ref, "down", down_ref, w_sem)
    loads_up = weight_copies(w_ref, "up", up_ref, w_sem, len(loads))
    count = rows * spots
    barrier = pltpu.get_barrier_semaphore()
    bits = [1] + ways(0, n)
    for bit in bits:
        pl.semaphore_signal(barrier, inc=1, device_id={"ctx": mine ^ bit}, device_id_type=pl.DeviceIdType.MESH)
    pl.semaphore_wait(barrier, len(bits))
    sends, locals_, arrival = [], [], {}

    def send(src, half, row, k, bit):
        at, to = len(sends), half * count + row * spots + k
        copy = pltpu.make_async_remote_copy(
            src_ref=src, dst_ref=got_s.at[to], send_sem=send_sem.at[at], recv_sem=recv_sem.at[at],
            device_id={"ctx": mine ^ bit}, device_id_type=pl.DeviceIdType.MESH)
        copy.start()
        sends.append(copy)
        arrival[half, row, k] = copy

    def held(half, row, k):
        if half == 0 and k == 0:
            return b_ref.at[pl.ds(row * size, size), :]
        return got_s.at[half * count + row * spots + k]

    def onward(row, k):
        way = ways(row, n)
        top = max([s for s, bit in enumerate(way) if k & (bit >> 1)], default=-1)
        for bit in way[top + 1:]:
            send(held(0, row, k), 0, row, k | (bit >> 1), bit)
        send(held(0, row, k), 1, row, k, 1)

    for r in range(rows):
        onward(r, 0)

    def fetch(t, slot):
        begin = pl.multiple_of(lax.rem(t, count) * size, size)

        @pl.when(t < count)
        def _():
            pltpu.make_async_copy(dy0_ref.at[pl.ds(begin, size), :], dy_s.at[slot], dy_sem.at[slot]).start()

        @pl.when(t >= count)
        def _():
            pltpu.make_async_copy(dy1_ref.at[pl.ds(begin, size), :], dy_s.at[slot], dy_sem.at[slot]).start()

    fetch(0, 0)
    for copy in loads:
        copy.wait()

    @pl.loop(0, 2 * count)
    def _(t):
        slot = lax.rem(t, 2)

        @pl.when(t + 1 < 2 * count)
        def _():
            fetch(t + 1, 1 - slot)

        pltpu.make_async_copy(dy0_ref.at[pl.ds(0, size), :], dy_s.at[slot], dy_sem.at[slot]).wait()

        @pl.loop(0, ff // cols)
        def _(c):
            at = pl.ds(pl.multiple_of(c * cols, cols), cols)
            d_s[t, :, at] = times_rows(dy_s[slot], down_ref[at, :])

    for t in range(2 * count):
        dst = (d0_ref, d1_ref)[t // count].at[pl.ds((t % count) * size, size), :]
        copy = pltpu.make_async_copy(d_s.at[t], dst, d_sem.at[t])
        copy.start()
        locals_.append(copy)

    for copy in loads_up:
        copy.wait()
    outs = []
    lane = lax.broadcasted_iota(jnp.int32, (32, 128), 1)

    def block(half, row, k):
        t = half * count + row * spots + k
        src = held(half, row, k)
        copy = pltpu.make_async_copy(src, (b0_ref, b1_ref)[half].at[pl.ds((t % count) * size, size), :], b_sem.at[t])
        copy.start()
        locals_.append(copy)
        slot = len(outs) % 2
        if len(outs) >= 2:
            outs[-2].wait()

        @pl.loop(0, ff // cols)
        def _(c):
            at = pl.ds(pl.multiple_of(c * cols, cols), cols)
            h_s[slot, :, at] = jnp.dot(src[...], up_ref[:, at], preferred_element_type=f32)

        copy = pltpu.make_async_copy(h_s.at[slot], (h0_ref, h1_ref)[half].at[pl.ds((t % count) * size, size), :], h_sem.at[t])
        copy.start()
        outs.append(copy)

        @pl.loop(0, size // 32)
        def _(c):
            at = pl.ds(pl.multiple_of(c * 32, 32), 32)
            h = h_s[slot, at, :]
            gel = h * (0.5 * (1.0 + lax.erf(h * (2.0**-0.5))))
            d = d_s[t, at, :]
            mean = jnp.mean(gel, axis=-1, keepdims=True)
            off = gel - mean
            spread = jnp.sum(off * off, axis=-1, keepdims=True)
            total = jnp.sum(d, axis=-1, keepdims=True)
            cross = jnp.sum(d * off, axis=-1, keepdims=True)
            line = jnp.where(lane == 0, mean, jnp.where(lane == 1, spread, jnp.where(lane == 2, total, cross)))
            stat_ref[pl.ds(pl.multiple_of(t * size + c * 32, 32), 32), :] = line

    order = []
    for k in range(spots):
        for r in range(rows):
            way = ways(r, n)
            order.append((r, sum((bit >> 1) for s, bit in enumerate(way) if k >> s & 1)))
    for begin in range(0, len(order), rows):
        some = order[begin:begin + rows]
        for r, k in some:
            if k:
                arrival[0, r, k].wait_recv()
                onward(r, k)
        for r, k in some:
            block(0, r, k)
        for r, k in some:
            arrival[1, r, k].wait_recv()
            block(1, r, k)
    for copy in outs[-2:] + locals_:
        copy.wait()
    for copy in sends:
        copy.wait_send()


def gather_product(b, dy0, dy1, weights, rows, n, collective_id):
    size = b.shape[0] // rows
    width, ff = b.shape[1], weights.shape[2]
    count = rows * (n // 2)
    half = count * size
    moves = rows * (n - 1)
    vmem, here = pl.BlockSpec(memory_space=pltpu.VMEM), pl.BlockSpec(memory_space=pl.ANY)
    sds = jax.ShapeDtypeStruct
    return pl.pallas_call(
        functools.partial(gather_product_kernel, n, rows, min(256, ff)),
        out_shape=(sds((half, width), bf16),) * 2 + (sds((half, ff), f32),) * 4 + (sds((2 * half, 128), f32),),
        in_specs=[vmem, here, here, here], out_specs=(here,) * 6 + (vmem,),
        scratch_shapes=[pltpu.VMEM((width, ff), bf16), pltpu.VMEM((ff, width), bf16),
                        pltpu.VMEM((2 * count, size, width), bf16), pltpu.VMEM((2 * count, size, ff), f32),
                        pltpu.VMEM((2, size, ff), f32), pltpu.VMEM((2, size, width), bf16), pltpu.SemaphoreType.DMA((64,)),
                        pltpu.SemaphoreType.DMA((moves,)), pltpu.SemaphoreType.DMA((moves,)), pltpu.SemaphoreType.DMA((2,))]
        + [pltpu.SemaphoreType.DMA((2 * count,))] * 3,
        compiler_params=pltpu.CompilerParams(collective_id=collective_id, has_side_effects=True, vmem_limit_bytes=62 * 2**20),
        name="gather_product",
        cost_estimate=pl.CostEstimate(flops=16 * half * width * ff, bytes_accessed=70 * 2**20, transcendentals=0),
    )(b, dy0, dy1, weights)


def standardize(values):
    center = values - jnp.mean(values, axis=-1, keepdims=True)
    spread = jnp.mean(center * center, axis=-1, keepdims=True)
    rstd = lax.rsqrt(spread + EPS)
    return center * rstd, rstd


def standardize_back(hat, rstd, grad):
    return rstd * (grad - jnp.mean(grad, axis=-1, keepdims=True) - hat * jnp.mean(grad * hat, axis=-1, keepdims=True))


def row_places(lengths, row_len):
    places = jnp.arange(row_len, dtype=jnp.int32)
    ends = jnp.cumsum(lengths, axis=-1)
    passed = ends[:, None, :] <= places[None, :, None]
    starts = jnp.sum(jnp.where(passed, lengths[:, None, :], 0), axis=-1)
    valid = places[None, :] < ends[:, -1:]
    lowest = jnp.where(valid, starts, places[None, :]).astype(jnp.int32)
    return (places[None, :] - starts).astype(f32), lowest


def xpos_tables(relative):
    ladder = jnp.arange(HALF, dtype=f32) / HALF
    rate = jnp.power(10000.0, -ladder)
    base = (ladder + 0.4) / 1.4
    angles = rate[None, :, None] * relative[:, None, :]
    power = (relative[:, None, :] - ROW_LEN / 2) / XPOS_BASE
    factor = jnp.power(base[None, :, None], power)
    cosine, sine = jnp.cos(angles), jnp.sin(angles)
    return jnp.stack([cosine * factor, sine * factor, cosine / factor, sine / factor], axis=1)


def dot(a, b, spec, kind=f32):
    return jnp.einsum(spec, a, b, preferred_element_type=f32).astype(kind)


def swap(x, bit):
    n = lax.axis_size("ctx")
    return lax.ppermute(x, "ctx", [(i, i ^ bit) for i in range(n)])


def exchange(blocks):
    n = lax.axis_size("ctx")
    mine = lax.axis_index("ctx")
    out = jnp.zeros_like(blocks)
    for bit in range(n):
        block = lax.dynamic_index_in_dim(blocks, mine ^ bit, 0, False)
        block = swap(block, bit) if bit else block
        out = lax.dynamic_update_index_in_dim(out, block, mine ^ bit, 0)
    return out


def after(x, *others):
    return lax.optimization_barrier((x, *others))[0]


def gather_start(x):
    return [{0: x[r]} for r in range(x.shape[0])]


def gather_step(held, step):
    n = lax.axis_size("ctx")
    out = []
    for r, parts in enumerate(held):
        bit = ways(r, n)[step]
        out.append({**parts, **{k | bit: swap(v, bit) for k, v in parts.items()}})
    return out


def gather_steps():
    return lax.axis_size("ctx").bit_length() - 2


def gather_end(held):
    return jnp.concatenate([parts[k] for parts in held for k in sorted(parts)], axis=0)


def gather_half(x):
    held = gather_start(x)
    for step in range(gather_steps()):
        held = gather_step(held, step)
    return gather_end(held)


def plus(a, b, kind=bf16):
    return (a.astype(f32) + b.astype(f32)).astype(kind)


def reduce_start(half0, half1, rows):
    n = lax.axis_size("ctx")
    width = half0.shape[-1]
    both = plus(half0, swap(half1, 1)).reshape(rows, n // 2, -1, width)
    return [{2 * k: both[r, k] for k in range(n // 2)} for r in range(rows)]


def reduce_step(held, step):
    n = lax.axis_size("ctx")
    out = []
    for r, parts in enumerate(held):
        bit = ways(r, n)[step]
        kind = bf16 if len(parts) > 2 else f32
        out.append({k: plus(v, swap(parts[k | bit], bit), kind) for k, v in parts.items() if not k & bit})
    return out


def reduce_end(held):
    return jnp.concatenate([parts[0] for parts in held], axis=0)


def reduce_halves(half0, half1, rows):
    held = reduce_start(half0, half1, rows)
    for step in range(gather_steps()):
        held = reduce_step(held, step)
    return reduce_end(held)


def body(inputs, doc_len, w_query, w_key, w_value, w_out, w_up, w_down, gain_attn, gain_attn_sub, gain_ffn,
         gain_ffn_sub, out_cotangent):
    rows, local_len, width = inputs.shape
    n, m = lax.axis_size("ctx"), lax.axis_size("row")
    row_len = local_len * n
    tokens, half = rows * local_len, rows * row_len // 2
    piece = w_query.shape[0]
    heads_dim = width // n
    ff = w_up.shape[1]
    unit = ff // (n * m)
    ff_dev = unit * m
    blk = min(512, row_len)
    mine = lax.axis_index("ctx")
    core, place = mine & 1, mine >> 1

    def scaled(w, gain):
        return (w.astype(f32) * gain.astype(f32)[:, None]).astype(bf16)

    x_own = inputs.reshape(tokens, width).astype(f32)
    x_hat, x_rstd = standardize(x_own)
    x_low = x_hat.astype(bf16)
    x_held = gather_step(gather_start(x_low.reshape(rows, local_len, width)), 0)

    qkv_local = jnp.concatenate(
        [scaled(w, gain_attn).reshape(piece, n, heads_dim) for w in (w_query, w_key, w_value)], axis=2)
    qkv_part = exchange(qkv_local.transpose(1, 0, 2)).reshape(n * piece, 3 * heads_dim)
    x_held, qkv_part = lax.optimization_barrier((x_held, qkv_part))
    w_qkv = lax.all_gather(qkv_part, "row", axis=0, tiled=True)
    up_local = scaled(after(w_up, qkv_part), gain_ffn).reshape(piece, m, n, unit).transpose(2, 0, 1, 3).reshape(n, piece, ff_dev)
    up_part = lax.all_to_all(up_local, "ctx", split_axis=0, concat_axis=0, tiled=True).reshape(n * piece, ff_dev)
    for step in range(1, gather_steps()):
        x_held = gather_step(x_held, step)
    xh0 = gather_end(x_held)
    xh0, up_part = lax.optimization_barrier((xh0, up_part))
    xh1 = swap(xh0, 1)
    down_local = scaled(w_down, gain_ffn_sub)
    ffn_local = jnp.concatenate([up_part] + [down_local[:, q:q + ff_dev] for q in range(0, width, ff_dev)], axis=0)
    out_all = lax.all_gather(scaled(w_out, gain_attn_sub), BOTH, axis=0, tiled=True)

    relative, lowest = row_places(doc_len, row_len)
    table = xpos_tables(relative)
    span = [span_of(lowest[r], blk, core, place) for r in range(rows)]
    qkv0 = dot(w_qkv, xh0, "df,td->ft")
    qkv1 = dot(w_qkv, xh1, "df,td->ft")
    qkv0, qkv1, cot = lax.optimization_barrier((qkv0, qkv1, out_cotangent))
    dy_held = gather_step(gather_start(cot), 0)
    dy_steps = gather_steps()
    saved, o = [], []
    for r in range(rows):
        o_row, *kept = attention_forward(r, qkv0, qkv1, table[r], lowest[r], span[r], blk, local_len)
        if r == 0:
            o_row, kept, qkv0, qkv1, dy_held, out_all = lax.optimization_barrier((o_row, kept, qkv0, qkv1, dy_held, out_all))
            ffn_all = lax.all_gather(after(ffn_local, out_all), "row", axis=0, tiled=False)
            for step in range(1, dy_steps):
                dy_held = gather_step(dy_held, step)
        if r == rows - 1:
            o_row, o = lax.optimization_barrier((o_row, o))
        saved.append(kept)
        o.append(lax.all_to_all(o_row.reshape(n, local_len, heads_dim), "ctx", split_axis=0, concat_axis=0, tiled=True))
    c, x1, b_low = zip(*[middle_forward(o[r], inputs[r], out_all) for r in range(rows)])
    b_low, dy_held = lax.optimization_barrier((b_low, dy_held))
    dy0 = gather_end(dy_held)
    dy1 = swap(dy0, 1)

    b0, b1, h0, h1, d_hat0, d_hat1, stats = gather_product(jnp.concatenate(b_low), dy0, dy1, ffn_all, rows, n, 4)
    stats = stats[:, :4].T
    order = jnp.arange(n // 2, dtype=jnp.int32) ^ place
    halves = jnp.arange(2, dtype=jnp.int32) ^ core

    def reorder(v):
        v = v.reshape(v.shape[0], 2, rows, n // 2, local_len)
        return jnp.take(jnp.take(v, halves, axis=1), order, axis=3).reshape(v.shape[0], 2 * half)

    stats = lax.all_gather(reorder(stats), "ctx", axis=0, tiled=False)
    mean = jnp.mean(stats[:, 0], axis=0)
    shift = stats[:, 0] - mean
    var = (jnp.sum(stats[:, 1], axis=0) + ff_dev * jnp.sum(shift * shift, axis=0)) / ff
    rstd = lax.rsqrt(var + EPS)
    d_mean = jnp.sum(stats[:, 2], axis=0) / ff
    d_corr = rstd * jnp.sum(stats[:, 3] + stats[:, 2] * shift, axis=0) / ff
    merged = reorder(jnp.stack([mean, rstd, d_mean, d_corr])).reshape(4, 2, half, 1)

    def finish(h, d_hat, which):
        cdf = 0.5 * (1.0 + lax.erf(h * (2.0**-0.5)))
        mean, rstd, d_mean, d_corr = (merged[k, which] for k in range(4))
        hat = (h * cdf - mean) * rstd
        d_gel = rstd * (d_hat - d_mean - hat * d_corr)
        pdf = jnp.exp(-0.5 * h * h) * 0.3989422804014327
        return hat.astype(bf16), (d_gel * (cdf + h * pdf)).astype(bf16)

    e0, dh0 = finish(h0, d_hat0, 0)
    e1, dh1 = finish(h1, d_hat1, 1)
    down_part = (dot(e0, dy0, "tf,td->fd") + dot(e1, dy1, "tf,td->fd")).astype(bf16)
    up_part = (dot(b0, dh0, "td,tf->df") + dot(b1, dh1, "td,tf->df")).astype(bf16)
    e0, e1, dh0, dh1, down_part, up_part = lax.optimization_barrier((e0, e1, dh0, dh1, down_part, up_part))
    down_sum = lax.psum_scatter(down_part, "row", scatter_dimension=0, tiled=True)
    db = product_sum(dh0, dh1, ffn_all, rows, n, 1, True, "up", width)
    db, up_part, down_sum = lax.optimization_barrier((db, up_part, down_sum))
    down_raw = down_sum.astype(f32)
    up_sum = lax.psum_scatter(up_part, "row", scatter_dimension=0, tiled=True)

    dx1, dx1b, d_o = zip(*[middle_backward(r, o[r], x1[r], db, out_cotangent[r], out_all) for r in range(rows)])
    do_heads = [lax.all_to_all(v, "ctx", split_axis=0, concat_axis=0, tiled=True).reshape(row_len, heads_dim) for v in d_o]
    c_order = jnp.concatenate(c).reshape(tokens, m, n, piece).transpose(0, 2, 1, 3).reshape(tokens, width)
    out_part = dot(c_order, jnp.concatenate(dx1b), "td,te->de", bf16)
    do_heads[0], out_part = lax.optimization_barrier((do_heads[0], out_part))
    grads = attention_backward(0, rows, saved[0], do_heads[0], table[0], lowest[0], span[0], blk, local_len, None)
    grads, do_heads, up_sum, out_part = lax.optimization_barrier((grads, do_heads, up_sum, out_part))
    out_part = lax.psum_scatter(out_part, "ctx", scatter_dimension=0, tiled=True)
    up_moved = lax.all_to_all(up_sum.reshape(n, piece, ff_dev), "ctx", split_axis=0, concat_axis=2, tiled=True)
    for r in range(1, rows):
        grads = attention_backward(r, rows, saved[r], do_heads[r], table[r], lowest[r], span[r], blk, local_len, grads)
    d0, d1 = grads
    qkv_part = (dot(xh0, d0, "td,tf->df") + dot(xh1, d1, "td,tf->df")).astype(bf16)
    d0, d1, qkv_part, out_part, up_moved = lax.optimization_barrier((d0, d1, qkv_part, out_part, up_moved))
    qkv_part = lax.psum_scatter(qkv_part, "row", scatter_dimension=0, tiled=True)
    da = product_sum(d0, d1, w_qkv, rows, n, 2, True)
    e0, e1, da, qkv_part, out_part = lax.optimization_barrier((e0, e1, da, qkv_part, out_part))
    out_raw = lax.psum_scatter(out_part, "row", scatter_dimension=0, tiled=True).astype(f32)
    up_raw = up_moved.reshape(piece, n, m, unit).transpose(0, 2, 1, 3).reshape(piece, ff).astype(f32)
    qkv_raw = lax.all_to_all(qkv_part.reshape(n, piece, 3 * heads_dim), "ctx", split_axis=0, concat_axis=2, tiled=True)

    ffn = product_sum(e0, e1, ffn_all, rows, n, 3, False, "down", width)
    ffn, out_raw, qkv_raw = lax.optimization_barrier((ffn, out_raw, qkv_raw))
    output = (jnp.stack(x1) + ffn.reshape(rows, local_len, width)).astype(bf16)
    qkv_raw = qkv_raw.reshape(piece, n, 3, heads_dim).astype(f32)
    query_raw, key_raw, value_raw = (qkv_raw[:, :, i].reshape(piece, width) for i in range(3))
    input_grad = jnp.stack(dx1) + standardize_back(x_hat, x_rstd, da).reshape(rows, local_len, width)

    def against(w, raw):
        return jnp.sum(w.astype(f32) * raw, axis=-1)

    def grown(raw, gain):
        return raw * gain.astype(f32)[:, None]

    gain_one = against(w_query, query_raw) + against(w_key, key_raw) + against(w_value, value_raw)
    return (output, input_grad, grown(query_raw, gain_attn), grown(key_raw, gain_attn), grown(value_raw, gain_attn),
            grown(out_raw, gain_attn_sub), grown(up_raw, gain_ffn), grown(down_raw, gain_ffn_sub),
            gain_one, against(w_out, out_raw), against(w_up, up_raw), against(w_down, down_raw))


def solution(mesh):
    split = P(BOTH, None)
    acts = P("row", "ctx", None)
    gain = P(BOTH)
    return jax.shard_map(
        body,
        mesh=mesh,
        in_specs=(acts, P("row", None)) + (split,) * 6 + (gain,) * 4 + (acts,),
        out_specs=(acts, acts) + (split,) * 6 + (gain,) * 4,
        check_vma=False,
    )
```

```python
import functools

import jax
import jax.numpy as jnp
from jax import lax
from jax.experimental import pallas as pl
from jax.experimental.pallas import tpu as pltpu
from jax.sharding import PartitionSpec as P

bf16 = jnp.bfloat16
f32 = jnp.float32
HEAD_DIM = 64
HALF = HEAD_DIM // 2
PAIR = 2 * HEAD_DIM
LOG2E = 1.4426950408889634
NEG = -1e30
ROW_LEN = 2048
XPOS_BASE = 512
EPS = 1e-5
BOTH = ("row", "ctx")


def walk(span_ref, qb, step):
    first = span_ref[2 + 2 * (qb)]
    clear = span_ref[3 + 2 * (qb)]

    def edge(t, carry):
        step(jnp.where(t < clear - first, first + t, qb), True)
        return carry

    def plain(kb, carry):
        step(kb, False)
        return carry

    lax.fori_loop(0, clear - first + 1, edge, 0)
    lax.fori_loop(clear, qb, plain, 0)


def allowed(lowest, kb, qb, blk):
    key = kb * blk + lax.broadcasted_iota(jnp.int32, (blk, blk), 0)
    query = qb * blk + lax.broadcasted_iota(jnp.int32, (blk, blk), 1)
    return (key <= query) & (key >= lowest)


def forward_kernel(nh, blk, unit, span_ref, q0_ref, q1_ref, k0_ref, k1_ref, v0_ref, v1_ref, table_ref, lo_ref,
                   o_ref, oT_ref, lse_ref, qT_ref, kT_ref, vT_ref, k_s, qm_s, acc_s, m_s, l_s):
    qb = pl.program_id(0)
    dim = nh * HEAD_DIM
    length = kT_ref.shape[1]
    core, place = span_ref[0], span_ref[1]
    spots = blk // (2 * unit)
    inner = lax.rem(place, spots)

    def turned(values, at, kind):
        cosine = table_ref[2 * kind, :, pl.ds(at, unit)]
        sine = table_ref[2 * kind + 1, :, pl.ds(at, unit)]
        out = []
        for h in range(nh):
            one = values[h * HEAD_DIM:h * HEAD_DIM + HALF]
            two = values[h * HEAD_DIM + HALF:(h + 1) * HEAD_DIM]
            out += [one * cosine - two * sine, two * cosine + one * sine]
        return jnp.concatenate(out, axis=0).astype(bf16)

    @pl.when(qb == 0)
    def _():
        def load(j, carry):
            src = pl.multiple_of((j ^ place) * unit, unit)
            for half, ref, v_ref in ((0, k0_ref, v0_ref), (1, k1_ref, v1_ref)):
                at = pl.multiple_of((2 * j + (core ^ half)) * unit, unit)
                key = turned(ref[:, pl.ds(src, unit)], at, 1)
                kT_ref[:, pl.ds(at, unit)] = key
                k_s[pl.ds(at, unit), :] = key.T
                vT_ref[:, pl.ds(at, unit)] = v_ref[:, pl.ds(src, unit)].astype(bf16)
            return carry

        lax.fori_loop(0, length // (2 * unit), load, 0)

    for u in range(spots):
        src = pl.multiple_of((u ^ inner) * unit, unit)
        for half, ref in ((0, q0_ref), (1, q1_ref)):
            at = pl.multiple_of((2 * u + (core ^ half)) * unit, unit)
            qT_ref[:, pl.ds(at, unit)] = turned(ref[:, pl.ds(src, unit)], pl.multiple_of(qb * blk + at, unit), 0)
    for h in range(nh):
        own = h % 2
        qm_s[h, pl.ds(own * HEAD_DIM, HEAD_DIM), :] = qT_ref[pl.ds(h * HEAD_DIM, HEAD_DIM), :]
        qm_s[h, pl.ds((1 - own) * HEAD_DIM, HEAD_DIM), :] = jnp.zeros((HEAD_DIM, blk), bf16)
    acc_s[...] = jnp.zeros_like(acc_s)
    m_s[...] = jnp.full_like(m_s, NEG)
    l_s[...] = jnp.zeros_like(l_s)
    lowest = lo_ref[...]

    def step(kb, masked):
        at = pl.multiple_of(kb * blk, blk)
        if masked:
            ok = allowed(lowest, kb, qb, blk)
        for h in range(nh):
            rows = pl.ds(h * HEAD_DIM, HEAD_DIM)
            s = jnp.dot(k_s[pl.ds(at, blk), pl.ds((h // 2) * PAIR, PAIR)], qm_s[h], preferred_element_type=f32)
            s = s * (LOG2E * HEAD_DIM**-0.5)
            if masked:
                s = jnp.where(ok, s, NEG)
            before = m_s[h:h + 1, :]
            now = jnp.maximum(before, jnp.max(s, axis=0, keepdims=True))
            p = jnp.exp2(s - now)
            fade = jnp.exp2(before - now)
            m_s[h:h + 1, :] = now
            l_s[h:h + 1, :] = l_s[h:h + 1, :] * fade + jnp.sum(p, axis=0, keepdims=True)
            acc_s[rows, :] = acc_s[rows, :] * fade + jnp.dot(
                vT_ref[rows, pl.ds(at, blk)], p.astype(bf16), preferred_element_type=f32)

    walk(span_ref, qb, step)
    for h in range(nh):
        rows = pl.ds(h * HEAD_DIM, HEAD_DIM)
        oT_ref[rows, :] = acc_s[rows, :] / l_s[h:h + 1, :]
        lse_ref[h:h + 1, :] = m_s[h:h + 1, :] + jnp.log2(l_s[h:h + 1, :])
    o_ref[...] = oT_ref[...].T.astype(bf16)


def backward_kernel(nh, blk, unit, span_ref, qT_ref, kT_ref, vT_ref, do_ref, oT_ref, lse_ref, table_ref, lo_ref,
                    old0_ref, old1_ref, d0_ref, d1_ref, k_s, v_s, qm_s, dm_s, qn_s, dn_s, acc_s, dk_s, dv_s, p_s, ds_s, dl_s):
    qb = pl.program_id(0)
    dim = nh * HEAD_DIM
    length = kT_ref.shape[1]
    count = length // blk
    scale = HEAD_DIM**-0.5
    core, place = span_ref[0], span_ref[1]

    @pl.when(qb == 0)
    def _():
        for c in range(count):
            k_s[pl.ds(c * blk, blk), :] = kT_ref[:, pl.ds(c * blk, blk)].T
            v_s[pl.ds(c * blk, blk), :] = vT_ref[:, pl.ds(c * blk, blk)].T
        dk_s[...] = jnp.zeros_like(dk_s)
        dv_s[...] = jnp.zeros_like(dv_s)

    doT = do_ref[...].T
    q = qT_ref[...].T
    lane = lax.broadcasted_iota(jnp.int32, (blk, PAIR), 1)
    prod = doT.astype(f32) * oT_ref[...]
    for h in range(nh):
        own = h % 2
        rows = slice(h * HEAD_DIM, (h + 1) * HEAD_DIM)
        zero = jnp.zeros((HEAD_DIM, blk), bf16)
        qm_s[h, pl.ds(own * HEAD_DIM, HEAD_DIM), :] = qT_ref[pl.ds(h * HEAD_DIM, HEAD_DIM), :]
        qm_s[h, pl.ds((1 - own) * HEAD_DIM, HEAD_DIM), :] = zero
        dm_s[h, pl.ds(own * HEAD_DIM, HEAD_DIM), :] = doT[rows, :]
        dm_s[h, pl.ds((1 - own) * HEAD_DIM, HEAD_DIM), :] = zero
        mine = (lane // HEAD_DIM) == own
        pair = slice((h // 2) * PAIR, (h // 2) * PAIR + PAIR)
        qn_s[h // 2, pl.ds(own * blk, blk), :] = jnp.where(mine, q[:, pair], jnp.zeros((), bf16))
        dn_s[h // 2, pl.ds(own * blk, blk), :] = jnp.where(mine, do_ref[:, pair], jnp.zeros((), bf16))
        dl_s[h:h + 1, :] = jnp.sum(prod[rows, :], axis=0, keepdims=True)
    acc_s[...] = jnp.zeros_like(acc_s)
    lowest = lo_ref[...]

    def step(kb, masked):
        at = pl.multiple_of(kb * blk, blk)
        if masked:
            ok = allowed(lowest, kb, qb, blk)
        for g in range(nh // 2):
            lanes = pl.ds(g * PAIR, PAIR)
            for own in range(2):
                h = 2 * g + own
                rows = pl.ds(h * HEAD_DIM, HEAD_DIM)
                s = jnp.dot(k_s[pl.ds(at, blk), lanes], qm_s[h], preferred_element_type=f32) * (LOG2E * scale)
                p = jnp.exp2(s - lse_ref[h:h + 1, :])
                if masked:
                    p = jnp.where(ok, p, 0.0)
                dp = jnp.dot(v_s[pl.ds(at, blk), lanes], dm_s[h], preferred_element_type=f32)
                ds = (p * (dp - dl_s[h:h + 1, :])).astype(bf16)
                p_s[g, :, pl.ds(own * blk, blk)] = p.astype(bf16)
                ds_s[g, :, pl.ds(own * blk, blk)] = ds
                acc_s[rows, :] += jnp.dot(kT_ref[rows, pl.ds(at, blk)], ds, preferred_element_type=f32)
            dv_s[pl.ds(at, blk), lanes] += jnp.dot(p_s[g], dn_s[g], preferred_element_type=f32)
            dk_s[pl.ds(at, blk), lanes] += jnp.dot(ds_s[g], qn_s[g], preferred_element_type=f32)

    walk(span_ref, qb, step)

    def turned_back(values, at, size, kind):
        cosine = table_ref[2 * kind, :, pl.ds(at, size)] * scale
        sine = table_ref[2 * kind + 1, :, pl.ds(at, size)] * scale
        out = []
        for h in range(nh):
            one = values[h * HEAD_DIM:h * HEAD_DIM + HALF]
            two = values[h * HEAD_DIM + HALF:(h + 1) * HEAD_DIM]
            out += [one * cosine + two * sine, two * cosine - one * sine]
        return jnp.concatenate(out, axis=0).T.astype(bf16)

    spots = blk // (2 * unit)
    for u in range(spots):
        dst = pl.multiple_of(((qb * spots + u) ^ place) * unit, unit)
        for half, ref in ((0, d0_ref), (1, d1_ref)):
            at = pl.multiple_of((2 * u + (core ^ half)) * unit, unit)
            ref[pl.ds(dst, unit), pl.ds(0, dim)] = turned_back(
                acc_s[:, pl.ds(at, unit)], pl.multiple_of(qb * blk + at, unit), unit, 0)

    @pl.when(qb == count - 1)
    def _():
        def store(j, carry):
            dst = pl.multiple_of((j ^ place) * unit, unit)
            for half, ref in ((0, d0_ref), (1, d1_ref)):
                at = pl.multiple_of((2 * j + (core ^ half)) * unit, unit)
                ref[pl.ds(dst, unit), pl.ds(dim, dim)] = turned_back(dk_s[pl.ds(at, unit), :].T, at, unit, 1)
                ref[pl.ds(dst, unit), pl.ds(2 * dim, dim)] = dv_s[pl.ds(at, unit), :].astype(bf16)
            return carry

        lax.fori_loop(0, length // (2 * unit), store, 0)


PARAMS = pltpu.CompilerParams(dimension_semantics=("arbitrary",), vmem_limit_bytes=60 * 2**20)


def span_of(lowest, blk, core, place):
    count = lowest.shape[0] // blk
    blocks = lowest.reshape(count, blk)
    own = jnp.arange(count, dtype=jnp.int32)
    first = jnp.minimum(blocks[:, 0] // blk, own)
    clear = jnp.minimum((blocks[:, -1] + blk - 1) // blk, own)
    both = jnp.stack([first, clear], axis=-1).reshape(-1)
    return jnp.concatenate([jnp.stack([core, place]), both]).astype(jnp.int32)


def attention_forward(row, half0, half1, table, lowest, span, blk, unit):
    length = lowest.shape[0]
    dim = half0.shape[0] // 3
    nh, count = dim // HEAD_DIM, length // blk
    spots = blk // (2 * unit)
    sds = jax.ShapeDtypeStruct
    pick = pl.BlockSpec((dim, blk // 2), lambda q, s: (0, row * count + (q ^ lax.div(s[1], spots))))
    keys = pl.BlockSpec((dim, length // 2), lambda q, s: (1, row))
    values = pl.BlockSpec((dim, length // 2), lambda q, s: (2, row))
    wide = pl.BlockSpec((dim, length), lambda q, s: (0, 0))
    cut = pl.BlockSpec((dim, blk), lambda q, s: (0, q))
    return pl.pallas_call(
        functools.partial(forward_kernel, nh, blk, unit),
        out_shape=(sds((length, dim), bf16), sds((dim, length), f32), sds((nh, length), f32),
                   sds((dim, length), bf16), sds((dim, length), bf16), sds((dim, length), bf16)),
        grid_spec=pltpu.PrefetchScalarGridSpec(
            num_scalar_prefetch=1, grid=(count,),
            in_specs=[pick, pick, keys, keys, values, values,
                      pl.BlockSpec((4, HALF, length), lambda q, s: (0, 0, 0)),
                      pl.BlockSpec((1, blk), lambda q, s: (0, q))],
            out_specs=[pl.BlockSpec((blk, dim), lambda q, s: (q, 0)), cut,
                       pl.BlockSpec((nh, blk), lambda q, s: (0, q)), cut, wide, wide],
            scratch_shapes=[pltpu.VMEM((length, dim), bf16), pltpu.VMEM((nh, PAIR, blk), bf16), pltpu.VMEM((dim, blk), f32),
                            pltpu.VMEM((8, blk), f32), pltpu.VMEM((8, blk), f32)]),
        compiler_params=PARAMS, name="attention_forward",
        cost_estimate=pl.CostEstimate(flops=4 * 4 * dim * length * length // 2, bytes_accessed=10 * 2**20,
                                      transcendentals=nh * length * length // 2),
    )(span, half0, half1, half0, half1, half0, half1, table, lowest[None, :])


def attention_backward(row, rows, saved, do, table, lowest, span, blk, unit, before):
    oT, lse, qT, kT, vT = saved
    length = lowest.shape[0]
    dim = qT.shape[0]
    nh, count = dim // HEAD_DIM, length // blk
    sds = jax.ShapeDtypeStruct
    cut = pl.BlockSpec((dim, blk), lambda q, s: (0, q))
    wide = pl.BlockSpec((dim, length), lambda q, s: (0, 0))
    grad = pl.BlockSpec((length // 2, 3 * dim), lambda q, s: (row, 0))
    whole = sds((rows * length // 2, 3 * dim), bf16)
    kernel = functools.partial(backward_kernel, nh, blk, unit)
    if before is None:
        def call(span_ref, *refs):
            kernel(span_ref, *refs[:8], None, None, *refs[8:])
    else:
        call = kernel
    return pl.pallas_call(
        call,
        out_shape=(whole, whole),
        grid_spec=pltpu.PrefetchScalarGridSpec(
            num_scalar_prefetch=1, grid=(count,),
            in_specs=[cut, wide, wide, pl.BlockSpec((blk, dim), lambda q, s: (q, 0)), cut,
                      pl.BlockSpec((nh, blk), lambda q, s: (0, q)),
                      pl.BlockSpec((4, HALF, length), lambda q, s: (0, 0, 0)),
                      pl.BlockSpec((1, blk), lambda q, s: (0, q))]
            + ([] if before is None else [pl.BlockSpec(memory_space=pl.ANY)] * 2),
            out_specs=[grad, grad],
            scratch_shapes=[pltpu.VMEM((length, dim), bf16), pltpu.VMEM((length, dim), bf16),
                            pltpu.VMEM((nh, PAIR, blk), bf16), pltpu.VMEM((nh, PAIR, blk), bf16),
                            pltpu.VMEM((nh // 2, 2 * blk, PAIR), bf16), pltpu.VMEM((nh // 2, 2 * blk, PAIR), bf16),
                            pltpu.VMEM((dim, blk), f32), pltpu.VMEM((length, dim), f32), pltpu.VMEM((length, dim), f32),
                            pltpu.VMEM((nh // 2, blk, 2 * blk), bf16), pltpu.VMEM((nh // 2, blk, 2 * blk), bf16),
                            pltpu.VMEM((8, blk), f32)]),
        compiler_params=PARAMS, name="attention_backward",
        input_output_aliases={} if before is None else {9: 0, 10: 1},
        cost_estimate=pl.CostEstimate(flops=10 * 4 * dim * length * length // 2, bytes_accessed=20 * 2**20,
                                      transcendentals=nh * length * length // 2),
    )(span, qT, kT, vT, do, oT, lse, table, lowest[None, :], *(before or ()))


def hat_of(values):
    center = values - jnp.mean(values, axis=-1, keepdims=True)
    rstd = lax.rsqrt(jnp.mean(center * center, axis=-1, keepdims=True) + EPS)
    return center * rstd, rstd


def hat_back(hat, rstd, grad):
    return rstd * (grad - jnp.mean(grad, axis=-1, keepdims=True) - hat * jnp.mean(grad * hat, axis=-1, keepdims=True))


def wide_row(o_ref):
    return jnp.concatenate([o_ref[i] for i in range(o_ref.shape[0])], axis=1).astype(f32)


def middle_forward_kernel(o_ref, x_ref, w_ref, c_ref, x1_ref, b_ref):
    c = hat_of(wide_row(o_ref))[0].astype(bf16)
    c_ref[...] = c
    x1 = x_ref[...].astype(f32) + jnp.dot(c, w_ref[...], preferred_element_type=f32)
    x1_ref[...] = x1
    b_ref[...] = hat_of(x1)[0].astype(bf16)


def middle_forward(o, x, w):
    n, size, dim = o.shape
    width = n * dim
    step = min(128, size)
    sds = jax.ShapeDtypeStruct
    flat = pl.BlockSpec((step, width), lambda t: (t, 0))
    return pl.pallas_call(
        middle_forward_kernel,
        out_shape=(sds((size, width), bf16), sds((size, width), f32), sds((size, width), bf16)),
        grid=(size // step,),
        in_specs=[pl.BlockSpec((n, step, dim), lambda t: (0, t, 0)), flat,
                  pl.BlockSpec((width, width), lambda t: (0, 0))],
        out_specs=(flat, flat, flat),
        compiler_params=PARAMS, name="middle_forward",
        cost_estimate=pl.CostEstimate(flops=2 * size * width * width, bytes_accessed=14 * 2**20, transcendentals=0),
    )(o, x, w)


def middle_backward_kernel(o_ref, x1_ref, db_ref, dy_ref, w_ref, dx_ref, low_ref, do_ref):
    hat, rstd = hat_of(x1_ref[...])
    dx1 = dy_ref[...].astype(f32) + hat_back(hat, rstd, db_ref[...])
    dx_ref[...] = dx1
    low_ref[...] = dx1.astype(bf16)
    dc = times_rows(dx1.astype(bf16), w_ref[...])
    hat, rstd = hat_of(wide_row(o_ref))
    d_o = hat_back(hat, rstd, dc).astype(bf16)
    dim = do_ref.shape[2]
    for i in range(do_ref.shape[0]):
        do_ref[i] = d_o[:, i * dim:(i + 1) * dim]


def middle_backward(row, o, x1, db, dy, w):
    n, size, dim = o.shape
    width = n * dim
    step = min(128, size)
    sds = jax.ShapeDtypeStruct
    flat = pl.BlockSpec((step, width), lambda t: (t, 0))
    part = pl.BlockSpec((n, step, dim), lambda t: (0, t, 0))
    return pl.pallas_call(
        middle_backward_kernel,
        out_shape=(sds((size, width), f32), sds((size, width), bf16), sds((n, size, dim), bf16)),
        grid=(size // step,),
        in_specs=[part, flat, pl.BlockSpec((step, width), lambda t: (row * (size // step) + t, 0)), flat,
                  pl.BlockSpec((width, width), lambda t: (0, 0))],
        out_specs=(flat, flat, part),
        compiler_params=PARAMS, name="middle_backward",
        cost_estimate=pl.CostEstimate(flops=2 * size * width * width, bytes_accessed=16 * 2**20, transcendentals=0),
    )(o, x1, db, dy, w)


def ways(row, n):
    bits = [1 << k for k in range(1, n.bit_length() - 1)]
    return bits if row % 2 == 0 else bits[::-1]


def times_rows(a, w):
    return lax.dot_general(a, w, (((1,), (1,)), ((), ())), preferred_element_type=f32)


def weight_copies(all_ref, kind, dst_ref, sems, first=0):
    m, lines, ff = all_ref.shape
    unit = ff // m
    pieces = dst_ref.shape[1 if kind == "down" else 0] // ff
    depth = lines - unit * pieces
    copies = []
    for r in range(m):
        if kind == "up":
            moves = [(all_ref.at[r, pl.ds(0, depth), :], dst_ref.at[pl.ds(r * depth, depth), :])]
        else:
            moves = [(all_ref.at[r, pl.ds(depth + q * unit, unit), :],
                      dst_ref.at[pl.ds(r * unit, unit), pl.ds(q * ff, ff)]) for q in range(pieces)]
        for src, dst in moves:
            copies.append(pltpu.make_async_copy(src, dst, sems.at[first + len(copies)]))
    for copy in copies:
        copy.start()
    return copies


def product_sum_kernel(n, rows, cols, turned, kind, x0_ref, x1_ref, w_ref, o_ref, part_s, core_s, sum_s, got_s, send_sem, recv_sem,
                       *own_w):
    mine = lax.axis_index("ctx")
    loads = []
    if kind:
        loads = weight_copies(w_ref, kind, *own_w)
        w_ref = own_w[0]
    spots = n // 2
    size = x0_ref.shape[0] // (rows * spots)
    width = o_ref.shape[1]
    barrier = pltpu.get_barrier_semaphore()
    bits = [1] + ways(0, n)
    for bit in bits:
        pl.semaphore_signal(barrier, inc=1, device_id={"ctx": mine ^ bit}, device_id_type=pl.DeviceIdType.MESH)
    pl.semaphore_wait(barrier, len(bits))
    for copy in loads:
        copy.wait()
    copies = []

    def send(src, dst, bit):
        at = len(copies)
        copy = pltpu.make_async_remote_copy(
            src_ref=src, dst_ref=dst, send_sem=send_sem.at[at], recv_sem=recv_sem.at[at],
            device_id={"ctx": mine ^ bit}, device_id_type=pl.DeviceIdType.MESH)
        copy.start()
        copies.append(copy)
        return copy

    def key(row, k):
        return [-(k & (bit >> 1)) for bit in ways(row, n)]

    orders = []
    for r in range(rows):
        way = [bit >> 1 for bit in ways(r, n)]
        orders.append(sorted(range(spots), key=lambda k: [0 if k & bit else 1 for bit in way]))
    todo = [(r, orders[r][t]) for t in range(spots) for r in range(rows)]
    inbox, slot, slots = {}, {}, 0

    def product(x_ref, r, k, finish):
        begin = (r * spots + k) * size

        @pl.loop(0, width // cols)
        def _(c):
            at = pl.ds(pl.multiple_of(c * cols, cols), cols)
            x = x_ref[pl.ds(begin, size), :]
            finish(at, times_rows(x, w_ref[at, :]) if turned else jnp.dot(x, w_ref[:, at], preferred_element_type=f32))

    def pair(r, k):
        spot = r * spots + k

        def keep(at, value):
            part_s[spot, :, at] = value.astype(bf16)

        product(x1_ref, r, k, keep)
        inbox[r, k] = send(part_s.at[spot], core_s.at[spot], 1)

    def own(r, k):
        spot = r * spots + k
        inbox[r, k].wait_recv()

        def add(at, value):
            sum_s[spot, :, at] = (value + core_s[spot, :, at].astype(f32)).astype(bf16)

        product(x0_ref, r, k, add)

    def pass_on(r, k, stage):
        nonlocal slots
        bit = ways(r, n)[stage]
        if k & (bit >> 1):
            inbox[r, k ^ (bit >> 1), stage] = (send(sum_s.at[r * spots + k], got_s.at[slots], bit), slots)
            slots += 1

    group = max(rows * spots // 2, 1)
    for begin in range(0, len(todo), group):
        for r, k in todo[begin:begin + group]:
            pair(r, k)
        for r, k in todo[begin:begin + group]:
            own(r, k)
            pass_on(r, k, 0)
    stages = len(bits) - 1
    for stage in range(stages):
        for r, k in todo:
            way = [bit >> 1 for bit in ways(r, n)]
            if any(k & bit for bit in way[:stage + 1]):
                continue
            copy, at = inbox[r, k, stage]
            copy.wait_recv()
            spot = r * spots + k
            if stage == stages - 1:
                o_ref[pl.ds(r * size, size), :] = sum_s[spot].astype(f32) + got_s[at].astype(f32)
            else:
                sum_s[spot] = (sum_s[spot].astype(f32) + got_s[at].astype(f32)).astype(bf16)
                pass_on(r, k, stage + 1)
    for copy in copies:
        copy.wait_send()


def product_sum(x0, x1, w, rows, n, collective_id, turned=False, kind=None, wide=None):
    size = x0.shape[0] // (rows * (n // 2))
    depth = x0.shape[1]
    width = wide if kind else w.shape[0 if turned else 1]
    count = rows * (n // 2)
    moves = count + rows * (n // 2 - 1)
    vmem = pl.BlockSpec(memory_space=pltpu.VMEM)
    flops = 4 * x0.shape[0] * x0.shape[1] * width
    return pl.pallas_call(
        functools.partial(product_sum_kernel, n, rows, min(512, width), turned, kind),
        out_shape=jax.ShapeDtypeStruct((rows * size, width), f32),
        in_specs=[vmem, vmem, pl.BlockSpec(memory_space=pl.ANY) if kind else vmem], out_specs=vmem,
        scratch_shapes=[pltpu.VMEM((count, size, width), bf16), pltpu.VMEM((count, size, width), bf16),
                        pltpu.VMEM((count, size, width), bf16), pltpu.VMEM((moves - count, size, width), bf16),
                        pltpu.SemaphoreType.DMA((moves,)), pltpu.SemaphoreType.DMA((moves,))]
        + ([pltpu.VMEM((width, depth) if turned else (depth, width), bf16), pltpu.SemaphoreType.DMA((64,))] if kind else []),
        compiler_params=pltpu.CompilerParams(collective_id=collective_id, has_side_effects=True, vmem_limit_bytes=60 * 2**20),
        name="product_sum",
        cost_estimate=pl.CostEstimate(flops=4 * flops, bytes_accessed=20 * 2**20, transcendentals=0),
    )(x0, x1, w)


def gather_product_kernel(n, rows, cols, b_ref, dy0_ref, dy1_ref, w_ref, b0_ref, b1_ref, h0_ref, h1_ref, d0_ref, d1_ref,
                          stat_ref, up_ref, down_ref, got_s, d_s, h_s, dy_s, w_sem, send_sem, recv_sem, dy_sem, b_sem, h_sem, d_sem):
    mine = lax.axis_index("ctx")
    spots = n // 2
    size = b_ref.shape[0] // rows
    ff = up_ref.shape[1]
    loads = weight_copies(w_ref, "down", down_ref, w_sem)
    loads_up = weight_copies(w_ref, "up", up_ref, w_sem, len(loads))
    count = rows * spots
    barrier = pltpu.get_barrier_semaphore()
    bits = [1] + ways(0, n)
    for bit in bits:
        pl.semaphore_signal(barrier, inc=1, device_id={"ctx": mine ^ bit}, device_id_type=pl.DeviceIdType.MESH)
    pl.semaphore_wait(barrier, len(bits))
    sends, locals_, arrival = [], [], {}

    def send(src, half, row, k, bit):
        at, to = len(sends), half * count + row * spots + k
        copy = pltpu.make_async_remote_copy(
            src_ref=src, dst_ref=got_s.at[to], send_sem=send_sem.at[at], recv_sem=recv_sem.at[at],
            device_id={"ctx": mine ^ bit}, device_id_type=pl.DeviceIdType.MESH)
        copy.start()
        sends.append(copy)
        arrival[half, row, k] = copy

    def held(half, row, k):
        if half == 0 and k == 0:
            return b_ref.at[pl.ds(row * size, size), :]
        return got_s.at[half * count + row * spots + k]

    def onward(row, k):
        way = ways(row, n)
        top = max([s for s, bit in enumerate(way) if k & (bit >> 1)], default=-1)
        for bit in way[top + 1:]:
            send(held(0, row, k), 0, row, k | (bit >> 1), bit)
        send(held(0, row, k), 1, row, k, 1)

    for r in range(rows):
        onward(r, 0)

    def fetch(t, slot):
        begin = pl.multiple_of(lax.rem(t, count) * size, size)

        @pl.when(t < count)
        def _():
            pltpu.make_async_copy(dy0_ref.at[pl.ds(begin, size), :], dy_s.at[slot], dy_sem.at[slot]).start()

        @pl.when(t >= count)
        def _():
            pltpu.make_async_copy(dy1_ref.at[pl.ds(begin, size), :], dy_s.at[slot], dy_sem.at[slot]).start()

    fetch(0, 0)
    for copy in loads:
        copy.wait()

    @pl.loop(0, 2 * count)
    def _(t):
        slot = lax.rem(t, 2)

        @pl.when(t + 1 < 2 * count)
        def _():
            fetch(t + 1, 1 - slot)

        pltpu.make_async_copy(dy0_ref.at[pl.ds(0, size), :], dy_s.at[slot], dy_sem.at[slot]).wait()

        @pl.loop(0, ff // cols)
        def _(c):
            at = pl.ds(pl.multiple_of(c * cols, cols), cols)
            d_s[t, :, at] = times_rows(dy_s[slot], down_ref[at, :])

    for t in range(2 * count):
        dst = (d0_ref, d1_ref)[t // count].at[pl.ds((t % count) * size, size), :]
        copy = pltpu.make_async_copy(d_s.at[t], dst, d_sem.at[t])
        copy.start()
        locals_.append(copy)

    for copy in loads_up:
        copy.wait()
    outs = []
    lane = lax.broadcasted_iota(jnp.int32, (32, 128), 1)

    def block(half, row, k):
        t = half * count + row * spots + k
        src = held(half, row, k)
        copy = pltpu.make_async_copy(src, (b0_ref, b1_ref)[half].at[pl.ds((t % count) * size, size), :], b_sem.at[t])
        copy.start()
        locals_.append(copy)
        slot = len(outs) % 2
        if len(outs) >= 2:
            outs[-2].wait()

        @pl.loop(0, ff // cols)
        def _(c):
            at = pl.ds(pl.multiple_of(c * cols, cols), cols)
            h_s[slot, :, at] = jnp.dot(src[...], up_ref[:, at], preferred_element_type=f32)

        copy = pltpu.make_async_copy(h_s.at[slot], (h0_ref, h1_ref)[half].at[pl.ds((t % count) * size, size), :], h_sem.at[t])
        copy.start()
        outs.append(copy)

        @pl.loop(0, size // 32)
        def _(c):
            at = pl.ds(pl.multiple_of(c * 32, 32), 32)
            h = h_s[slot, at, :]
            gel = h * (0.5 * (1.0 + lax.erf(h * (2.0**-0.5))))
            d = d_s[t, at, :]
            mean = jnp.mean(gel, axis=-1, keepdims=True)
            off = gel - mean
            spread = jnp.sum(off * off, axis=-1, keepdims=True)
            total = jnp.sum(d, axis=-1, keepdims=True)
            cross = jnp.sum(d * off, axis=-1, keepdims=True)
            line = jnp.where(lane == 0, mean, jnp.where(lane == 1, spread, jnp.where(lane == 2, total, cross)))
            stat_ref[pl.ds(pl.multiple_of(t * size + c * 32, 32), 32), :] = line

    order = []
    for k in range(spots):
        for r in range(rows):
            way = ways(r, n)
            order.append((r, sum((bit >> 1) for s, bit in enumerate(way) if k >> s & 1)))
    for begin in range(0, len(order), rows):
        some = order[begin:begin + rows]
        for r, k in some:
            if k:
                arrival[0, r, k].wait_recv()
                onward(r, k)
        for r, k in some:
            block(0, r, k)
        for r, k in some:
            arrival[1, r, k].wait_recv()
            block(1, r, k)
    for copy in outs[-2:] + locals_:
        copy.wait()
    for copy in sends:
        copy.wait_send()


def gather_product(b, dy0, dy1, weights, rows, n, collective_id):
    size = b.shape[0] // rows
    width, ff = b.shape[1], weights.shape[2]
    count = rows * (n // 2)
    half = count * size
    moves = rows * (n - 1)
    vmem, here = pl.BlockSpec(memory_space=pltpu.VMEM), pl.BlockSpec(memory_space=pl.ANY)
    sds = jax.ShapeDtypeStruct
    return pl.pallas_call(
        functools.partial(gather_product_kernel, n, rows, min(256, ff)),
        out_shape=(sds((half, width), bf16),) * 2 + (sds((half, ff), f32),) * 4 + (sds((2 * half, 128), f32),),
        in_specs=[vmem, here, here, here], out_specs=(here,) * 6 + (vmem,),
        scratch_shapes=[pltpu.VMEM((width, ff), bf16), pltpu.VMEM((ff, width), bf16),
                        pltpu.VMEM((2 * count, size, width), bf16), pltpu.VMEM((2 * count, size, ff), f32),
                        pltpu.VMEM((2, size, ff), f32), pltpu.VMEM((2, size, width), bf16), pltpu.SemaphoreType.DMA((64,)),
                        pltpu.SemaphoreType.DMA((moves,)), pltpu.SemaphoreType.DMA((moves,)), pltpu.SemaphoreType.DMA((2,))]
        + [pltpu.SemaphoreType.DMA((2 * count,))] * 3,
        compiler_params=pltpu.CompilerParams(collective_id=collective_id, has_side_effects=True, vmem_limit_bytes=62 * 2**20),
        name="gather_product",
        cost_estimate=pl.CostEstimate(flops=16 * half * width * ff, bytes_accessed=70 * 2**20, transcendentals=0),
    )(b, dy0, dy1, weights)


def standardize(values):
    center = values - jnp.mean(values, axis=-1, keepdims=True)
    spread = jnp.mean(center * center, axis=-1, keepdims=True)
    rstd = lax.rsqrt(spread + EPS)
    return center * rstd, rstd


def standardize_back(hat, rstd, grad):
    return rstd * (grad - jnp.mean(grad, axis=-1, keepdims=True) - hat * jnp.mean(grad * hat, axis=-1, keepdims=True))


def row_places(lengths, row_len):
    places = jnp.arange(row_len, dtype=jnp.int32)
    ends = jnp.cumsum(lengths, axis=-1)
    passed = ends[:, None, :] <= places[None, :, None]
    starts = jnp.sum(jnp.where(passed, lengths[:, None, :], 0), axis=-1)
    valid = places[None, :] < ends[:, -1:]
    lowest = jnp.where(valid, starts, places[None, :]).astype(jnp.int32)
    return (places[None, :] - starts).astype(f32), lowest


def xpos_tables(relative):
    ladder = jnp.arange(HALF, dtype=f32) / HALF
    rate = jnp.power(10000.0, -ladder)
    base = (ladder + 0.4) / 1.4
    angles = rate[None, :, None] * relative[:, None, :]
    power = (relative[:, None, :] - ROW_LEN / 2) / XPOS_BASE
    factor = jnp.power(base[None, :, None], power)
    cosine, sine = jnp.cos(angles), jnp.sin(angles)
    return jnp.stack([cosine * factor, sine * factor, cosine / factor, sine / factor], axis=1)


def dot(a, b, spec, kind=f32):
    return jnp.einsum(spec, a, b, preferred_element_type=f32).astype(kind)


def swap(x, bit):
    n = lax.axis_size("ctx")
    return lax.ppermute(x, "ctx", [(i, i ^ bit) for i in range(n)])


def exchange(blocks):
    n = lax.axis_size("ctx")
    mine = lax.axis_index("ctx")
    out = jnp.zeros_like(blocks)
    for bit in range(n):
        block = lax.dynamic_index_in_dim(blocks, mine ^ bit, 0, False)
        block = swap(block, bit) if bit else block
        out = lax.dynamic_update_index_in_dim(out, block, mine ^ bit, 0)
    return out


def after(x, *others):
    return lax.optimization_barrier((x, *others))[0]


def gather_start(x):
    return [{0: x[r]} for r in range(x.shape[0])]


def gather_step(held, step):
    n = lax.axis_size("ctx")
    out = []
    for r, parts in enumerate(held):
        bit = ways(r, n)[step]
        out.append({**parts, **{k | bit: swap(v, bit) for k, v in parts.items()}})
    return out


def gather_own(held, step):
    n = lax.axis_size("ctx")
    out = []
    for r, parts in enumerate(held):
        bit = ways(r, n)[step]
        out.append({**parts, bit: swap(parts[0], bit)})
    return out


def gather_rest(held, step):
    n = lax.axis_size("ctx")
    out = []
    for r, parts in enumerate(held):
        bit = ways(r, n)[step]
        moved = {k | bit: swap(v, bit) for k, v in parts.items() if k and not k & bit}
        out.append({**parts, **moved})
    return out


def gather_steps():
    return lax.axis_size("ctx").bit_length() - 2


def gather_end(held):
    return jnp.concatenate([parts[k] for parts in held for k in sorted(parts)], axis=0)


def gather_half(x):
    held = gather_start(x)
    for step in range(gather_steps()):
        held = gather_step(held, step)
    return gather_end(held)


def plus(a, b, kind=bf16):
    return (a.astype(f32) + b.astype(f32)).astype(kind)


def reduce_start(half0, half1, rows):
    n = lax.axis_size("ctx")
    width = half0.shape[-1]
    both = plus(half0, swap(half1, 1)).reshape(rows, n // 2, -1, width)
    return [{2 * k: both[r, k] for k in range(n // 2)} for r in range(rows)]


def reduce_step(held, step):
    n = lax.axis_size("ctx")
    out = []
    for r, parts in enumerate(held):
        bit = ways(r, n)[step]
        kind = bf16 if len(parts) > 2 else f32
        out.append({k: plus(v, swap(parts[k | bit], bit), kind) for k, v in parts.items() if not k & bit})
    return out


def reduce_end(held):
    return jnp.concatenate([parts[0] for parts in held], axis=0)


def reduce_halves(half0, half1, rows):
    held = reduce_start(half0, half1, rows)
    for step in range(gather_steps()):
        held = reduce_step(held, step)
    return reduce_end(held)


def body(inputs, doc_len, w_query, w_key, w_value, w_out, w_up, w_down, gain_attn, gain_attn_sub, gain_ffn,
         gain_ffn_sub, out_cotangent):
    rows, local_len, width = inputs.shape
    n, m = lax.axis_size("ctx"), lax.axis_size("row")
    row_len = local_len * n
    tokens, half = rows * local_len, rows * row_len // 2
    piece = w_query.shape[0]
    heads_dim = width // n
    ff = w_up.shape[1]
    unit = ff // (n * m)
    ff_dev = unit * m
    blk = min(512, row_len)
    mine = lax.axis_index("ctx")
    core, place = mine & 1, mine >> 1

    def scaled(w, gain):
        return (w.astype(f32) * gain.astype(f32)[:, None]).astype(bf16)

    x_own = inputs.reshape(tokens, width).astype(f32)
    x_hat, x_rstd = standardize(x_own)
    x_low = x_hat.astype(bf16)
    x_held = gather_step(gather_start(x_low.reshape(rows, local_len, width)), 0)

    qkv_local = jnp.concatenate(
        [scaled(w, gain_attn).reshape(piece, n, heads_dim) for w in (w_query, w_key, w_value)], axis=2)
    qkv_part = exchange(qkv_local.transpose(1, 0, 2)).reshape(n * piece, 3 * heads_dim)
    w_qkv = lax.all_gather(qkv_part, "row", axis=0, tiled=True)
    up_local = scaled(after(w_up, qkv_part), gain_ffn).reshape(piece, m, n, unit).transpose(2, 0, 1, 3).reshape(n, piece, ff_dev)
    up_part = lax.all_to_all(up_local, "ctx", split_axis=0, concat_axis=0, tiled=True).reshape(n * piece, ff_dev)
    for step in range(1, gather_steps()):
        x_held = gather_step(x_held, step)
    xh0 = gather_end(x_held)
    xh0, up_part = lax.optimization_barrier((xh0, up_part))
    xh1 = swap(xh0, 1)
    down_local = scaled(w_down, gain_ffn_sub)
    ffn_local = jnp.concatenate([up_part] + [down_local[:, q:q + ff_dev] for q in range(0, width, ff_dev)], axis=0)
    out_all = lax.all_gather(scaled(w_out, gain_attn_sub), BOTH, axis=0, tiled=True)

    relative, lowest = row_places(doc_len, row_len)
    table = xpos_tables(relative)
    span = [span_of(lowest[r], blk, core, place) for r in range(rows)]
    qkv0 = dot(w_qkv, xh0, "df,td->ft")
    qkv1 = dot(w_qkv, xh1, "df,td->ft")
    qkv0, qkv1, cot = lax.optimization_barrier((qkv0, qkv1, out_cotangent))
    dy_held = gather_step(gather_start(cot), 0)
    dy_steps = gather_steps()
    saved, o = [], []
    for r in range(rows):
        o_row, *kept = attention_forward(r, qkv0, qkv1, table[r], lowest[r], span[r], blk, local_len)
        if r == 0:
            o_row, kept, qkv0, qkv1, dy_held, out_all = lax.optimization_barrier((o_row, kept, qkv0, qkv1, dy_held, out_all))
            ffn_all = lax.all_gather(after(ffn_local, out_all), "row", axis=0, tiled=False)
            dy_held = gather_own(dy_held, 1)
        if r == rows - 1:
            o_row, o, dy_held = lax.optimization_barrier((o_row, o, dy_held))
            dy_held = gather_rest(dy_held, 1)
            for step in range(2, dy_steps):
                dy_held = gather_step(dy_held, step)
        saved.append(kept)
        o.append(lax.all_to_all(o_row.reshape(n, local_len, heads_dim), "ctx", split_axis=0, concat_axis=0, tiled=True))
    c, x1, b_low = zip(*[middle_forward(o[r], inputs[r], out_all) for r in range(rows)])
    b_low, dy_held = lax.optimization_barrier((b_low, dy_held))
    dy0 = gather_end(dy_held)
    dy1 = swap(dy0, 1)

    b0, b1, h0, h1, d_hat0, d_hat1, stats = gather_product(jnp.concatenate(b_low), dy0, dy1, ffn_all, rows, n, 4)
    stats = stats[:, :4].T
    order = jnp.arange(n // 2, dtype=jnp.int32) ^ place
    halves = jnp.arange(2, dtype=jnp.int32) ^ core

    def reorder(v):
        v = v.reshape(v.shape[0], 2, rows, n // 2, local_len)
        return jnp.take(jnp.take(v, halves, axis=1), order, axis=3).reshape(v.shape[0], 2 * half)

    stats = lax.all_gather(reorder(stats), "ctx", axis=0, tiled=False)
    mean = jnp.mean(stats[:, 0], axis=0)
    shift = stats[:, 0] - mean
    var = (jnp.sum(stats[:, 1], axis=0) + ff_dev * jnp.sum(shift * shift, axis=0)) / ff
    rstd = lax.rsqrt(var + EPS)
    d_mean = jnp.sum(stats[:, 2], axis=0) / ff
    d_corr = rstd * jnp.sum(stats[:, 3] + stats[:, 2] * shift, axis=0) / ff
    merged = reorder(jnp.stack([mean, rstd, d_mean, d_corr])).reshape(4, 2, half, 1)

    def finish(h, d_hat, which):
        cdf = 0.5 * (1.0 + lax.erf(h * (2.0**-0.5)))
        mean, rstd, d_mean, d_corr = (merged[k, which] for k in range(4))
        hat = (h * cdf - mean) * rstd
        d_gel = rstd * (d_hat - d_mean - hat * d_corr)
        pdf = jnp.exp(-0.5 * h * h) * 0.3989422804014327
        return hat.astype(bf16), (d_gel * (cdf + h * pdf)).astype(bf16)

    e0, dh0 = finish(h0, d_hat0, 0)
    e1, dh1 = finish(h1, d_hat1, 1)
    down_part = (dot(e0, dy0, "tf,td->fd") + dot(e1, dy1, "tf,td->fd")).astype(bf16)
    up_part = (dot(b0, dh0, "td,tf->df") + dot(b1, dh1, "td,tf->df")).astype(bf16)
    e0, e1, dh0, dh1, down_part, up_part = lax.optimization_barrier((e0, e1, dh0, dh1, down_part, up_part))
    down_sum = lax.psum_scatter(down_part, "row", scatter_dimension=0, tiled=True)
    db = product_sum(dh0, dh1, ffn_all, rows, n, 1, True, "up", width)
    db, up_part, down_sum = lax.optimization_barrier((db, up_part, down_sum))
    down_raw = down_sum.astype(f32)
    up_sum = lax.psum_scatter(up_part, "row", scatter_dimension=0, tiled=True)

    dx1, dx1b, d_o = zip(*[middle_backward(r, o[r], x1[r], db, out_cotangent[r], out_all) for r in range(rows)])
    do_heads = [lax.all_to_all(v, "ctx", split_axis=0, concat_axis=0, tiled=True).reshape(row_len, heads_dim) for v in d_o]
    c_order = jnp.concatenate(c).reshape(tokens, m, n, piece).transpose(0, 2, 1, 3).reshape(tokens, width)
    out_part = dot(c_order, jnp.concatenate(dx1b), "td,te->de", bf16)
    do_heads[0], out_part = lax.optimization_barrier((do_heads[0], out_part))
    grads = attention_backward(0, rows, saved[0], do_heads[0], table[0], lowest[0], span[0], blk, local_len, None)
    grads, do_heads, up_sum, out_part = lax.optimization_barrier((grads, do_heads, up_sum, out_part))
    out_part = lax.psum_scatter(out_part, "ctx", scatter_dimension=0, tiled=True)
    up_moved = lax.all_to_all(up_sum.reshape(n, piece, ff_dev), "ctx", split_axis=0, concat_axis=2, tiled=True)
    for r in range(1, rows):
        grads = attention_backward(r, rows, saved[r], do_heads[r], table[r], lowest[r], span[r], blk, local_len, grads)
    d0, d1 = grads
    qkv_part = (dot(xh0, d0, "td,tf->df") + dot(xh1, d1, "td,tf->df")).astype(bf16)
    d0, d1, qkv_part, out_part, up_moved = lax.optimization_barrier((d0, d1, qkv_part, out_part, up_moved))
    qkv_part = lax.psum_scatter(qkv_part, "row", scatter_dimension=0, tiled=True)
    da = product_sum(d0, d1, w_qkv, rows, n, 2, True)
    e0, e1, da, qkv_part, out_part = lax.optimization_barrier((e0, e1, da, qkv_part, out_part))
    out_raw = lax.psum_scatter(out_part, "row", scatter_dimension=0, tiled=True).astype(f32)
    up_raw = up_moved.reshape(piece, n, m, unit).transpose(0, 2, 1, 3).reshape(piece, ff).astype(f32)
    qkv_raw = lax.all_to_all(qkv_part.reshape(n, piece, 3 * heads_dim), "ctx", split_axis=0, concat_axis=2, tiled=True)

    ffn = product_sum(e0, e1, ffn_all, rows, n, 3, False, "down", width)
    ffn, out_raw, qkv_raw = lax.optimization_barrier((ffn, out_raw, qkv_raw))
    output = (jnp.stack(x1) + ffn.reshape(rows, local_len, width)).astype(bf16)
    qkv_raw = qkv_raw.reshape(piece, n, 3, heads_dim).astype(f32)
    query_raw, key_raw, value_raw = (qkv_raw[:, :, i].reshape(piece, width) for i in range(3))
    input_grad = jnp.stack(dx1) + standardize_back(x_hat, x_rstd, da).reshape(rows, local_len, width)

    def against(w, raw):
        return jnp.sum(w.astype(f32) * raw, axis=-1)

    def grown(raw, gain):
        return raw * gain.astype(f32)[:, None]

    gain_one = against(w_query, query_raw) + against(w_key, key_raw) + against(w_value, value_raw)
    return (output, input_grad, grown(query_raw, gain_attn), grown(key_raw, gain_attn), grown(value_raw, gain_attn),
            grown(out_raw, gain_attn_sub), grown(up_raw, gain_ffn), grown(down_raw, gain_ffn_sub),
            gain_one, against(w_out, out_raw), against(w_up, up_raw), against(w_down, down_raw))


def solution(mesh):
    split = P(BOTH, None)
    acts = P("row", "ctx", None)
    gain = P(BOTH)
    return jax.shard_map(
        body,
        mesh=mesh,
        in_specs=(acts, P("row", None)) + (split,) * 6 + (gain,) * 4 + (acts,),
        out_specs=(acts, acts) + (split,) * 6 + (gain,) * 4,
        check_vma=False,
    )
```

```python
import functools

import jax
import jax.numpy as jnp
from jax import lax
from jax.experimental import pallas as pl
from jax.experimental.pallas import tpu as pltpu
from jax.sharding import PartitionSpec as P

bf16 = jnp.bfloat16
f32 = jnp.float32
HEAD_DIM = 64
HALF = HEAD_DIM // 2
PAIR = 2 * HEAD_DIM
LOG2E = 1.4426950408889634
NEG = -1e30
ROW_LEN = 2048
XPOS_BASE = 512
EPS = 1e-5
BOTH = ("row", "ctx")


def walk(span_ref, qb, step):
    first = span_ref[2 + 2 * (qb)]
    clear = span_ref[3 + 2 * (qb)]

    def edge(t, carry):
        step(jnp.where(t < clear - first, first + t, qb), True)
        return carry

    def plain(kb, carry):
        step(kb, False)
        return carry

    lax.fori_loop(0, clear - first + 1, edge, 0)
    lax.fori_loop(clear, qb, plain, 0)


def allowed(lowest, kb, qb, blk):
    key = kb * blk + lax.broadcasted_iota(jnp.int32, (blk, blk), 0)
    query = qb * blk + lax.broadcasted_iota(jnp.int32, (blk, blk), 1)
    return (key <= query) & (key >= lowest)


def forward_kernel(nh, blk, unit, span_ref, q0_ref, q1_ref, k0_ref, k1_ref, v0_ref, v1_ref, table_ref, lo_ref,
                   o_ref, oT_ref, lse_ref, qT_ref, kT_ref, vT_ref, k_s, qm_s, acc_s, m_s, l_s):
    qb = pl.program_id(0)
    dim = nh * HEAD_DIM
    length = kT_ref.shape[1]
    core, place = span_ref[0], span_ref[1]
    spots = blk // (2 * unit)
    inner = lax.rem(place, spots)

    def turned(values, at, kind):
        cosine = table_ref[2 * kind, :, pl.ds(at, unit)]
        sine = table_ref[2 * kind + 1, :, pl.ds(at, unit)]
        out = []
        for h in range(nh):
            one = values[h * HEAD_DIM:h * HEAD_DIM + HALF]
            two = values[h * HEAD_DIM + HALF:(h + 1) * HEAD_DIM]
            out += [one * cosine - two * sine, two * cosine + one * sine]
        return jnp.concatenate(out, axis=0).astype(bf16)

    @pl.when(qb == 0)
    def _():
        def load(j, carry):
            src = pl.multiple_of((j ^ place) * unit, unit)
            for half, ref, v_ref in ((0, k0_ref, v0_ref), (1, k1_ref, v1_ref)):
                at = pl.multiple_of((2 * j + (core ^ half)) * unit, unit)
                key = turned(ref[:, pl.ds(src, unit)], at, 1)
                kT_ref[:, pl.ds(at, unit)] = key
                k_s[pl.ds(at, unit), :] = key.T
                vT_ref[:, pl.ds(at, unit)] = v_ref[:, pl.ds(src, unit)].astype(bf16)
            return carry

        lax.fori_loop(0, length // (2 * unit), load, 0)

    for u in range(spots):
        src = pl.multiple_of((u ^ inner) * unit, unit)
        for half, ref in ((0, q0_ref), (1, q1_ref)):
            at = pl.multiple_of((2 * u + (core ^ half)) * unit, unit)
            qT_ref[:, pl.ds(at, unit)] = turned(ref[:, pl.ds(src, unit)], pl.multiple_of(qb * blk + at, unit), 0)
    for h in range(nh):
        own = h % 2
        qm_s[h, pl.ds(own * HEAD_DIM, HEAD_DIM), :] = qT_ref[pl.ds(h * HEAD_DIM, HEAD_DIM), :]
        qm_s[h, pl.ds((1 - own) * HEAD_DIM, HEAD_DIM), :] = jnp.zeros((HEAD_DIM, blk), bf16)
    acc_s[...] = jnp.zeros_like(acc_s)
    m_s[...] = jnp.full_like(m_s, NEG)
    l_s[...] = jnp.zeros_like(l_s)
    lowest = lo_ref[...]

    def step(kb, masked):
        at = pl.multiple_of(kb * blk, blk)
        if masked:
            ok = allowed(lowest, kb, qb, blk)
        for h in range(nh):
            rows = pl.ds(h * HEAD_DIM, HEAD_DIM)
            s = jnp.dot(k_s[pl.ds(at, blk), pl.ds((h // 2) * PAIR, PAIR)], qm_s[h], preferred_element_type=f32)
            s = s * (LOG2E * HEAD_DIM**-0.5)
            if masked:
                s = jnp.where(ok, s, NEG)
            before = m_s[h:h + 1, :]
            now = jnp.maximum(before, jnp.max(s, axis=0, keepdims=True))
            p = jnp.exp2(s - now)
            fade = jnp.exp2(before - now)
            m_s[h:h + 1, :] = now
            l_s[h:h + 1, :] = l_s[h:h + 1, :] * fade + jnp.sum(p, axis=0, keepdims=True)
            acc_s[rows, :] = acc_s[rows, :] * fade + jnp.dot(
                vT_ref[rows, pl.ds(at, blk)], p.astype(bf16), preferred_element_type=f32)

    walk(span_ref, qb, step)
    for h in range(nh):
        rows = pl.ds(h * HEAD_DIM, HEAD_DIM)
        oT_ref[rows, :] = acc_s[rows, :] / l_s[h:h + 1, :]
        lse_ref[h:h + 1, :] = m_s[h:h + 1, :] + jnp.log2(l_s[h:h + 1, :])
    o_ref[...] = oT_ref[...].T.astype(bf16)


def backward_kernel(nh, blk, unit, span_ref, qT_ref, kT_ref, vT_ref, do_ref, oT_ref, lse_ref, table_ref, lo_ref,
                    old0_ref, old1_ref, d0_ref, d1_ref, k_s, v_s, qm_s, dm_s, qn_s, dn_s, acc_s, dk_s, dv_s, p_s, ds_s, dl_s):
    qb = pl.program_id(0)
    dim = nh * HEAD_DIM
    length = kT_ref.shape[1]
    count = length // blk
    scale = HEAD_DIM**-0.5
    core, place = span_ref[0], span_ref[1]

    @pl.when(qb == 0)
    def _():
        for c in range(count):
            k_s[pl.ds(c * blk, blk), :] = kT_ref[:, pl.ds(c * blk, blk)].T
            v_s[pl.ds(c * blk, blk), :] = vT_ref[:, pl.ds(c * blk, blk)].T
        dk_s[...] = jnp.zeros_like(dk_s)
        dv_s[...] = jnp.zeros_like(dv_s)

    doT = do_ref[...].T
    q = qT_ref[...].T
    lane = lax.broadcasted_iota(jnp.int32, (blk, PAIR), 1)
    prod = doT.astype(f32) * oT_ref[...]
    for h in range(nh):
        own = h % 2
        rows = slice(h * HEAD_DIM, (h + 1) * HEAD_DIM)
        zero = jnp.zeros((HEAD_DIM, blk), bf16)
        qm_s[h, pl.ds(own * HEAD_DIM, HEAD_DIM), :] = qT_ref[pl.ds(h * HEAD_DIM, HEAD_DIM), :]
        qm_s[h, pl.ds((1 - own) * HEAD_DIM, HEAD_DIM), :] = zero
        dm_s[h, pl.ds(own * HEAD_DIM, HEAD_DIM), :] = doT[rows, :]
        dm_s[h, pl.ds((1 - own) * HEAD_DIM, HEAD_DIM), :] = zero
        mine = (lane // HEAD_DIM) == own
        pair = slice((h // 2) * PAIR, (h // 2) * PAIR + PAIR)
        qn_s[h // 2, pl.ds(own * blk, blk), :] = jnp.where(mine, q[:, pair], jnp.zeros((), bf16))
        dn_s[h // 2, pl.ds(own * blk, blk), :] = jnp.where(mine, do_ref[:, pair], jnp.zeros((), bf16))
        dl_s[h:h + 1, :] = jnp.sum(prod[rows, :], axis=0, keepdims=True)
    acc_s[...] = jnp.zeros_like(acc_s)
    lowest = lo_ref[...]

    def step(kb, masked):
        at = pl.multiple_of(kb * blk, blk)
        if masked:
            ok = allowed(lowest, kb, qb, blk)
        for g in range(nh // 2):
            lanes = pl.ds(g * PAIR, PAIR)
            for own in range(2):
                h = 2 * g + own
                rows = pl.ds(h * HEAD_DIM, HEAD_DIM)
                s = jnp.dot(k_s[pl.ds(at, blk), lanes], qm_s[h], preferred_element_type=f32) * (LOG2E * scale)
                p = jnp.exp2(s - lse_ref[h:h + 1, :])
                if masked:
                    p = jnp.where(ok, p, 0.0)
                dp = jnp.dot(v_s[pl.ds(at, blk), lanes], dm_s[h], preferred_element_type=f32)
                ds = (p * (dp - dl_s[h:h + 1, :])).astype(bf16)
                p_s[g, :, pl.ds(own * blk, blk)] = p.astype(bf16)
                ds_s[g, :, pl.ds(own * blk, blk)] = ds
                acc_s[rows, :] += jnp.dot(kT_ref[rows, pl.ds(at, blk)], ds, preferred_element_type=f32)
            dv_s[pl.ds(at, blk), lanes] += jnp.dot(p_s[g], dn_s[g], preferred_element_type=f32)
            dk_s[pl.ds(at, blk), lanes] += jnp.dot(ds_s[g], qn_s[g], preferred_element_type=f32)

    walk(span_ref, qb, step)

    def turned_back(values, at, size, kind):
        cosine = table_ref[2 * kind, :, pl.ds(at, size)] * scale
        sine = table_ref[2 * kind + 1, :, pl.ds(at, size)] * scale
        out = []
        for h in range(nh):
            one = values[h * HEAD_DIM:h * HEAD_DIM + HALF]
            two = values[h * HEAD_DIM + HALF:(h + 1) * HEAD_DIM]
            out += [one * cosine + two * sine, two * cosine - one * sine]
        return jnp.concatenate(out, axis=0).T.astype(bf16)

    spots = blk // (2 * unit)
    for u in range(spots):
        dst = pl.multiple_of(((qb * spots + u) ^ place) * unit, unit)
        for half, ref in ((0, d0_ref), (1, d1_ref)):
            at = pl.multiple_of((2 * u + (core ^ half)) * unit, unit)
            ref[pl.ds(dst, unit), pl.ds(0, dim)] = turned_back(
                acc_s[:, pl.ds(at, unit)], pl.multiple_of(qb * blk + at, unit), unit, 0)

    @pl.when(qb == count - 1)
    def _():
        def store(j, carry):
            dst = pl.multiple_of((j ^ place) * unit, unit)
            for half, ref in ((0, d0_ref), (1, d1_ref)):
                at = pl.multiple_of((2 * j + (core ^ half)) * unit, unit)
                ref[pl.ds(dst, unit), pl.ds(dim, dim)] = turned_back(dk_s[pl.ds(at, unit), :].T, at, unit, 1)
                ref[pl.ds(dst, unit), pl.ds(2 * dim, dim)] = dv_s[pl.ds(at, unit), :].astype(bf16)
            return carry

        lax.fori_loop(0, length // (2 * unit), store, 0)


PARAMS = pltpu.CompilerParams(dimension_semantics=("arbitrary",), vmem_limit_bytes=60 * 2**20)


def span_of(lowest, blk, core, place):
    count = lowest.shape[0] // blk
    blocks = lowest.reshape(count, blk)
    own = jnp.arange(count, dtype=jnp.int32)
    first = jnp.minimum(blocks[:, 0] // blk, own)
    clear = jnp.minimum((blocks[:, -1] + blk - 1) // blk, own)
    both = jnp.stack([first, clear], axis=-1).reshape(-1)
    return jnp.concatenate([jnp.stack([core, place]), both]).astype(jnp.int32)


def attention_forward(row, half0, half1, table, lowest, span, blk, unit):
    length = lowest.shape[0]
    dim = half0.shape[0] // 3
    nh, count = dim // HEAD_DIM, length // blk
    spots = blk // (2 * unit)
    sds = jax.ShapeDtypeStruct
    pick = pl.BlockSpec((dim, blk // 2), lambda q, s: (0, row * count + (q ^ lax.div(s[1], spots))))
    keys = pl.BlockSpec((dim, length // 2), lambda q, s: (1, row))
    values = pl.BlockSpec((dim, length // 2), lambda q, s: (2, row))
    wide = pl.BlockSpec((dim, length), lambda q, s: (0, 0))
    cut = pl.BlockSpec((dim, blk), lambda q, s: (0, q))
    return pl.pallas_call(
        functools.partial(forward_kernel, nh, blk, unit),
        out_shape=(sds((length, dim), bf16), sds((dim, length), f32), sds((nh, length), f32),
                   sds((dim, length), bf16), sds((dim, length), bf16), sds((dim, length), bf16)),
        grid_spec=pltpu.PrefetchScalarGridSpec(
            num_scalar_prefetch=1, grid=(count,),
            in_specs=[pick, pick, keys, keys, values, values,
                      pl.BlockSpec((4, HALF, length), lambda q, s: (0, 0, 0)),
                      pl.BlockSpec((1, blk), lambda q, s: (0, q))],
            out_specs=[pl.BlockSpec((blk, dim), lambda q, s: (q, 0)), cut,
                       pl.BlockSpec((nh, blk), lambda q, s: (0, q)), cut, wide, wide],
            scratch_shapes=[pltpu.VMEM((length, dim), bf16), pltpu.VMEM((nh, PAIR, blk), bf16), pltpu.VMEM((dim, blk), f32),
                            pltpu.VMEM((8, blk), f32), pltpu.VMEM((8, blk), f32)]),
        compiler_params=PARAMS, name="attention_forward",
        cost_estimate=pl.CostEstimate(flops=4 * 4 * dim * length * length // 2, bytes_accessed=10 * 2**20,
                                      transcendentals=nh * length * length // 2),
    )(span, half0, half1, half0, half1, half0, half1, table, lowest[None, :])


def attention_backward(row, rows, saved, do, table, lowest, span, blk, unit, before):
    oT, lse, qT, kT, vT = saved
    length = lowest.shape[0]
    dim = qT.shape[0]
    nh, count = dim // HEAD_DIM, length // blk
    sds = jax.ShapeDtypeStruct
    cut = pl.BlockSpec((dim, blk), lambda q, s: (0, q))
    wide = pl.BlockSpec((dim, length), lambda q, s: (0, 0))
    grad = pl.BlockSpec((length // 2, 3 * dim), lambda q, s: (row, 0))
    whole = sds((rows * length // 2, 3 * dim), bf16)
    kernel = functools.partial(backward_kernel, nh, blk, unit)
    if before is None:
        def call(span_ref, *refs):
            kernel(span_ref, *refs[:8], None, None, *refs[8:])
    else:
        call = kernel
    return pl.pallas_call(
        call,
        out_shape=(whole, whole),
        grid_spec=pltpu.PrefetchScalarGridSpec(
            num_scalar_prefetch=1, grid=(count,),
            in_specs=[cut, wide, wide, pl.BlockSpec((blk, dim), lambda q, s: (q, 0)), cut,
                      pl.BlockSpec((nh, blk), lambda q, s: (0, q)),
                      pl.BlockSpec((4, HALF, length), lambda q, s: (0, 0, 0)),
                      pl.BlockSpec((1, blk), lambda q, s: (0, q))]
            + ([] if before is None else [pl.BlockSpec(memory_space=pl.ANY)] * 2),
            out_specs=[grad, grad],
            scratch_shapes=[pltpu.VMEM((length, dim), bf16), pltpu.VMEM((length, dim), bf16),
                            pltpu.VMEM((nh, PAIR, blk), bf16), pltpu.VMEM((nh, PAIR, blk), bf16),
                            pltpu.VMEM((nh // 2, 2 * blk, PAIR), bf16), pltpu.VMEM((nh // 2, 2 * blk, PAIR), bf16),
                            pltpu.VMEM((dim, blk), f32), pltpu.VMEM((length, dim), f32), pltpu.VMEM((length, dim), f32),
                            pltpu.VMEM((nh // 2, blk, 2 * blk), bf16), pltpu.VMEM((nh // 2, blk, 2 * blk), bf16),
                            pltpu.VMEM((8, blk), f32)]),
        compiler_params=PARAMS, name="attention_backward",
        input_output_aliases={} if before is None else {9: 0, 10: 1},
        cost_estimate=pl.CostEstimate(flops=10 * 4 * dim * length * length // 2, bytes_accessed=20 * 2**20,
                                      transcendentals=nh * length * length // 2),
    )(span, qT, kT, vT, do, oT, lse, table, lowest[None, :], *(before or ()))


def hat_of(values):
    center = values - jnp.mean(values, axis=-1, keepdims=True)
    rstd = lax.rsqrt(jnp.mean(center * center, axis=-1, keepdims=True) + EPS)
    return center * rstd, rstd


def hat_back(hat, rstd, grad):
    return rstd * (grad - jnp.mean(grad, axis=-1, keepdims=True) - hat * jnp.mean(grad * hat, axis=-1, keepdims=True))


def wide_row(o_ref):
    return jnp.concatenate([o_ref[i] for i in range(o_ref.shape[0])], axis=1).astype(f32)


def middle_forward_kernel(o_ref, x_ref, w_ref, c_ref, x1_ref, b_ref):
    c = hat_of(wide_row(o_ref))[0].astype(bf16)
    c_ref[...] = c
    x1 = x_ref[...].astype(f32) + jnp.dot(c, w_ref[...], preferred_element_type=f32)
    x1_ref[...] = x1
    b_ref[...] = hat_of(x1)[0].astype(bf16)


def middle_forward(o, x, w):
    n, size, dim = o.shape
    width = n * dim
    step = min(128, size)
    sds = jax.ShapeDtypeStruct
    flat = pl.BlockSpec((step, width), lambda t: (t, 0))
    return pl.pallas_call(
        middle_forward_kernel,
        out_shape=(sds((size, width), bf16), sds((size, width), f32), sds((size, width), bf16)),
        grid=(size // step,),
        in_specs=[pl.BlockSpec((n, step, dim), lambda t: (0, t, 0)), flat,
                  pl.BlockSpec((width, width), lambda t: (0, 0))],
        out_specs=(flat, flat, flat),
        compiler_params=PARAMS, name="middle_forward",
        cost_estimate=pl.CostEstimate(flops=2 * size * width * width, bytes_accessed=14 * 2**20, transcendentals=0),
    )(o, x, w)


def middle_backward_kernel(o_ref, x1_ref, db_ref, dy_ref, w_ref, dx_ref, low_ref, do_ref):
    hat, rstd = hat_of(x1_ref[...])
    dx1 = dy_ref[...].astype(f32) + hat_back(hat, rstd, db_ref[...])
    dx_ref[...] = dx1
    low_ref[...] = dx1.astype(bf16)
    dc = times_rows(dx1.astype(bf16), w_ref[...])
    hat, rstd = hat_of(wide_row(o_ref))
    d_o = hat_back(hat, rstd, dc).astype(bf16)
    dim = do_ref.shape[2]
    for i in range(do_ref.shape[0]):
        do_ref[i] = d_o[:, i * dim:(i + 1) * dim]


def middle_backward(row, o, x1, db, dy, w):
    n, size, dim = o.shape
    width = n * dim
    step = min(128, size)
    sds = jax.ShapeDtypeStruct
    flat = pl.BlockSpec((step, width), lambda t: (t, 0))
    part = pl.BlockSpec((n, step, dim), lambda t: (0, t, 0))
    return pl.pallas_call(
        middle_backward_kernel,
        out_shape=(sds((size, width), f32), sds((size, width), bf16), sds((n, size, dim), bf16)),
        grid=(size // step,),
        in_specs=[part, flat, pl.BlockSpec((step, width), lambda t: (row * (size // step) + t, 0)), flat,
                  pl.BlockSpec((width, width), lambda t: (0, 0))],
        out_specs=(flat, flat, part),
        compiler_params=PARAMS, name="middle_backward",
        cost_estimate=pl.CostEstimate(flops=2 * size * width * width, bytes_accessed=16 * 2**20, transcendentals=0),
    )(o, x1, db, dy, w)


def ways(row, n):
    bits = [1 << k for k in range(1, n.bit_length() - 1)]
    return bits if row % 2 == 0 else bits[::-1]


def times_rows(a, w):
    return lax.dot_general(a, w, (((1,), (1,)), ((), ())), preferred_element_type=f32)


def weight_copies(all_ref, kind, dst_ref, sems, first=0):
    m, lines, ff = all_ref.shape
    unit = ff // m
    pieces = dst_ref.shape[1 if kind == "down" else 0] // ff
    depth = lines - unit * pieces
    copies = []
    for r in range(m):
        if kind == "up":
            moves = [(all_ref.at[r, pl.ds(0, depth), :], dst_ref.at[pl.ds(r * depth, depth), :])]
        else:
            moves = [(all_ref.at[r, pl.ds(depth + q * unit, unit), :],
                      dst_ref.at[pl.ds(r * unit, unit), pl.ds(q * ff, ff)]) for q in range(pieces)]
        for src, dst in moves:
            copies.append(pltpu.make_async_copy(src, dst, sems.at[first + len(copies)]))
    for copy in copies:
        copy.start()
    return copies


def product_sum_kernel(n, rows, cols, turned, kind, x0_ref, x1_ref, w_ref, o_ref, part_s, core_s, sum_s, got_s, send_sem, recv_sem,
                       *own_w):
    mine = lax.axis_index("ctx")
    loads = []
    if kind:
        loads = weight_copies(w_ref, kind, *own_w)
        w_ref = own_w[0]
    spots = n // 2
    size = x0_ref.shape[0] // (rows * spots)
    width = o_ref.shape[1]
    barrier = pltpu.get_barrier_semaphore()
    bits = [1] + ways(0, n)
    for bit in bits:
        pl.semaphore_signal(barrier, inc=1, device_id={"ctx": mine ^ bit}, device_id_type=pl.DeviceIdType.MESH)
    pl.semaphore_wait(barrier, len(bits))
    for copy in loads:
        copy.wait()
    copies = []

    def send(src, dst, bit):
        at = len(copies)
        copy = pltpu.make_async_remote_copy(
            src_ref=src, dst_ref=dst, send_sem=send_sem.at[at], recv_sem=recv_sem.at[at],
            device_id={"ctx": mine ^ bit}, device_id_type=pl.DeviceIdType.MESH)
        copy.start()
        copies.append(copy)
        return copy

    def key(row, k):
        return [-(k & (bit >> 1)) for bit in ways(row, n)]

    orders = []
    for r in range(rows):
        way = [bit >> 1 for bit in ways(r, n)]
        orders.append(sorted(range(spots), key=lambda k: [0 if k & bit else 1 for bit in way]))
    todo = [(r, orders[r][t]) for t in range(spots) for r in range(rows)]
    inbox, slot, slots = {}, {}, 0

    def product(x_ref, r, k, finish):
        begin = (r * spots + k) * size

        @pl.loop(0, width // cols)
        def _(c):
            at = pl.ds(pl.multiple_of(c * cols, cols), cols)
            x = x_ref[pl.ds(begin, size), :]
            finish(at, times_rows(x, w_ref[at, :]) if turned else jnp.dot(x, w_ref[:, at], preferred_element_type=f32))

    def pair(r, k):
        spot = r * spots + k

        def keep(at, value):
            part_s[spot, :, at] = value.astype(bf16)

        product(x1_ref, r, k, keep)
        inbox[r, k] = send(part_s.at[spot], core_s.at[spot], 1)

    def own(r, k):
        spot = r * spots + k
        inbox[r, k].wait_recv()

        def add(at, value):
            sum_s[spot, :, at] = (value + core_s[spot, :, at].astype(f32)).astype(bf16)

        product(x0_ref, r, k, add)

    def pass_on(r, k, stage):
        nonlocal slots
        bit = ways(r, n)[stage]
        if k & (bit >> 1):
            inbox[r, k ^ (bit >> 1), stage] = (send(sum_s.at[r * spots + k], got_s.at[slots], bit), slots)
            slots += 1

    group = max(rows * spots // 2, 1)
    for begin in range(0, len(todo), group):
        for r, k in todo[begin:begin + group]:
            pair(r, k)
        for r, k in todo[begin:begin + group]:
            own(r, k)
            pass_on(r, k, 0)
    stages = len(bits) - 1
    for stage in range(stages):
        for r, k in todo:
            way = [bit >> 1 for bit in ways(r, n)]
            if any(k & bit for bit in way[:stage + 1]):
                continue
            copy, at = inbox[r, k, stage]
            copy.wait_recv()
            spot = r * spots + k
            if stage == stages - 1:
                o_ref[pl.ds(r * size, size), :] = sum_s[spot].astype(f32) + got_s[at].astype(f32)
            else:
                sum_s[spot] = (sum_s[spot].astype(f32) + got_s[at].astype(f32)).astype(bf16)
                pass_on(r, k, stage + 1)
    for copy in copies:
        copy.wait_send()


def product_sum(x0, x1, w, rows, n, collective_id, turned=False, kind=None, wide=None):
    size = x0.shape[0] // (rows * (n // 2))
    depth = x0.shape[1]
    width = wide if kind else w.shape[0 if turned else 1]
    count = rows * (n // 2)
    moves = count + rows * (n // 2 - 1)
    vmem = pl.BlockSpec(memory_space=pltpu.VMEM)
    flops = 4 * x0.shape[0] * x0.shape[1] * width
    return pl.pallas_call(
        functools.partial(product_sum_kernel, n, rows, min(512, width), turned, kind),
        out_shape=jax.ShapeDtypeStruct((rows * size, width), f32),
        in_specs=[vmem, vmem, pl.BlockSpec(memory_space=pl.ANY) if kind else vmem], out_specs=vmem,
        scratch_shapes=[pltpu.VMEM((count, size, width), bf16), pltpu.VMEM((count, size, width), bf16),
                        pltpu.VMEM((count, size, width), bf16), pltpu.VMEM((moves - count, size, width), bf16),
                        pltpu.SemaphoreType.DMA((moves,)), pltpu.SemaphoreType.DMA((moves,))]
        + ([pltpu.VMEM((width, depth) if turned else (depth, width), bf16), pltpu.SemaphoreType.DMA((64,))] if kind else []),
        compiler_params=pltpu.CompilerParams(collective_id=collective_id, has_side_effects=True, vmem_limit_bytes=60 * 2**20),
        name="product_sum",
        cost_estimate=pl.CostEstimate(flops=4 * flops, bytes_accessed=20 * 2**20, transcendentals=0),
    )(x0, x1, w)


def gather_product_kernel(n, rows, cols, b_ref, dy0_ref, dy1_ref, w_ref, b0_ref, b1_ref, h0_ref, h1_ref, d0_ref, d1_ref,
                          stat_ref, up_ref, down_ref, got_s, d_s, h_s, dy_s, w_sem, send_sem, recv_sem, dy_sem, b_sem, h_sem, d_sem):
    mine = lax.axis_index("ctx")
    spots = n // 2
    size = b_ref.shape[0] // rows
    ff = up_ref.shape[1]
    loads = weight_copies(w_ref, "down", down_ref, w_sem)
    loads_up = weight_copies(w_ref, "up", up_ref, w_sem, len(loads))
    count = rows * spots
    barrier = pltpu.get_barrier_semaphore()
    bits = [1] + ways(0, n)
    for bit in bits:
        pl.semaphore_signal(barrier, inc=1, device_id={"ctx": mine ^ bit}, device_id_type=pl.DeviceIdType.MESH)
    pl.semaphore_wait(barrier, len(bits))
    sends, locals_, arrival = [], [], {}

    def send(src, half, row, k, bit):
        at, to = len(sends), half * count + row * spots + k
        copy = pltpu.make_async_remote_copy(
            src_ref=src, dst_ref=got_s.at[to], send_sem=send_sem.at[at], recv_sem=recv_sem.at[at],
            device_id={"ctx": mine ^ bit}, device_id_type=pl.DeviceIdType.MESH)
        copy.start()
        sends.append(copy)
        arrival[half, row, k] = copy

    def held(half, row, k):
        if half == 0 and k == 0:
            return b_ref.at[pl.ds(row * size, size), :]
        return got_s.at[half * count + row * spots + k]

    def onward(row, k):
        way = ways(row, n)
        top = max([s for s, bit in enumerate(way) if k & (bit >> 1)], default=-1)
        for bit in way[top + 1:]:
            send(held(0, row, k), 0, row, k | (bit >> 1), bit)
        send(held(0, row, k), 1, row, k, 1)

    for r in range(rows):
        onward(r, 0)

    def fetch(t, slot):
        begin = pl.multiple_of(lax.rem(t, count) * size, size)

        @pl.when(t < count)
        def _():
            pltpu.make_async_copy(dy0_ref.at[pl.ds(begin, size), :], dy_s.at[slot], dy_sem.at[slot]).start()

        @pl.when(t >= count)
        def _():
            pltpu.make_async_copy(dy1_ref.at[pl.ds(begin, size), :], dy_s.at[slot], dy_sem.at[slot]).start()

    fetch(0, 0)
    for copy in loads:
        copy.wait()

    @pl.loop(0, 2 * count)
    def _(t):
        slot = lax.rem(t, 2)

        @pl.when(t + 1 < 2 * count)
        def _():
            fetch(t + 1, 1 - slot)

        pltpu.make_async_copy(dy0_ref.at[pl.ds(0, size), :], dy_s.at[slot], dy_sem.at[slot]).wait()

        @pl.loop(0, ff // cols)
        def _(c):
            at = pl.ds(pl.multiple_of(c * cols, cols), cols)
            d_s[t, :, at] = times_rows(dy_s[slot], down_ref[at, :])

    for t in range(2 * count):
        dst = (d0_ref, d1_ref)[t // count].at[pl.ds((t % count) * size, size), :]
        copy = pltpu.make_async_copy(d_s.at[t], dst, d_sem.at[t])
        copy.start()
        locals_.append(copy)

    for copy in loads_up:
        copy.wait()
    outs = []
    lane = lax.broadcasted_iota(jnp.int32, (32, 128), 1)

    def block(half, row, k):
        t = half * count + row * spots + k
        src = held(half, row, k)
        copy = pltpu.make_async_copy(src, (b0_ref, b1_ref)[half].at[pl.ds((t % count) * size, size), :], b_sem.at[t])
        copy.start()
        locals_.append(copy)
        slot = len(outs) % 2
        if len(outs) >= 2:
            outs[-2].wait()

        @pl.loop(0, ff // cols)
        def _(c):
            at = pl.ds(pl.multiple_of(c * cols, cols), cols)
            h_s[slot, :, at] = jnp.dot(src[...], up_ref[:, at], preferred_element_type=f32)

        copy = pltpu.make_async_copy(h_s.at[slot], (h0_ref, h1_ref)[half].at[pl.ds((t % count) * size, size), :], h_sem.at[t])
        copy.start()
        outs.append(copy)

        @pl.loop(0, size // 32)
        def _(c):
            at = pl.ds(pl.multiple_of(c * 32, 32), 32)
            h = h_s[slot, at, :]
            gel = h * (0.5 * (1.0 + lax.erf(h * (2.0**-0.5))))
            d = d_s[t, at, :]
            mean = jnp.mean(gel, axis=-1, keepdims=True)
            off = gel - mean
            spread = jnp.sum(off * off, axis=-1, keepdims=True)
            total = jnp.sum(d, axis=-1, keepdims=True)
            cross = jnp.sum(d * off, axis=-1, keepdims=True)
            line = jnp.where(lane == 0, mean, jnp.where(lane == 1, spread, jnp.where(lane == 2, total, cross)))
            stat_ref[pl.ds(pl.multiple_of(t * size + c * 32, 32), 32), :] = line

    order = []
    for k in range(spots):
        for r in range(rows):
            way = ways(r, n)
            order.append((r, sum((bit >> 1) for s, bit in enumerate(way) if k >> s & 1)))
    for begin in range(0, len(order), rows):
        some = order[begin:begin + rows]
        for r, k in some:
            if k:
                arrival[0, r, k].wait_recv()
                onward(r, k)
        for r, k in some:
            block(0, r, k)
        for r, k in some:
            arrival[1, r, k].wait_recv()
            block(1, r, k)
    for copy in outs[-2:] + locals_:
        copy.wait()
    for copy in sends:
        copy.wait_send()


def gather_product(b, dy0, dy1, weights, rows, n, collective_id):
    size = b.shape[0] // rows
    width, ff = b.shape[1], weights.shape[2]
    count = rows * (n // 2)
    half = count * size
    moves = rows * (n - 1)
    vmem, here = pl.BlockSpec(memory_space=pltpu.VMEM), pl.BlockSpec(memory_space=pl.ANY)
    sds = jax.ShapeDtypeStruct
    return pl.pallas_call(
        functools.partial(gather_product_kernel, n, rows, min(256, ff)),
        out_shape=(sds((half, width), bf16),) * 2 + (sds((half, ff), f32),) * 4 + (sds((2 * half, 128), f32),),
        in_specs=[vmem, here, here, here], out_specs=(here,) * 6 + (vmem,),
        scratch_shapes=[pltpu.VMEM((width, ff), bf16), pltpu.VMEM((ff, width), bf16),
                        pltpu.VMEM((2 * count, size, width), bf16), pltpu.VMEM((2 * count, size, ff), f32),
                        pltpu.VMEM((2, size, ff), f32), pltpu.VMEM((2, size, width), bf16), pltpu.SemaphoreType.DMA((64,)),
                        pltpu.SemaphoreType.DMA((moves,)), pltpu.SemaphoreType.DMA((moves,)), pltpu.SemaphoreType.DMA((2,))]
        + [pltpu.SemaphoreType.DMA((2 * count,))] * 3,
        compiler_params=pltpu.CompilerParams(collective_id=collective_id, has_side_effects=True, vmem_limit_bytes=62 * 2**20),
        name="gather_product",
        cost_estimate=pl.CostEstimate(flops=16 * half * width * ff, bytes_accessed=70 * 2**20, transcendentals=0),
    )(b, dy0, dy1, weights)


def standardize(values):
    center = values - jnp.mean(values, axis=-1, keepdims=True)
    spread = jnp.mean(center * center, axis=-1, keepdims=True)
    rstd = lax.rsqrt(spread + EPS)
    return center * rstd, rstd


def standardize_back(hat, rstd, grad):
    return rstd * (grad - jnp.mean(grad, axis=-1, keepdims=True) - hat * jnp.mean(grad * hat, axis=-1, keepdims=True))


def row_places(lengths, row_len):
    places = jnp.arange(row_len, dtype=jnp.int32)
    ends = jnp.cumsum(lengths, axis=-1)
    passed = ends[:, None, :] <= places[None, :, None]
    starts = jnp.sum(jnp.where(passed, lengths[:, None, :], 0), axis=-1)
    valid = places[None, :] < ends[:, -1:]
    lowest = jnp.where(valid, starts, places[None, :]).astype(jnp.int32)
    return (places[None, :] - starts).astype(f32), lowest


def xpos_tables(relative):
    ladder = jnp.arange(HALF, dtype=f32) / HALF
    rate = jnp.power(10000.0, -ladder)
    base = (ladder + 0.4) / 1.4
    angles = rate[None, :, None] * relative[:, None, :]
    power = (relative[:, None, :] - ROW_LEN / 2) / XPOS_BASE
    factor = jnp.power(base[None, :, None], power)
    cosine, sine = jnp.cos(angles), jnp.sin(angles)
    return jnp.stack([cosine * factor, sine * factor, cosine / factor, sine / factor], axis=1)


def dot(a, b, spec, kind=f32):
    return jnp.einsum(spec, a, b, preferred_element_type=f32).astype(kind)


def swap(x, bit):
    n = lax.axis_size("ctx")
    return lax.ppermute(x, "ctx", [(i, i ^ bit) for i in range(n)])


def exchange(blocks):
    n = lax.axis_size("ctx")
    mine = lax.axis_index("ctx")
    out = jnp.zeros_like(blocks)
    for bit in range(n):
        block = lax.dynamic_index_in_dim(blocks, mine ^ bit, 0, False)
        block = swap(block, bit) if bit else block
        out = lax.dynamic_update_index_in_dim(out, block, mine ^ bit, 0)
    return out


def after(x, *others):
    return lax.optimization_barrier((x, *others))[0]


def gather_start(x):
    return [{0: x[r]} for r in range(x.shape[0])]


def gather_step(held, step):
    n = lax.axis_size("ctx")
    out = []
    for r, parts in enumerate(held):
        bit = ways(r, n)[step]
        out.append({**parts, **{k | bit: swap(v, bit) for k, v in parts.items()}})
    return out


def gather_own(held, step):
    n = lax.axis_size("ctx")
    out = []
    for r, parts in enumerate(held):
        bit = ways(r, n)[step]
        out.append({**parts, bit: swap(parts[0], bit)})
    return out


def gather_rest(held, step):
    n = lax.axis_size("ctx")
    out = []
    for r, parts in enumerate(held):
        bit = ways(r, n)[step]
        moved = {k | bit: swap(v, bit) for k, v in parts.items() if k and not k & bit}
        out.append({**parts, **moved})
    return out


def gather_steps():
    return lax.axis_size("ctx").bit_length() - 2


def gather_end(held):
    return jnp.concatenate([parts[k] for parts in held for k in sorted(parts)], axis=0)


def gather_half(x):
    held = gather_start(x)
    for step in range(gather_steps()):
        held = gather_step(held, step)
    return gather_end(held)


def plus(a, b, kind=bf16):
    return (a.astype(f32) + b.astype(f32)).astype(kind)


def reduce_start(half0, half1, rows):
    n = lax.axis_size("ctx")
    width = half0.shape[-1]
    both = plus(half0, swap(half1, 1)).reshape(rows, n // 2, -1, width)
    return [{2 * k: both[r, k] for k in range(n // 2)} for r in range(rows)]


def reduce_step(held, step):
    n = lax.axis_size("ctx")
    out = []
    for r, parts in enumerate(held):
        bit = ways(r, n)[step]
        kind = bf16 if len(parts) > 2 else f32
        out.append({k: plus(v, swap(parts[k | bit], bit), kind) for k, v in parts.items() if not k & bit})
    return out


def reduce_end(held):
    return jnp.concatenate([parts[0] for parts in held], axis=0)


def reduce_halves(half0, half1, rows):
    held = reduce_start(half0, half1, rows)
    for step in range(gather_steps()):
        held = reduce_step(held, step)
    return reduce_end(held)


def body(inputs, doc_len, w_query, w_key, w_value, w_out, w_up, w_down, gain_attn, gain_attn_sub, gain_ffn,
         gain_ffn_sub, out_cotangent):
    rows, local_len, width = inputs.shape
    n, m = lax.axis_size("ctx"), lax.axis_size("row")
    row_len = local_len * n
    tokens, half = rows * local_len, rows * row_len // 2
    piece = w_query.shape[0]
    heads_dim = width // n
    ff = w_up.shape[1]
    unit = ff // (n * m)
    ff_dev = unit * m
    blk = min(512, row_len)
    mine = lax.axis_index("ctx")
    core, place = mine & 1, mine >> 1

    def scaled(w, gain):
        return (w.astype(f32) * gain.astype(f32)[:, None]).astype(bf16)

    x_own = inputs.reshape(tokens, width).astype(f32)
    x_hat, x_rstd = standardize(x_own)
    x_low = x_hat.astype(bf16)
    x_held = gather_step(gather_start(x_low.reshape(rows, local_len, width)), 0)

    qkv_local = jnp.concatenate(
        [scaled(w, gain_attn).reshape(piece, n, heads_dim) for w in (w_query, w_key, w_value)], axis=2)
    qkv_part = exchange(qkv_local.transpose(1, 0, 2)).reshape(n * piece, 3 * heads_dim)
    w_qkv = lax.all_gather(qkv_part, "row", axis=0, tiled=True)
    up_local = scaled(after(w_up, qkv_part), gain_ffn).reshape(piece, m, n, unit).transpose(2, 0, 1, 3).reshape(n, piece, ff_dev)
    up_part = lax.all_to_all(up_local, "ctx", split_axis=0, concat_axis=0, tiled=True).reshape(n * piece, ff_dev)
    for step in range(1, gather_steps()):
        x_held = gather_step(x_held, step)
    xh0 = gather_end(x_held)
    xh0, up_part = lax.optimization_barrier((xh0, up_part))
    xh1 = swap(xh0, 1)
    down_local = scaled(w_down, gain_ffn_sub)
    ffn_local = jnp.concatenate([up_part] + [down_local[:, q:q + ff_dev] for q in range(0, width, ff_dev)], axis=0)
    out_all = lax.all_gather(scaled(w_out, gain_attn_sub), BOTH, axis=0, tiled=True)

    relative, lowest = row_places(doc_len, row_len)
    table = xpos_tables(relative)
    span = [span_of(lowest[r], blk, core, place) for r in range(rows)]
    qkv0 = dot(w_qkv, xh0, "df,td->ft")
    qkv1 = dot(w_qkv, xh1, "df,td->ft")
    qkv0, qkv1, cot, out_all = lax.optimization_barrier((qkv0, qkv1, out_cotangent, out_all))
    ffn_all = lax.all_gather(after(ffn_local, out_all), "row", axis=0, tiled=False)
    dy_held = gather_step(gather_start(cot), 0)
    dy_steps = gather_steps()
    saved, o = [], []
    for r in range(rows):
        o_row, *kept = attention_forward(r, qkv0, qkv1, table[r], lowest[r], span[r], blk, local_len)
        if r == 0:
            o_row, kept, qkv0, qkv1, dy_held = lax.optimization_barrier((o_row, kept, qkv0, qkv1, dy_held))
            dy_held = gather_own(dy_held, 1)
        if r == rows - 1:
            o_row, o, dy_held = lax.optimization_barrier((o_row, o, dy_held))
            dy_held = gather_rest(dy_held, 1)
            for step in range(2, dy_steps):
                dy_held = gather_step(dy_held, step)
        saved.append(kept)
        o.append(lax.all_to_all(o_row.reshape(n, local_len, heads_dim), "ctx", split_axis=0, concat_axis=0, tiled=True))
    c, x1, b_low = zip(*[middle_forward(o[r], inputs[r], out_all) for r in range(rows)])
    b_low, dy_held = lax.optimization_barrier((b_low, dy_held))
    dy0 = gather_end(dy_held)
    dy1 = swap(dy0, 1)

    b0, b1, h0, h1, d_hat0, d_hat1, stats = gather_product(jnp.concatenate(b_low), dy0, dy1, ffn_all, rows, n, 4)
    stats = stats[:, :4].T
    order = jnp.arange(n // 2, dtype=jnp.int32) ^ place
    halves = jnp.arange(2, dtype=jnp.int32) ^ core

    def reorder(v):
        v = v.reshape(v.shape[0], 2, rows, n // 2, local_len)
        return jnp.take(jnp.take(v, halves, axis=1), order, axis=3).reshape(v.shape[0], 2 * half)

    stats = lax.all_gather(reorder(stats), "ctx", axis=0, tiled=False)
    mean = jnp.mean(stats[:, 0], axis=0)
    shift = stats[:, 0] - mean
    var = (jnp.sum(stats[:, 1], axis=0) + ff_dev * jnp.sum(shift * shift, axis=0)) / ff
    rstd = lax.rsqrt(var + EPS)
    d_mean = jnp.sum(stats[:, 2], axis=0) / ff
    d_corr = rstd * jnp.sum(stats[:, 3] + stats[:, 2] * shift, axis=0) / ff
    merged = reorder(jnp.stack([mean, rstd, d_mean, d_corr])).reshape(4, 2, half, 1)

    def finish(h, d_hat, which):
        cdf = 0.5 * (1.0 + lax.erf(h * (2.0**-0.5)))
        mean, rstd, d_mean, d_corr = (merged[k, which] for k in range(4))
        hat = (h * cdf - mean) * rstd
        d_gel = rstd * (d_hat - d_mean - hat * d_corr)
        pdf = jnp.exp(-0.5 * h * h) * 0.3989422804014327
        return hat.astype(bf16), (d_gel * (cdf + h * pdf)).astype(bf16)

    e0, dh0 = finish(h0, d_hat0, 0)
    e1, dh1 = finish(h1, d_hat1, 1)
    down_part = (dot(e0, dy0, "tf,td->fd") + dot(e1, dy1, "tf,td->fd")).astype(bf16)
    up_part = (dot(b0, dh0, "td,tf->df") + dot(b1, dh1, "td,tf->df")).astype(bf16)
    e0, e1, dh0, dh1, down_part, up_part = lax.optimization_barrier((e0, e1, dh0, dh1, down_part, up_part))
    down_sum = lax.psum_scatter(down_part, "row", scatter_dimension=0, tiled=True)
    db = product_sum(dh0, dh1, ffn_all, rows, n, 1, True, "up", width)
    db, up_part, down_sum = lax.optimization_barrier((db, up_part, down_sum))
    down_raw = down_sum.astype(f32)
    up_sum = lax.psum_scatter(up_part, "row", scatter_dimension=0, tiled=True)

    dx1, dx1b, d_o = zip(*[middle_backward(r, o[r], x1[r], db, out_cotangent[r], out_all) for r in range(rows)])
    do_heads = [lax.all_to_all(v, "ctx", split_axis=0, concat_axis=0, tiled=True).reshape(row_len, heads_dim) for v in d_o]
    c_order = jnp.concatenate(c).reshape(tokens, m, n, piece).transpose(0, 2, 1, 3).reshape(tokens, width)
    out_part = dot(c_order, jnp.concatenate(dx1b), "td,te->de", bf16)
    do_heads[0], out_part = lax.optimization_barrier((do_heads[0], out_part))
    grads = attention_backward(0, rows, saved[0], do_heads[0], table[0], lowest[0], span[0], blk, local_len, None)
    grads, do_heads, up_sum, out_part = lax.optimization_barrier((grads, do_heads, up_sum, out_part))
    out_part = lax.psum_scatter(out_part, "ctx", scatter_dimension=0, tiled=True)
    up_moved = lax.all_to_all(up_sum.reshape(n, piece, ff_dev), "ctx", split_axis=0, concat_axis=2, tiled=True)
    for r in range(1, rows):
        grads = attention_backward(r, rows, saved[r], do_heads[r], table[r], lowest[r], span[r], blk, local_len, grads)
    d0, d1 = grads
    qkv_part = (dot(xh0, d0, "td,tf->df") + dot(xh1, d1, "td,tf->df")).astype(bf16)
    d0, d1, qkv_part, out_part, up_moved = lax.optimization_barrier((d0, d1, qkv_part, out_part, up_moved))
    qkv_part = lax.psum_scatter(qkv_part, "row", scatter_dimension=0, tiled=True)
    da = product_sum(d0, d1, w_qkv, rows, n, 2, True)
    e0, e1, da, qkv_part, out_part = lax.optimization_barrier((e0, e1, da, qkv_part, out_part))
    out_raw = lax.psum_scatter(out_part, "row", scatter_dimension=0, tiled=True).astype(f32)
    up_raw = up_moved.reshape(piece, n, m, unit).transpose(0, 2, 1, 3).reshape(piece, ff).astype(f32)
    qkv_raw = lax.all_to_all(qkv_part.reshape(n, piece, 3 * heads_dim), "ctx", split_axis=0, concat_axis=2, tiled=True)

    ffn = product_sum(e0, e1, ffn_all, rows, n, 3, False, "down", width)
    ffn, out_raw, qkv_raw = lax.optimization_barrier((ffn, out_raw, qkv_raw))
    output = (jnp.stack(x1) + ffn.reshape(rows, local_len, width)).astype(bf16)
    qkv_raw = qkv_raw.reshape(piece, n, 3, heads_dim).astype(f32)
    query_raw, key_raw, value_raw = (qkv_raw[:, :, i].reshape(piece, width) for i in range(3))
    input_grad = jnp.stack(dx1) + standardize_back(x_hat, x_rstd, da).reshape(rows, local_len, width)

    def against(w, raw):
        return jnp.sum(w.astype(f32) * raw, axis=-1)

    def grown(raw, gain):
        return raw * gain.astype(f32)[:, None]

    gain_one = against(w_query, query_raw) + against(w_key, key_raw) + against(w_value, value_raw)
    return (output, input_grad, grown(query_raw, gain_attn), grown(key_raw, gain_attn), grown(value_raw, gain_attn),
            grown(out_raw, gain_attn_sub), grown(up_raw, gain_ffn), grown(down_raw, gain_ffn_sub),
            gain_one, against(w_out, out_raw), against(w_up, up_raw), against(w_down, down_raw))


def solution(mesh):
    split = P(BOTH, None)
    acts = P("row", "ctx", None)
    gain = P(BOTH)
    return jax.shard_map(
        body,
        mesh=mesh,
        in_specs=(acts, P("row", None)) + (split,) * 6 + (gain,) * 4 + (acts,),
        out_specs=(acts, acts) + (split,) * 6 + (gain,) * 4,
        check_vma=False,
    )
```

```python
import functools

import jax
import jax.numpy as jnp
from jax import lax
from jax.experimental import pallas as pl
from jax.experimental.pallas import tpu as pltpu
from jax.sharding import PartitionSpec as P

bf16 = jnp.bfloat16
f32 = jnp.float32
HEAD_DIM = 64
HALF = HEAD_DIM // 2
PAIR = 2 * HEAD_DIM
LOG2E = 1.4426950408889634
NEG = -1e30
ROW_LEN = 2048
XPOS_BASE = 512
EPS = 1e-5
BOTH = ("row", "ctx")


def walk(span_ref, qb, step):
    first = span_ref[2 + 2 * (qb)]
    clear = span_ref[3 + 2 * (qb)]

    def edge(t, carry):
        step(jnp.where(t < clear - first, first + t, qb), True)
        return carry

    def plain(kb, carry):
        step(kb, False)
        return carry

    lax.fori_loop(0, clear - first + 1, edge, 0)
    lax.fori_loop(clear, qb, plain, 0)


def allowed(lowest, kb, qb, blk):
    key = kb * blk + lax.broadcasted_iota(jnp.int32, (blk, blk), 0)
    query = qb * blk + lax.broadcasted_iota(jnp.int32, (blk, blk), 1)
    return (key <= query) & (key >= lowest)


def forward_kernel(nh, blk, unit, span_ref, q0_ref, q1_ref, k0_ref, k1_ref, v0_ref, v1_ref, table_ref, lo_ref,
                   o_ref, oT_ref, lse_ref, qT_ref, kT_ref, vT_ref, k_s, qm_s, acc_s, m_s, l_s):
    qb = pl.program_id(0)
    dim = nh * HEAD_DIM
    length = kT_ref.shape[1]
    core, place = span_ref[0], span_ref[1]
    spots = blk // (2 * unit)
    inner = lax.rem(place, spots)

    def turned(values, at, kind):
        cosine = table_ref[2 * kind, :, pl.ds(at, unit)]
        sine = table_ref[2 * kind + 1, :, pl.ds(at, unit)]
        out = []
        for h in range(nh):
            one = values[h * HEAD_DIM:h * HEAD_DIM + HALF]
            two = values[h * HEAD_DIM + HALF:(h + 1) * HEAD_DIM]
            out += [one * cosine - two * sine, two * cosine + one * sine]
        return jnp.concatenate(out, axis=0).astype(bf16)

    @pl.when(qb == 0)
    def _():
        def load(j, carry):
            src = pl.multiple_of((j ^ place) * unit, unit)
            for half, ref, v_ref in ((0, k0_ref, v0_ref), (1, k1_ref, v1_ref)):
                at = pl.multiple_of((2 * j + (core ^ half)) * unit, unit)
                key = turned(ref[:, pl.ds(src, unit)], at, 1)
                kT_ref[:, pl.ds(at, unit)] = key
                k_s[pl.ds(at, unit), :] = key.T
                vT_ref[:, pl.ds(at, unit)] = v_ref[:, pl.ds(src, unit)].astype(bf16)
            return carry

        lax.fori_loop(0, length // (2 * unit), load, 0)

    for u in range(spots):
        src = pl.multiple_of((u ^ inner) * unit, unit)
        for half, ref in ((0, q0_ref), (1, q1_ref)):
            at = pl.multiple_of((2 * u + (core ^ half)) * unit, unit)
            qT_ref[:, pl.ds(at, unit)] = turned(ref[:, pl.ds(src, unit)], pl.multiple_of(qb * blk + at, unit), 0)
    for h in range(nh):
        own = h % 2
        qm_s[h, pl.ds(own * HEAD_DIM, HEAD_DIM), :] = qT_ref[pl.ds(h * HEAD_DIM, HEAD_DIM), :]
        qm_s[h, pl.ds((1 - own) * HEAD_DIM, HEAD_DIM), :] = jnp.zeros((HEAD_DIM, blk), bf16)
    acc_s[...] = jnp.zeros_like(acc_s)
    m_s[...] = jnp.full_like(m_s, NEG)
    l_s[...] = jnp.zeros_like(l_s)
    lowest = lo_ref[...]

    def step(kb, masked):
        at = pl.multiple_of(kb * blk, blk)
        if masked:
            ok = allowed(lowest, kb, qb, blk)
        for h in range(nh):
            rows = pl.ds(h * HEAD_DIM, HEAD_DIM)
            s = jnp.dot(k_s[pl.ds(at, blk), pl.ds((h // 2) * PAIR, PAIR)], qm_s[h], preferred_element_type=f32)
            s = s * (LOG2E * HEAD_DIM**-0.5)
            if masked:
                s = jnp.where(ok, s, NEG)
            before = m_s[h:h + 1, :]
            now = jnp.maximum(before, jnp.max(s, axis=0, keepdims=True))
            p = jnp.exp2(s - now)
            fade = jnp.exp2(before - now)
            m_s[h:h + 1, :] = now
            l_s[h:h + 1, :] = l_s[h:h + 1, :] * fade + jnp.sum(p, axis=0, keepdims=True)
            acc_s[rows, :] = acc_s[rows, :] * fade + jnp.dot(
                vT_ref[rows, pl.ds(at, blk)], p.astype(bf16), preferred_element_type=f32)

    walk(span_ref, qb, step)
    for h in range(nh):
        rows = pl.ds(h * HEAD_DIM, HEAD_DIM)
        oT_ref[rows, :] = acc_s[rows, :] / l_s[h:h + 1, :]
        lse_ref[h:h + 1, :] = m_s[h:h + 1, :] + jnp.log2(l_s[h:h + 1, :])
    o_ref[...] = oT_ref[...].T.astype(bf16)


def backward_kernel(nh, blk, unit, span_ref, qT_ref, kT_ref, vT_ref, do_ref, oT_ref, lse_ref, table_ref, lo_ref,
                    old0_ref, old1_ref, d0_ref, d1_ref, k_s, v_s, qm_s, dm_s, qn_s, dn_s, acc_s, dk_s, dv_s, p_s, ds_s, dl_s):
    qb = pl.program_id(0)
    dim = nh * HEAD_DIM
    length = kT_ref.shape[1]
    count = length // blk
    scale = HEAD_DIM**-0.5
    core, place = span_ref[0], span_ref[1]

    @pl.when(qb == 0)
    def _():
        for c in range(count):
            k_s[pl.ds(c * blk, blk), :] = kT_ref[:, pl.ds(c * blk, blk)].T
            v_s[pl.ds(c * blk, blk), :] = vT_ref[:, pl.ds(c * blk, blk)].T
        dk_s[...] = jnp.zeros_like(dk_s)
        dv_s[...] = jnp.zeros_like(dv_s)

    doT = do_ref[...].T
    q = qT_ref[...].T
    lane = lax.broadcasted_iota(jnp.int32, (blk, PAIR), 1)
    prod = doT.astype(f32) * oT_ref[...]
    for h in range(nh):
        own = h % 2
        rows = slice(h * HEAD_DIM, (h + 1) * HEAD_DIM)
        zero = jnp.zeros((HEAD_DIM, blk), bf16)
        qm_s[h, pl.ds(own * HEAD_DIM, HEAD_DIM), :] = qT_ref[pl.ds(h * HEAD_DIM, HEAD_DIM), :]
        qm_s[h, pl.ds((1 - own) * HEAD_DIM, HEAD_DIM), :] = zero
        dm_s[h, pl.ds(own * HEAD_DIM, HEAD_DIM), :] = doT[rows, :]
        dm_s[h, pl.ds((1 - own) * HEAD_DIM, HEAD_DIM), :] = zero
        mine = (lane // HEAD_DIM) == own
        pair = slice((h // 2) * PAIR, (h // 2) * PAIR + PAIR)
        qn_s[h // 2, pl.ds(own * blk, blk), :] = jnp.where(mine, q[:, pair], jnp.zeros((), bf16))
        dn_s[h // 2, pl.ds(own * blk, blk), :] = jnp.where(mine, do_ref[:, pair], jnp.zeros((), bf16))
        dl_s[h:h + 1, :] = jnp.sum(prod[rows, :], axis=0, keepdims=True)
    acc_s[...] = jnp.zeros_like(acc_s)
    lowest = lo_ref[...]

    def step(kb, masked):
        at = pl.multiple_of(kb * blk, blk)
        if masked:
            ok = allowed(lowest, kb, qb, blk)
        for g in range(nh // 2):
            lanes = pl.ds(g * PAIR, PAIR)
            for own in range(2):
                h = 2 * g + own
                rows = pl.ds(h * HEAD_DIM, HEAD_DIM)
                s = jnp.dot(k_s[pl.ds(at, blk), lanes], qm_s[h], preferred_element_type=f32) * (LOG2E * scale)
                p = jnp.exp2(s - lse_ref[h:h + 1, :])
                if masked:
                    p = jnp.where(ok, p, 0.0)
                dp = jnp.dot(v_s[pl.ds(at, blk), lanes], dm_s[h], preferred_element_type=f32)
                ds = (p * (dp - dl_s[h:h + 1, :])).astype(bf16)
                p_s[g, :, pl.ds(own * blk, blk)] = p.astype(bf16)
                ds_s[g, :, pl.ds(own * blk, blk)] = ds
                acc_s[rows, :] += jnp.dot(kT_ref[rows, pl.ds(at, blk)], ds, preferred_element_type=f32)
            dv_s[pl.ds(at, blk), lanes] += jnp.dot(p_s[g], dn_s[g], preferred_element_type=f32)
            dk_s[pl.ds(at, blk), lanes] += jnp.dot(ds_s[g], qn_s[g], preferred_element_type=f32)

    walk(span_ref, qb, step)

    def turned_back(values, at, size, kind):
        cosine = table_ref[2 * kind, :, pl.ds(at, size)] * scale
        sine = table_ref[2 * kind + 1, :, pl.ds(at, size)] * scale
        out = []
        for h in range(nh):
            one = values[h * HEAD_DIM:h * HEAD_DIM + HALF]
            two = values[h * HEAD_DIM + HALF:(h + 1) * HEAD_DIM]
            out += [one * cosine + two * sine, two * cosine - one * sine]
        return jnp.concatenate(out, axis=0).T.astype(bf16)

    spots = blk // (2 * unit)
    for u in range(spots):
        dst = pl.multiple_of(((qb * spots + u) ^ place) * unit, unit)
        for half, ref in ((0, d0_ref), (1, d1_ref)):
            at = pl.multiple_of((2 * u + (core ^ half)) * unit, unit)
            ref[pl.ds(dst, unit), pl.ds(0, dim)] = turned_back(
                acc_s[:, pl.ds(at, unit)], pl.multiple_of(qb * blk + at, unit), unit, 0)

    @pl.when(qb == count - 1)
    def _():
        def store(j, carry):
            dst = pl.multiple_of((j ^ place) * unit, unit)
            for half, ref in ((0, d0_ref), (1, d1_ref)):
                at = pl.multiple_of((2 * j + (core ^ half)) * unit, unit)
                ref[pl.ds(dst, unit), pl.ds(dim, dim)] = turned_back(dk_s[pl.ds(at, unit), :].T, at, unit, 1)
                ref[pl.ds(dst, unit), pl.ds(2 * dim, dim)] = dv_s[pl.ds(at, unit), :].astype(bf16)
            return carry

        lax.fori_loop(0, length // (2 * unit), store, 0)


PARAMS = pltpu.CompilerParams(dimension_semantics=("arbitrary",), vmem_limit_bytes=60 * 2**20)


def span_of(lowest, blk, core, place):
    count = lowest.shape[0] // blk
    blocks = lowest.reshape(count, blk)
    own = jnp.arange(count, dtype=jnp.int32)
    first = jnp.minimum(blocks[:, 0] // blk, own)
    clear = jnp.minimum((blocks[:, -1] + blk - 1) // blk, own)
    both = jnp.stack([first, clear], axis=-1).reshape(-1)
    return jnp.concatenate([jnp.stack([core, place]), both]).astype(jnp.int32)


def attention_forward(row, half0, half1, table, lowest, span, blk, unit):
    length = lowest.shape[0]
    dim = half0.shape[0] // 3
    nh, count = dim // HEAD_DIM, length // blk
    spots = blk // (2 * unit)
    sds = jax.ShapeDtypeStruct
    pick = pl.BlockSpec((dim, blk // 2), lambda q, s: (0, row * count + (q ^ lax.div(s[1], spots))))
    keys = pl.BlockSpec((dim, length // 2), lambda q, s: (1, row))
    values = pl.BlockSpec((dim, length // 2), lambda q, s: (2, row))
    wide = pl.BlockSpec((dim, length), lambda q, s: (0, 0))
    cut = pl.BlockSpec((dim, blk), lambda q, s: (0, q))
    return pl.pallas_call(
        functools.partial(forward_kernel, nh, blk, unit),
        out_shape=(sds((length, dim), bf16), sds((dim, length), f32), sds((nh, length), f32),
                   sds((dim, length), bf16), sds((dim, length), bf16), sds((dim, length), bf16)),
        grid_spec=pltpu.PrefetchScalarGridSpec(
            num_scalar_prefetch=1, grid=(count,),
            in_specs=[pick, pick, keys, keys, values, values,
                      pl.BlockSpec((4, HALF, length), lambda q, s: (0, 0, 0)),
                      pl.BlockSpec((1, blk), lambda q, s: (0, q))],
            out_specs=[pl.BlockSpec((blk, dim), lambda q, s: (q, 0)), cut,
                       pl.BlockSpec((nh, blk), lambda q, s: (0, q)), cut, wide, wide],
            scratch_shapes=[pltpu.VMEM((length, dim), bf16), pltpu.VMEM((nh, PAIR, blk), bf16), pltpu.VMEM((dim, blk), f32),
                            pltpu.VMEM((8, blk), f32), pltpu.VMEM((8, blk), f32)]),
        compiler_params=PARAMS, name="attention_forward",
        cost_estimate=pl.CostEstimate(flops=4 * 4 * dim * length * length // 2, bytes_accessed=10 * 2**20,
                                      transcendentals=nh * length * length // 2),
    )(span, half0, half1, half0, half1, half0, half1, table, lowest[None, :])


def attention_backward(row, rows, saved, do, table, lowest, span, blk, unit, before):
    oT, lse, qT, kT, vT = saved
    length = lowest.shape[0]
    dim = qT.shape[0]
    nh, count = dim // HEAD_DIM, length // blk
    sds = jax.ShapeDtypeStruct
    cut = pl.BlockSpec((dim, blk), lambda q, s: (0, q))
    wide = pl.BlockSpec((dim, length), lambda q, s: (0, 0))
    grad = pl.BlockSpec((length // 2, 3 * dim), lambda q, s: (row, 0))
    whole = sds((rows * length // 2, 3 * dim), bf16)
    kernel = functools.partial(backward_kernel, nh, blk, unit)
    if before is None:
        def call(span_ref, *refs):
            kernel(span_ref, *refs[:8], None, None, *refs[8:])
    else:
        call = kernel
    return pl.pallas_call(
        call,
        out_shape=(whole, whole),
        grid_spec=pltpu.PrefetchScalarGridSpec(
            num_scalar_prefetch=1, grid=(count,),
            in_specs=[cut, wide, wide, pl.BlockSpec((blk, dim), lambda q, s: (q, 0)), cut,
                      pl.BlockSpec((nh, blk), lambda q, s: (0, q)),
                      pl.BlockSpec((4, HALF, length), lambda q, s: (0, 0, 0)),
                      pl.BlockSpec((1, blk), lambda q, s: (0, q))]
            + ([] if before is None else [pl.BlockSpec(memory_space=pl.ANY)] * 2),
            out_specs=[grad, grad],
            scratch_shapes=[pltpu.VMEM((length, dim), bf16), pltpu.VMEM((length, dim), bf16),
                            pltpu.VMEM((nh, PAIR, blk), bf16), pltpu.VMEM((nh, PAIR, blk), bf16),
                            pltpu.VMEM((nh // 2, 2 * blk, PAIR), bf16), pltpu.VMEM((nh // 2, 2 * blk, PAIR), bf16),
                            pltpu.VMEM((dim, blk), f32), pltpu.VMEM((length, dim), f32), pltpu.VMEM((length, dim), f32),
                            pltpu.VMEM((nh // 2, blk, 2 * blk), bf16), pltpu.VMEM((nh // 2, blk, 2 * blk), bf16),
                            pltpu.VMEM((8, blk), f32)]),
        compiler_params=PARAMS, name="attention_backward",
        input_output_aliases={} if before is None else {9: 0, 10: 1},
        cost_estimate=pl.CostEstimate(flops=10 * 4 * dim * length * length // 2, bytes_accessed=20 * 2**20,
                                      transcendentals=nh * length * length // 2),
    )(span, qT, kT, vT, do, oT, lse, table, lowest[None, :], *(before or ()))


def hat_of(values):
    center = values - jnp.mean(values, axis=-1, keepdims=True)
    rstd = lax.rsqrt(jnp.mean(center * center, axis=-1, keepdims=True) + EPS)
    return center * rstd, rstd


def hat_back(hat, rstd, grad):
    return rstd * (grad - jnp.mean(grad, axis=-1, keepdims=True) - hat * jnp.mean(grad * hat, axis=-1, keepdims=True))


def wide_row(o_ref):
    return jnp.concatenate([o_ref[i] for i in range(o_ref.shape[0])], axis=1).astype(f32)


def middle_forward_kernel(o_ref, x_ref, w_ref, c_ref, x1_ref, b_ref):
    c = hat_of(wide_row(o_ref))[0].astype(bf16)
    c_ref[...] = c
    x1 = x_ref[...].astype(f32) + jnp.dot(c, w_ref[...], preferred_element_type=f32)
    x1_ref[...] = x1
    b_ref[...] = hat_of(x1)[0].astype(bf16)


def middle_forward(o, x, w):
    n, size, dim = o.shape
    width = n * dim
    step = min(128, size)
    sds = jax.ShapeDtypeStruct
    flat = pl.BlockSpec((step, width), lambda t: (t, 0))
    return pl.pallas_call(
        middle_forward_kernel,
        out_shape=(sds((size, width), bf16), sds((size, width), f32), sds((size, width), bf16)),
        grid=(size // step,),
        in_specs=[pl.BlockSpec((n, step, dim), lambda t: (0, t, 0)), flat,
                  pl.BlockSpec((width, width), lambda t: (0, 0))],
        out_specs=(flat, flat, flat),
        compiler_params=PARAMS, name="middle_forward",
        cost_estimate=pl.CostEstimate(flops=2 * size * width * width, bytes_accessed=14 * 2**20, transcendentals=0),
    )(o, x, w)


def middle_backward_kernel(o_ref, x1_ref, db_ref, dy_ref, w_ref, dx_ref, low_ref, do_ref):
    hat, rstd = hat_of(x1_ref[...])
    dx1 = dy_ref[...].astype(f32) + hat_back(hat, rstd, db_ref[...])
    dx_ref[...] = dx1
    low_ref[...] = dx1.astype(bf16)
    dc = times_rows(dx1.astype(bf16), w_ref[...])
    hat, rstd = hat_of(wide_row(o_ref))
    d_o = hat_back(hat, rstd, dc).astype(bf16)
    dim = do_ref.shape[2]
    for i in range(do_ref.shape[0]):
        do_ref[i] = d_o[:, i * dim:(i + 1) * dim]


def middle_backward(row, o, x1, db, dy, w):
    n, size, dim = o.shape
    width = n * dim
    step = min(128, size)
    sds = jax.ShapeDtypeStruct
    flat = pl.BlockSpec((step, width), lambda t: (t, 0))
    part = pl.BlockSpec((n, step, dim), lambda t: (0, t, 0))
    return pl.pallas_call(
        middle_backward_kernel,
        out_shape=(sds((size, width), f32), sds((size, width), bf16), sds((n, size, dim), bf16)),
        grid=(size // step,),
        in_specs=[part, flat, pl.BlockSpec((step, width), lambda t: (row * (size // step) + t, 0)), flat,
                  pl.BlockSpec((width, width), lambda t: (0, 0))],
        out_specs=(flat, flat, part),
        compiler_params=PARAMS, name="middle_backward",
        cost_estimate=pl.CostEstimate(flops=2 * size * width * width, bytes_accessed=16 * 2**20, transcendentals=0),
    )(o, x1, db, dy, w)


def ways(row, n):
    bits = [1 << k for k in range(1, n.bit_length() - 1)]
    return bits if row % 2 == 0 else bits[::-1]


def times_rows(a, w):
    return lax.dot_general(a, w, (((1,), (1,)), ((), ())), preferred_element_type=f32)


def weight_copies(all_ref, kind, dst_ref, sems, first=0):
    m, lines, ff = all_ref.shape
    unit = ff // m
    pieces = dst_ref.shape[1 if kind == "down" else 0] // ff
    depth = lines - unit * pieces
    copies = []
    for r in range(m):
        if kind == "up":
            moves = [(all_ref.at[r, pl.ds(0, depth), :], dst_ref.at[pl.ds(r * depth, depth), :])]
        else:
            moves = [(all_ref.at[r, pl.ds(depth + q * unit, unit), :],
                      dst_ref.at[pl.ds(r * unit, unit), pl.ds(q * ff, ff)]) for q in range(pieces)]
        for src, dst in moves:
            copies.append(pltpu.make_async_copy(src, dst, sems.at[first + len(copies)]))
    for copy in copies:
        copy.start()
    return copies


def product_sum_kernel(n, rows, cols, turned, kind, x0_ref, x1_ref, w_ref, o_ref, part_s, core_s, sum_s, got_s, send_sem, recv_sem,
                       *own_w):
    mine = lax.axis_index("ctx")
    loads = []
    if kind:
        loads = weight_copies(w_ref, kind, *own_w)
        w_ref = own_w[0]
    spots = n // 2
    size = x0_ref.shape[0] // (rows * spots)
    width = o_ref.shape[1]
    barrier = pltpu.get_barrier_semaphore()
    bits = [1] + ways(0, n)
    for bit in bits:
        pl.semaphore_signal(barrier, inc=1, device_id={"ctx": mine ^ bit}, device_id_type=pl.DeviceIdType.MESH)
    pl.semaphore_wait(barrier, len(bits))
    for copy in loads:
        copy.wait()
    copies = []

    def send(src, dst, bit):
        at = len(copies)
        copy = pltpu.make_async_remote_copy(
            src_ref=src, dst_ref=dst, send_sem=send_sem.at[at], recv_sem=recv_sem.at[at],
            device_id={"ctx": mine ^ bit}, device_id_type=pl.DeviceIdType.MESH)
        copy.start()
        copies.append(copy)
        return copy

    def key(row, k):
        return [-(k & (bit >> 1)) for bit in ways(row, n)]

    orders = []
    for r in range(rows):
        way = [bit >> 1 for bit in ways(r, n)]
        orders.append(sorted(range(spots), key=lambda k: [0 if k & bit else 1 for bit in way]))
    todo = [(r, orders[r][t]) for t in range(spots) for r in range(rows)]
    inbox, slot, slots = {}, {}, 0

    def product(x_ref, r, k, finish):
        begin = (r * spots + k) * size

        @pl.loop(0, width // cols)
        def _(c):
            at = pl.ds(pl.multiple_of(c * cols, cols), cols)
            x = x_ref[pl.ds(begin, size), :]
            finish(at, times_rows(x, w_ref[at, :]) if turned else jnp.dot(x, w_ref[:, at], preferred_element_type=f32))

    def pair(r, k):
        spot = r * spots + k

        def keep(at, value):
            part_s[spot, :, at] = value.astype(bf16)

        product(x1_ref, r, k, keep)
        inbox[r, k] = send(part_s.at[spot], core_s.at[spot], 1)

    def own(r, k):
        spot = r * spots + k
        inbox[r, k].wait_recv()

        def add(at, value):
            sum_s[spot, :, at] = (value + core_s[spot, :, at].astype(f32)).astype(bf16)

        product(x0_ref, r, k, add)

    def pass_on(r, k, stage):
        nonlocal slots
        bit = ways(r, n)[stage]
        if k & (bit >> 1):
            inbox[r, k ^ (bit >> 1), stage] = (send(sum_s.at[r * spots + k], got_s.at[slots], bit), slots)
            slots += 1

    group = max(rows * spots // 2, 1)
    for begin in range(0, len(todo), group):
        for r, k in todo[begin:begin + group]:
            pair(r, k)
        for r, k in todo[begin:begin + group]:
            own(r, k)
            pass_on(r, k, 0)
    stages = len(bits) - 1
    for stage in range(stages):
        for r, k in todo:
            way = [bit >> 1 for bit in ways(r, n)]
            if any(k & bit for bit in way[:stage + 1]):
                continue
            copy, at = inbox[r, k, stage]
            copy.wait_recv()
            spot = r * spots + k
            if stage == stages - 1:
                o_ref[pl.ds(r * size, size), :] = sum_s[spot].astype(f32) + got_s[at].astype(f32)
            else:
                sum_s[spot] = (sum_s[spot].astype(f32) + got_s[at].astype(f32)).astype(bf16)
                pass_on(r, k, stage + 1)
    for copy in copies:
        copy.wait_send()


def product_sum(x0, x1, w, rows, n, collective_id, turned=False, kind=None, wide=None):
    size = x0.shape[0] // (rows * (n // 2))
    depth = x0.shape[1]
    width = wide if kind else w.shape[0 if turned else 1]
    count = rows * (n // 2)
    moves = count + rows * (n // 2 - 1)
    vmem = pl.BlockSpec(memory_space=pltpu.VMEM)
    flops = 4 * x0.shape[0] * x0.shape[1] * width
    return pl.pallas_call(
        functools.partial(product_sum_kernel, n, rows, min(512, width), turned, kind),
        out_shape=jax.ShapeDtypeStruct((rows * size, width), f32),
        in_specs=[vmem, vmem, pl.BlockSpec(memory_space=pl.ANY) if kind else vmem], out_specs=vmem,
        scratch_shapes=[pltpu.VMEM((count, size, width), bf16), pltpu.VMEM((count, size, width), bf16),
                        pltpu.VMEM((count, size, width), bf16), pltpu.VMEM((moves - count, size, width), bf16),
                        pltpu.SemaphoreType.DMA((moves,)), pltpu.SemaphoreType.DMA((moves,))]
        + ([pltpu.VMEM((width, depth) if turned else (depth, width), bf16), pltpu.SemaphoreType.DMA((64,))] if kind else []),
        compiler_params=pltpu.CompilerParams(collective_id=collective_id, has_side_effects=True, vmem_limit_bytes=60 * 2**20),
        name="product_sum",
        cost_estimate=pl.CostEstimate(flops=4 * flops, bytes_accessed=20 * 2**20, transcendentals=0),
    )(x0, x1, w)


def gather_product_kernel(n, rows, cols, b_ref, dy0_ref, dy1_ref, w_ref, b0_ref, b1_ref, h0_ref, h1_ref, d0_ref, d1_ref,
                          stat_ref, up_ref, down_ref, got_s, d_s, h_s, dy_s, w_sem, send_sem, recv_sem, dy_sem, b_sem, h_sem, d_sem):
    mine = lax.axis_index("ctx")
    spots = n // 2
    size = b_ref.shape[0] // rows
    ff = up_ref.shape[1]
    loads = weight_copies(w_ref, "down", down_ref, w_sem)
    loads_up = weight_copies(w_ref, "up", up_ref, w_sem, len(loads))
    count = rows * spots
    barrier = pltpu.get_barrier_semaphore()
    bits = [1] + ways(0, n)
    for bit in bits:
        pl.semaphore_signal(barrier, inc=1, device_id={"ctx": mine ^ bit}, device_id_type=pl.DeviceIdType.MESH)
    pl.semaphore_wait(barrier, len(bits))
    sends, locals_, arrival = [], [], {}

    def send(src, half, row, k, bit):
        at, to = len(sends), half * count + row * spots + k
        copy = pltpu.make_async_remote_copy(
            src_ref=src, dst_ref=got_s.at[to], send_sem=send_sem.at[at], recv_sem=recv_sem.at[at],
            device_id={"ctx": mine ^ bit}, device_id_type=pl.DeviceIdType.MESH)
        copy.start()
        sends.append(copy)
        arrival[half, row, k] = copy

    def held(half, row, k):
        if half == 0 and k == 0:
            return b_ref.at[pl.ds(row * size, size), :]
        return got_s.at[half * count + row * spots + k]

    def onward(row, k):
        way = ways(row, n)
        top = max([s for s, bit in enumerate(way) if k & (bit >> 1)], default=-1)
        for bit in way[top + 1:]:
            send(held(0, row, k), 0, row, k | (bit >> 1), bit)
        send(held(0, row, k), 1, row, k, 1)

    for r in range(rows):
        onward(r, 0)

    def fetch(t, slot):
        begin = pl.multiple_of(lax.rem(t, count) * size, size)

        @pl.when(t < count)
        def _():
            pltpu.make_async_copy(dy0_ref.at[pl.ds(begin, size), :], dy_s.at[slot], dy_sem.at[slot]).start()

        @pl.when(t >= count)
        def _():
            pltpu.make_async_copy(dy1_ref.at[pl.ds(begin, size), :], dy_s.at[slot], dy_sem.at[slot]).start()

    fetch(0, 0)
    for copy in loads:
        copy.wait()

    @pl.loop(0, 2 * count)
    def _(t):
        slot = lax.rem(t, 2)

        @pl.when(t + 1 < 2 * count)
        def _():
            fetch(t + 1, 1 - slot)

        pltpu.make_async_copy(dy0_ref.at[pl.ds(0, size), :], dy_s.at[slot], dy_sem.at[slot]).wait()

        @pl.loop(0, ff // cols)
        def _(c):
            at = pl.ds(pl.multiple_of(c * cols, cols), cols)
            d_s[t, :, at] = times_rows(dy_s[slot], down_ref[at, :])

    for t in range(2 * count):
        dst = (d0_ref, d1_ref)[t // count].at[pl.ds((t % count) * size, size), :]
        copy = pltpu.make_async_copy(d_s.at[t], dst, d_sem.at[t])
        copy.start()
        locals_.append(copy)

    for copy in loads_up:
        copy.wait()
    outs = []
    lane = lax.broadcasted_iota(jnp.int32, (32, 128), 1)

    def block(half, row, k):
        t = half * count + row * spots + k
        src = held(half, row, k)
        copy = pltpu.make_async_copy(src, (b0_ref, b1_ref)[half].at[pl.ds((t % count) * size, size), :], b_sem.at[t])
        copy.start()
        locals_.append(copy)
        slot = len(outs) % 2
        if len(outs) >= 2:
            outs[-2].wait()

        @pl.loop(0, ff // cols)
        def _(c):
            at = pl.ds(pl.multiple_of(c * cols, cols), cols)
            h_s[slot, :, at] = jnp.dot(src[...], up_ref[:, at], preferred_element_type=f32)

        copy = pltpu.make_async_copy(h_s.at[slot], (h0_ref, h1_ref)[half].at[pl.ds((t % count) * size, size), :], h_sem.at[t])
        copy.start()
        outs.append(copy)

        @pl.loop(0, size // 32)
        def _(c):
            at = pl.ds(pl.multiple_of(c * 32, 32), 32)
            h = h_s[slot, at, :]
            gel = h * (0.5 * (1.0 + lax.erf(h * (2.0**-0.5))))
            d = d_s[t, at, :]
            mean = jnp.mean(gel, axis=-1, keepdims=True)
            off = gel - mean
            spread = jnp.sum(off * off, axis=-1, keepdims=True)
            total = jnp.sum(d, axis=-1, keepdims=True)
            cross = jnp.sum(d * off, axis=-1, keepdims=True)
            line = jnp.where(lane == 0, mean, jnp.where(lane == 1, spread, jnp.where(lane == 2, total, cross)))
            stat_ref[pl.ds(pl.multiple_of(t * size + c * 32, 32), 32), :] = line

    order = []
    for k in range(spots):
        for r in range(rows):
            way = ways(r, n)
            order.append((r, sum((bit >> 1) for s, bit in enumerate(way) if k >> s & 1)))
    for begin in range(0, len(order), rows):
        some = order[begin:begin + rows]
        for r, k in some:
            if k:
                arrival[0, r, k].wait_recv()
                onward(r, k)
        for r, k in some:
            block(0, r, k)
        for r, k in some:
            arrival[1, r, k].wait_recv()
            block(1, r, k)
    for copy in outs[-2:] + locals_:
        copy.wait()
    for copy in sends:
        copy.wait_send()


def gather_product(b, dy0, dy1, weights, rows, n, collective_id):
    size = b.shape[0] // rows
    width, ff = b.shape[1], weights.shape[2]
    count = rows * (n // 2)
    half = count * size
    moves = rows * (n - 1)
    vmem, here = pl.BlockSpec(memory_space=pltpu.VMEM), pl.BlockSpec(memory_space=pl.ANY)
    sds = jax.ShapeDtypeStruct
    return pl.pallas_call(
        functools.partial(gather_product_kernel, n, rows, min(256, ff)),
        out_shape=(sds((half, width), bf16),) * 2 + (sds((half, ff), f32),) * 4 + (sds((2 * half, 128), f32),),
        in_specs=[vmem, here, here, here], out_specs=(here,) * 6 + (vmem,),
        scratch_shapes=[pltpu.VMEM((width, ff), bf16), pltpu.VMEM((ff, width), bf16),
                        pltpu.VMEM((2 * count, size, width), bf16), pltpu.VMEM((2 * count, size, ff), f32),
                        pltpu.VMEM((2, size, ff), f32), pltpu.VMEM((2, size, width), bf16), pltpu.SemaphoreType.DMA((64,)),
                        pltpu.SemaphoreType.DMA((moves,)), pltpu.SemaphoreType.DMA((moves,)), pltpu.SemaphoreType.DMA((2,))]
        + [pltpu.SemaphoreType.DMA((2 * count,))] * 3,
        compiler_params=pltpu.CompilerParams(collective_id=collective_id, has_side_effects=True, vmem_limit_bytes=62 * 2**20),
        name="gather_product",
        cost_estimate=pl.CostEstimate(flops=16 * half * width * ff, bytes_accessed=70 * 2**20, transcendentals=0),
    )(b, dy0, dy1, weights)


def standardize(values):
    center = values - jnp.mean(values, axis=-1, keepdims=True)
    spread = jnp.mean(center * center, axis=-1, keepdims=True)
    rstd = lax.rsqrt(spread + EPS)
    return center * rstd, rstd


def standardize_back(hat, rstd, grad):
    return rstd * (grad - jnp.mean(grad, axis=-1, keepdims=True) - hat * jnp.mean(grad * hat, axis=-1, keepdims=True))


def row_places(lengths, row_len):
    places = jnp.arange(row_len, dtype=jnp.int32)
    ends = jnp.cumsum(lengths, axis=-1)
    passed = ends[:, None, :] <= places[None, :, None]
    starts = jnp.sum(jnp.where(passed, lengths[:, None, :], 0), axis=-1)
    valid = places[None, :] < ends[:, -1:]
    lowest = jnp.where(valid, starts, places[None, :]).astype(jnp.int32)
    return (places[None, :] - starts).astype(f32), lowest


def xpos_tables(relative):
    ladder = jnp.arange(HALF, dtype=f32) / HALF
    rate = jnp.power(10000.0, -ladder)
    base = (ladder + 0.4) / 1.4
    angles = rate[None, :, None] * relative[:, None, :]
    power = (relative[:, None, :] - ROW_LEN / 2) / XPOS_BASE
    factor = jnp.power(base[None, :, None], power)
    cosine, sine = jnp.cos(angles), jnp.sin(angles)
    return jnp.stack([cosine * factor, sine * factor, cosine / factor, sine / factor], axis=1)


def dot(a, b, spec, kind=f32):
    return jnp.einsum(spec, a, b, preferred_element_type=f32).astype(kind)


def swap(x, bit):
    n = lax.axis_size("ctx")
    return lax.ppermute(x, "ctx", [(i, i ^ bit) for i in range(n)])


def exchange(blocks):
    n = lax.axis_size("ctx")
    mine = lax.axis_index("ctx")
    out = jnp.zeros_like(blocks)
    for bit in range(n):
        block = lax.dynamic_index_in_dim(blocks, mine ^ bit, 0, False)
        block = swap(block, bit) if bit else block
        out = lax.dynamic_update_index_in_dim(out, block, mine ^ bit, 0)
    return out


def after(x, *others):
    return lax.optimization_barrier((x, *others))[0]


def gather_start(x):
    return [{0: x[r]} for r in range(x.shape[0])]


def gather_step(held, step):
    n = lax.axis_size("ctx")
    out = []
    for r, parts in enumerate(held):
        bit = ways(r, n)[step]
        out.append({**parts, **{k | bit: swap(v, bit) for k, v in parts.items()}})
    return out


def gather_own(held, step):
    n = lax.axis_size("ctx")
    out = []
    for r, parts in enumerate(held):
        bit = ways(r, n)[step]
        out.append({**parts, bit: swap(parts[0], bit)})
    return out


def gather_rest(held, step):
    n = lax.axis_size("ctx")
    out = []
    for r, parts in enumerate(held):
        bit = ways(r, n)[step]
        moved = {k | bit: swap(v, bit) for k, v in parts.items() if k and not k & bit}
        out.append({**parts, **moved})
    return out


def gather_steps():
    return lax.axis_size("ctx").bit_length() - 2


def gather_end(held):
    return jnp.concatenate([parts[k] for parts in held for k in sorted(parts)], axis=0)


def gather_half(x):
    held = gather_start(x)
    for step in range(gather_steps()):
        held = gather_step(held, step)
    return gather_end(held)


def plus(a, b, kind=bf16):
    return (a.astype(f32) + b.astype(f32)).astype(kind)


def reduce_start(half0, half1, rows):
    n = lax.axis_size("ctx")
    width = half0.shape[-1]
    both = plus(half0, swap(half1, 1)).reshape(rows, n // 2, -1, width)
    return [{2 * k: both[r, k] for k in range(n // 2)} for r in range(rows)]


def reduce_step(held, step):
    n = lax.axis_size("ctx")
    out = []
    for r, parts in enumerate(held):
        bit = ways(r, n)[step]
        kind = bf16 if len(parts) > 2 else f32
        out.append({k: plus(v, swap(parts[k | bit], bit), kind) for k, v in parts.items() if not k & bit})
    return out


def reduce_end(held):
    return jnp.concatenate([parts[0] for parts in held], axis=0)


def reduce_halves(half0, half1, rows):
    held = reduce_start(half0, half1, rows)
    for step in range(gather_steps()):
        held = reduce_step(held, step)
    return reduce_end(held)


def body(inputs, doc_len, w_query, w_key, w_value, w_out, w_up, w_down, gain_attn, gain_attn_sub, gain_ffn,
         gain_ffn_sub, out_cotangent):
    rows, local_len, width = inputs.shape
    n, m = lax.axis_size("ctx"), lax.axis_size("row")
    row_len = local_len * n
    tokens, half = rows * local_len, rows * row_len // 2
    piece = w_query.shape[0]
    heads_dim = width // n
    ff = w_up.shape[1]
    unit = ff // (n * m)
    ff_dev = unit * m
    blk = min(512, row_len)
    mine = lax.axis_index("ctx")
    core, place = mine & 1, mine >> 1

    def scaled(w, gain):
        return (w.astype(f32) * gain.astype(f32)[:, None]).astype(bf16)

    def against(w, raw):
        return jnp.sum(w.astype(f32) * raw, axis=-1)

    def grown(raw, gain):
        return raw * gain.astype(f32)[:, None]

    x_own = inputs.reshape(tokens, width).astype(f32)
    x_hat, x_rstd = standardize(x_own)
    x_low = x_hat.astype(bf16)
    x_held = gather_step(gather_start(x_low.reshape(rows, local_len, width)), 0)

    qkv_local = jnp.concatenate(
        [scaled(w, gain_attn).reshape(piece, n, heads_dim) for w in (w_query, w_key, w_value)], axis=2)
    qkv_part = exchange(qkv_local.transpose(1, 0, 2)).reshape(n * piece, 3 * heads_dim)
    w_qkv = lax.all_gather(qkv_part, "row", axis=0, tiled=True)
    up_local = scaled(after(w_up, qkv_part), gain_ffn).reshape(piece, m, n, unit).transpose(2, 0, 1, 3).reshape(n, piece, ff_dev)
    up_part = lax.all_to_all(up_local, "ctx", split_axis=0, concat_axis=0, tiled=True).reshape(n * piece, ff_dev)
    for step in range(1, gather_steps()):
        x_held = gather_step(x_held, step)
    xh0 = gather_end(x_held)
    xh0, up_part = lax.optimization_barrier((xh0, up_part))
    xh1 = swap(xh0, 1)
    down_local = scaled(w_down, gain_ffn_sub)
    ffn_local = jnp.concatenate([up_part] + [down_local[:, q:q + ff_dev] for q in range(0, width, ff_dev)], axis=0)
    out_all = lax.all_gather(scaled(w_out, gain_attn_sub), BOTH, axis=0, tiled=True)

    relative, lowest = row_places(doc_len, row_len)
    table = xpos_tables(relative)
    span = [span_of(lowest[r], blk, core, place) for r in range(rows)]
    qkv0 = dot(w_qkv, xh0, "df,td->ft")
    qkv1 = dot(w_qkv, xh1, "df,td->ft")
    qkv0, qkv1, cot, out_all = lax.optimization_barrier((qkv0, qkv1, out_cotangent, out_all))
    ffn_all = lax.all_gather(after(ffn_local, out_all), "row", axis=0, tiled=False)
    dy_held = gather_step(gather_start(cot), 0)
    dy_steps = gather_steps()
    saved, o = [], []
    for r in range(rows):
        o_row, *kept = attention_forward(r, qkv0, qkv1, table[r], lowest[r], span[r], blk, local_len)
        if r == 0:
            o_row, kept, qkv0, qkv1, dy_held = lax.optimization_barrier((o_row, kept, qkv0, qkv1, dy_held))
            dy_held = gather_own(dy_held, 1)
        if r == rows - 1:
            o_row, o, dy_held = lax.optimization_barrier((o_row, o, dy_held))
            dy_held = gather_rest(dy_held, 1)
            for step in range(2, dy_steps):
                dy_held = gather_step(dy_held, step)
        saved.append(kept)
        o.append(lax.all_to_all(o_row.reshape(n, local_len, heads_dim), "ctx", split_axis=0, concat_axis=0, tiled=True))
    c, x1, b_low = zip(*[middle_forward(o[r], inputs[r], out_all) for r in range(rows)])
    b_low, dy_held = lax.optimization_barrier((b_low, dy_held))
    dy0 = gather_end(dy_held)
    dy1 = swap(dy0, 1)

    b0, b1, h0, h1, d_hat0, d_hat1, stats = gather_product(jnp.concatenate(b_low), dy0, dy1, ffn_all, rows, n, 4)
    stats = stats[:, :4].T
    order = jnp.arange(n // 2, dtype=jnp.int32) ^ place
    halves = jnp.arange(2, dtype=jnp.int32) ^ core

    def reorder(v):
        v = v.reshape(v.shape[0], 2, rows, n // 2, local_len)
        return jnp.take(jnp.take(v, halves, axis=1), order, axis=3).reshape(v.shape[0], 2 * half)

    stats = lax.all_gather(reorder(stats), "ctx", axis=0, tiled=False)
    mean = jnp.mean(stats[:, 0], axis=0)
    shift = stats[:, 0] - mean
    var = (jnp.sum(stats[:, 1], axis=0) + ff_dev * jnp.sum(shift * shift, axis=0)) / ff
    rstd = lax.rsqrt(var + EPS)
    d_mean = jnp.sum(stats[:, 2], axis=0) / ff
    d_corr = rstd * jnp.sum(stats[:, 3] + stats[:, 2] * shift, axis=0) / ff
    merged = reorder(jnp.stack([mean, rstd, d_mean, d_corr])).reshape(4, 2, half, 1)

    def finish(h, d_hat, which):
        cdf = 0.5 * (1.0 + lax.erf(h * (2.0**-0.5)))
        mean, rstd, d_mean, d_corr = (merged[k, which] for k in range(4))
        hat = (h * cdf - mean) * rstd
        d_gel = rstd * (d_hat - d_mean - hat * d_corr)
        pdf = jnp.exp(-0.5 * h * h) * 0.3989422804014327
        return hat.astype(bf16), (d_gel * (cdf + h * pdf)).astype(bf16)

    e0, dh0 = finish(h0, d_hat0, 0)
    e1, dh1 = finish(h1, d_hat1, 1)
    down_part = (dot(e0, dy0, "tf,td->fd") + dot(e1, dy1, "tf,td->fd")).astype(bf16)
    up_part = (dot(b0, dh0, "td,tf->df") + dot(b1, dh1, "td,tf->df")).astype(bf16)
    e0, e1, dh0, dh1, down_part, up_part = lax.optimization_barrier((e0, e1, dh0, dh1, down_part, up_part))
    down_sum = lax.psum_scatter(down_part, "row", scatter_dimension=0, tiled=True)
    db = product_sum(dh0, dh1, ffn_all, rows, n, 1, True, "up", width)
    db, up_part, down_sum = lax.optimization_barrier((db, up_part, down_sum))
    down_raw = down_sum.astype(f32)
    up_sum = lax.psum_scatter(up_part, "row", scatter_dimension=0, tiled=True)

    dx1, dx1b, d_o = zip(*[middle_backward(r, o[r], x1[r], db, out_cotangent[r], out_all) for r in range(rows)])
    do_heads = [lax.all_to_all(v, "ctx", split_axis=0, concat_axis=0, tiled=True).reshape(row_len, heads_dim) for v in d_o]
    c_order = jnp.concatenate(c).reshape(tokens, m, n, piece).transpose(0, 2, 1, 3).reshape(tokens, width)
    out_part = dot(c_order, jnp.concatenate(dx1b), "td,te->de", bf16)
    do_heads[0], out_part = lax.optimization_barrier((do_heads[0], out_part))
    grads = attention_backward(0, rows, saved[0], do_heads[0], table[0], lowest[0], span[0], blk, local_len, None)
    grads, do_heads, up_sum, out_part = lax.optimization_barrier((grads, do_heads, up_sum, out_part))
    out_part = lax.psum_scatter(out_part, "ctx", scatter_dimension=0, tiled=True)
    up_moved = lax.all_to_all(up_sum.reshape(n, piece, ff_dev), "ctx", split_axis=0, concat_axis=2, tiled=True)
    for r in range(1, rows):
        grads = attention_backward(r, rows, saved[r], do_heads[r], table[r], lowest[r], span[r], blk, local_len, grads)
    d0, d1 = grads
    qkv_part = (dot(xh0, d0, "td,tf->df") + dot(xh1, d1, "td,tf->df")).astype(bf16)
    up_raw = up_moved.reshape(piece, n, m, unit).transpose(0, 2, 1, 3).reshape(piece, ff).astype(f32)
    ffn_grads = (grown(up_raw, gain_ffn), against(w_up, up_raw), grown(down_raw, gain_ffn_sub), against(w_down, down_raw))
    d0, d1, qkv_part, out_part, ffn_grads = lax.optimization_barrier((d0, d1, qkv_part, out_part, ffn_grads))
    qkv_part = lax.psum_scatter(qkv_part, "row", scatter_dimension=0, tiled=True)
    da = product_sum(d0, d1, w_qkv, rows, n, 2, True)
    e0, e1, da, qkv_part, out_part = lax.optimization_barrier((e0, e1, da, qkv_part, out_part))
    out_raw = lax.psum_scatter(out_part, "row", scatter_dimension=0, tiled=True).astype(f32)
    qkv_raw = lax.all_to_all(qkv_part.reshape(n, piece, 3 * heads_dim), "ctx", split_axis=0, concat_axis=2, tiled=True)

    ffn = product_sum(e0, e1, ffn_all, rows, n, 3, False, "down", width)
    ffn, out_raw, qkv_raw = lax.optimization_barrier((ffn, out_raw, qkv_raw))
    output = (jnp.stack(x1) + ffn.reshape(rows, local_len, width)).astype(bf16)
    qkv_raw = qkv_raw.reshape(piece, n, 3, heads_dim).astype(f32)
    query_raw, key_raw, value_raw = (qkv_raw[:, :, i].reshape(piece, width) for i in range(3))
    input_grad = jnp.stack(dx1) + standardize_back(x_hat, x_rstd, da).reshape(rows, local_len, width)

    gain_one = against(w_query, query_raw) + against(w_key, key_raw) + against(w_value, value_raw)
    return (output, input_grad, grown(query_raw, gain_attn), grown(key_raw, gain_attn), grown(value_raw, gain_attn),
            grown(out_raw, gain_attn_sub), ffn_grads[0], ffn_grads[2],
            gain_one, against(w_out, out_raw), ffn_grads[1], ffn_grads[3])


def solution(mesh):
    split = P(BOTH, None)
    acts = P("row", "ctx", None)
    gain = P(BOTH)
    return jax.shard_map(
        body,
        mesh=mesh,
        in_specs=(acts, P("row", None)) + (split,) * 6 + (gain,) * 4 + (acts,),
        out_specs=(acts, acts) + (split,) * 6 + (gain,) * 4,
        check_vma=False,
    )
```
